32 devices in a mesh: dp: 8 (over z, core), seq: 4 (over y, x).
Axes of the slice: x: 2, y: 2, z: 4, core: 2. Of those that a mesh axis runs over, the one named last changes fastest.
Arguments:
- block_in: bfloat16 [8, 1024, 1024], P('dp', 'seq'), may hold values from -6 to 6
- positions: int32 [8, 1024], P('dp', 'seq'), may hold values from 0 to 2046, as said below
- doc_ids: int32 [8, 1024], P('dp'), may hold values from 0 to 3, never falling along the last dimension, each value on 1 to 512 neighbouring positions
- first_gain: bfloat16 [1024], P('dp'), may hold values from 0.29882812 to 3
- query_weight: bfloat16 [1024, 2048], P('dp'), may hold values from -0.1875 to 0.1875
- key_weight: bfloat16 [1024, 1024], P('dp'), may hold values from -0.1875 to 0.1875
- value_matrix: bfloat16 [1024, 1024], P('dp'), may hold values from -0.1875 to 0.1875
- query_gain: bfloat16 [128], P('dp'), may hold values from 0.59765625 to 1.59375
- key_gain: bfloat16 [128], P('dp'), may hold values from 0.59765625 to 1.59375
- out_weight: bfloat16 [2048, 1024], P('dp'), may hold values from -1 to 1
- second_gain: bfloat16 [1024], P('dp'), may hold values from 0.29882812 to 3
- gate_weight: bfloat16 [1024, 3072], P('dp'), may hold values from -0.1875 to 0.1875
- up_weight: bfloat16 [1024, 3072], P('dp'), may hold values from -0.1875 to 0.1875
- down_weight: bfloat16 [3072, 1024], P('dp'), may hold values from -0.109375 to 0.109375
- grad_out: bfloat16 [8, 1024, 1024], P('dp', 'seq'), may hold values from -6 to 6
Outputs:
- block_out: bfloat16 [8, 1024, 1024], P('dp', 'seq')
- input_grad: float32 [8, 1024, 1024], P('dp', 'seq')
- first_gain_grad: float32 [1024], P('dp')
- query_weight_grad: float32 [1024, 2048], P('dp')
- key_weight_grad: float32 [1024, 1024], P('dp')
- value_weight_grad: float32 [1024, 1024], P('dp')
- query_gain_grad: float32 [128], P('dp')
- key_gain_grad: float32 [128], P('dp')
- out_weight_grad: float32 [2048, 1024], P('dp')
- second_gain_grad: float32 [1024], P('dp')
- gate_weight_grad: float32 [1024, 3072], P('dp')
- up_weight_grad: float32 [1024, 3072], P('dp')
- down_weight_grad: float32 [3072, 1024], P('dp')
The draws below stay inside these ranges and needn't reach their ends.
Inputs may be any that keep to these rules, and one draw needn't show every extreme that they name: positions start at 0 in every sequence and rise by 1 or 2 from token to token. `doc_ids`: document numbers never fall along a sequence; each document is 1 to 512 tokens long.
All inputs are finite; a program needn't handle non-finite values.
Results may differ from the reference program's by a relative error of at most 0.015.
Values may be sent and summed in bfloat16 or wider, within the bound.
No kernel may reach another device: no remote copies, remote signals or barrier semaphores. Data moves between devices by JAX's collectives and lax.ppermute only.
A program may use at most 256 MiB of HBM per device.

```python
import math
import jax
import jax.numpy as jnp
import numpy as np
from jax import lax

MODEL_DIM = 1024
QUERY_HEADS = 16
KEY_VALUE_HEADS = 8
HEAD_SIZE = 128
FF = 3072
LEN = 1024
DOCS = 4
SEQS = 8


def draw_positions(key, part):
    increments = jax.random.randint(key, (SEQS, LEN), 1, 3)
    first_row = jnp.arange(SEQS, dtype=jnp.int32)[:, None] == 0
    increments = jnp.where(first_row, 2, increments).astype(jnp.int32)
    return (jnp.cumsum(increments, axis=1) - increments[:, :1]).astype(jnp.int32)


def levels(rng, extent, cuts, least, high):
    def one(position, parts):
        steps = jax.random.uniform(jax.random.fold_in(jax.random.fold_in(rng, 6), position), (parts,), jnp.float32, least / len(cuts), high / len(cuts))
        return jnp.repeat(jnp.exp(steps), extent[position] // parts).reshape((-1,) + (1,) * (len(extent) - position - 1))

    factor_of = one(*cuts[0])
    for cut in cuts[1:]:
        factor_of = factor_of * one(*cut)
    return factor_of


def split_up(amount, total, most, lean):
    portions = [(1 << 20) // math.isqrt(standing ** lean) + 1 for standing in range(2, amount + 1)]
    spare, holding = total - most - (amount - 1), [1] * (amount - 1)
    while spare > 0:
        candidates = [i for i in range(amount - 1) if holding[i] < most]
        whole, remaining = sum([portions[i] for i in candidates]), spare
        for i in candidates:
            more = min(most - holding[i], max(1, remaining * portions[i] // whole), spare)
            holding[i] = holding[i] + more
            spare = spare - more
    return np.array([most] + holding)


def ragged_sizes(own_key, number_of, total, reach, skew):
    if number_of == 2:
        one = jax.random.randint(own_key, (), max(1, total - reach), min(reach, total - 1) + 1)
        return jnp.stack([one, total - one])
    sizes = jnp.asarray(split_up(number_of, total, reach, skew), jnp.int32)
    couples = (number_of - 1) // 2
    donor, taker = sizes[1:1 + 2 * couples:2], sizes[2:2 + 2 * couples:2]
    margin = jnp.minimum(donor - 1, reach - taker)
    shifted = jax.random.randint(jax.random.fold_in(own_key, 1), (couples,), 0, 1 << 20) % (margin + 1)
    sizes = sizes.at[1:1 + 2 * couples:2].set(donor - shifted).at[2:2 + 2 * couples:2].set(taker + shifted)
    return sizes[jax.random.permutation(jax.random.fold_in(own_key, 2), number_of)]


def normal_values(own_key, dims, scale, most, split=(), held_as=jnp.bfloat16):
    values = jax.random.normal(own_key, dims, jnp.float32) * scale
    if len(split) > 0:
        values = levels(own_key, dims, split, -0.22, 0.18) * values
    return jnp.clip(values, min=-most, max=most).astype(held_as)


def setup_inputs(seed: int = 0) -> dict:
    key_list = jax.random.split(jax.random.key(seed), 16)
    block_in = normal_values(key_list[0], (SEQS, LEN, MODEL_DIM), 1.0, 6.0, ((0, 8), (1, 4)))
    positions = draw_positions(jax.random.fold_in(key_list[15], 71), 0)
    doc_ids = jax.vmap(lambda own: jnp.searchsorted(jnp.cumsum(ragged_sizes(own, DOCS, LEN, LEN // 2, 1)), jnp.arange(LEN), side="right"))(jax.random.split(key_list[2], SEQS)).reshape((SEQS, LEN)).astype(jnp.int32)
    first_gain = jnp.clip(jnp.exp(math.log(3.0) - 2.306499 * jax.random.uniform(key_list[3], (MODEL_DIM,), jnp.float32) ** levels(key_list[3], (MODEL_DIM,), ((0, 8),), -0.2, 0.2)), 0.29882812, 3.0).astype(jnp.bfloat16)
    query_weight = normal_values(key_list[4], (MODEL_DIM, QUERY_HEADS * HEAD_SIZE), MODEL_DIM ** -0.5, 0.1875, ((0, 8),))
    key_weight = normal_values(key_list[5], (MODEL_DIM, KEY_VALUE_HEADS * HEAD_SIZE), MODEL_DIM ** -0.5, 0.1875, ((0, 8),))
    value_matrix = normal_values(key_list[6], (MODEL_DIM, KEY_VALUE_HEADS * HEAD_SIZE), MODEL_DIM ** -0.5, 0.1875, ((0, 8),))
    query_gain = jnp.clip(jnp.exp(math.log(1.59375) - 0.98082925 * jax.random.uniform(key_list[7], (HEAD_SIZE,), jnp.float32) ** levels(key_list[7], (HEAD_SIZE,), ((0, 8),), -0.2, 0.2)), 0.59765625, 1.59375).astype(jnp.bfloat16)
    key_gain = jnp.clip(jnp.exp(math.log(1.59375) - 0.98082925 * jax.random.uniform(key_list[8], (HEAD_SIZE,), jnp.float32) ** levels(key_list[8], (HEAD_SIZE,), ((0, 8),), -0.2, 0.2)), 0.59765625, 1.59375).astype(jnp.bfloat16)
    out_weight = normal_values(key_list[9], (QUERY_HEADS * HEAD_SIZE, MODEL_DIM), (QUERY_HEADS * HEAD_SIZE // 64) ** -0.5, 1.0, ((0, 8),))
    second_gain = jnp.clip(jnp.exp(math.log(3.0) - 2.306499 * jax.random.uniform(key_list[10], (MODEL_DIM,), jnp.float32) ** levels(key_list[10], (MODEL_DIM,), ((0, 8),), -0.2, 0.2)), 0.29882812, 3.0).astype(jnp.bfloat16)
    gate_weight = normal_values(key_list[11], (MODEL_DIM, FF), MODEL_DIM ** -0.5, 0.1875, ((0, 8),))
    up_weight = normal_values(key_list[12], (MODEL_DIM, FF), MODEL_DIM ** -0.5, 0.1875, ((0, 8),))
    down_weight = normal_values(key_list[13], (FF, MODEL_DIM), FF ** -0.5, 0.109375, ((0, 8),))
    grad_out = normal_values(key_list[14], (SEQS, LEN, MODEL_DIM), 1.0, 6.0, ((0, 8), (1, 4)))
    return {"block_in": block_in, "positions": positions, "doc_ids": doc_ids, "first_gain": first_gain, "query_weight": query_weight, "key_weight": key_weight, "value_matrix": value_matrix, "query_gain": query_gain, "key_gain": key_gain, "out_weight": out_weight, "second_gain": second_gain, "gate_weight": gate_weight, "up_weight": up_weight, "down_weight": down_weight, "grad_out": grad_out}


EPSILON = 1e-06
THETA = 1000000.0

def product(einsum_form, left_side, right_side):
    return jnp.einsum(einsum_form, left_side.astype(jnp.float32), right_side.astype(jnp.float32))

def normalize(values):
    inverse = lax.rsqrt(lax.optimization_barrier(jnp.mean(values * values, axis=-1, keepdims=True)) + EPSILON)
    return (values * inverse, inverse)

def norm_backward(upstream, unit_rows, inverse, gain_values):
    scaled = upstream * gain_values
    return inverse * (scaled - unit_rows * lax.optimization_barrier(jnp.mean(scaled * unit_rows, axis=-1, keepdims=True)))

def rope_tables(positions, head_dim):
    half_dim = head_dim // 2
    inverse_freq = 1.0 / THETA ** (jnp.arange(half_dim, dtype=jnp.float32) * 2.0 / head_dim)
    angles = positions.astype(jnp.float32)[..., None] * inverse_freq
    return (jnp.cos(angles)[..., None, :], jnp.sin(angles)[..., None, :])

def rotate(values, cosine, sine):
    half_dim = values.shape[-1] // 2
    first_half = values[..., :half_dim]
    second_half = values[..., half_dim:]
    return jnp.concatenate([first_half * cosine - second_half * sine, second_half * cosine + first_half * sine], axis=-1)

def block_mask(doc_ids, first_row, last_row):
    query_index = jnp.arange(first_row, last_row)[:, None]
    key_index = jnp.arange(last_row)[None, :]
    causal = key_index <= query_index
    same_doc = doc_ids[:, first_row:last_row, None] == doc_ids[:, None, :last_row]
    return (causal[None] & same_doc)[:, None, None]

def attend_forward(grouped, key_rows, value_rows, doc_ids):
    full_len = grouped.shape[1]
    block_rows = min(512, full_len)
    scale = grouped.shape[-1] ** (-0.5)
    outputs = []
    logs = []
    for first_row in range(0, full_len, block_rows):
        last_row = first_row + block_rows
        allowed = block_mask(doc_ids, first_row, last_row)
        scores = product('bqkgd,btkd->bkgqt', grouped[:, first_row:last_row], key_rows[:, :last_row]) * scale
        masked = jnp.where(allowed, scores, -jnp.inf)
        largest = lax.optimization_barrier(jnp.max(masked, axis=-1, keepdims=True))
        log_block = largest + jnp.log(lax.optimization_barrier(jnp.sum(jnp.exp(masked - largest), axis=-1, keepdims=True)))
        probs = jnp.exp(masked - log_block).astype(jnp.bfloat16)
        outputs.append(product('bkgqt,btkd->bqkgd', probs, value_rows[:, :last_row]).astype(jnp.bfloat16))
        logs.append(log_block)
    return (jnp.concatenate(outputs, axis=1), jnp.concatenate(logs, axis=3))

def attend_backward(grouped, key_rows, value_rows, doc_ids, log_totals, grouped_grad):
    full_len = grouped.shape[1]
    block_rows = min(512, full_len)
    scale = grouped.shape[-1] ** (-0.5)
    key_acc = jnp.zeros(key_rows.shape, jnp.float32)
    value_acc = jnp.zeros(value_rows.shape, jnp.float32)
    query_parts = []
    for first_row in range(0, full_len, block_rows):
        last_row = first_row + block_rows
        allowed = block_mask(doc_ids, first_row, last_row)
        scores = product('bqkgd,btkd->bkgqt', grouped[:, first_row:last_row], key_rows[:, :last_row]) * scale
        weights = jnp.exp(jnp.where(allowed, scores, -jnp.inf) - log_totals[:, :, :, first_row:last_row])
        grad_block = grouped_grad[:, first_row:last_row]
        value_acc = value_acc.at[:, :last_row].add(product('bkgqt,bqkgd->btkd', weights.astype(jnp.bfloat16), grad_block))
        prob_grad = product('bqkgd,btkd->bkgqt', grad_block, value_rows[:, :last_row])
        row_delta = lax.optimization_barrier(jnp.sum(weights * prob_grad, axis=-1, keepdims=True))
        score_grad = (weights * (prob_grad - row_delta) * scale).astype(jnp.bfloat16)
        query_parts.append(product('bkgqt,btkd->bqkgd', score_grad, key_rows[:, :last_row]).astype(jnp.bfloat16))
        key_acc = key_acc.at[:, :last_row].add(product('bkgqt,bqkgd->btkd', score_grad, grouped[:, first_row:last_row]))
    return (jnp.concatenate(query_parts, axis=1), key_acc.astype(jnp.bfloat16), value_acc.astype(jnp.bfloat16))

def layer(block_in, positions, doc_ids, grad_out, params):
    first_gain, query_weight, key_weight, value_matrix, query_gain, key_gain, out_weight, second_gain, gate_weight, up_weight, down_weight = params
    seq_count, seq_len, model_width = block_in.shape
    head_dim = query_gain.shape[0]
    query_heads = query_weight.shape[1] // head_dim
    kv_heads = key_weight.shape[1] // head_dim
    group_size = query_heads // kv_heads
    residual = block_in.astype(jnp.float32)
    first_unit, first_inverse = normalize(residual)
    first_normed = (first_unit * first_gain.astype(jnp.float32)).astype(jnp.bfloat16)
    query_raw = product('bld,de->ble', first_normed, query_weight).reshape(seq_count, seq_len, query_heads, head_dim)
    key_raw = product('bld,de->ble', first_normed, key_weight).reshape(seq_count, seq_len, kv_heads, head_dim)
    value_rows = product('bld,de->ble', first_normed, value_matrix).astype(jnp.bfloat16).reshape(seq_count, seq_len, kv_heads, head_dim)
    query_unit, query_inverse = normalize(query_raw)
    key_unit, key_inverse = normalize(key_raw)
    cosine, sine = rope_tables(positions, head_dim)
    query_rot = rotate(query_unit * query_gain.astype(jnp.float32), cosine, sine).astype(jnp.bfloat16)
    key_rot = rotate(key_unit * key_gain.astype(jnp.float32), cosine, sine).astype(jnp.bfloat16)
    grouped = query_rot.reshape(seq_count, seq_len, kv_heads, group_size, head_dim)
    attended, log_totals = attend_forward(grouped, key_rot, value_rows, doc_ids)
    attended_flat = attended.reshape(seq_count, seq_len, query_heads * head_dim)
    middle = residual + product('ble,ed->bld', attended_flat, out_weight)
    second_unit, second_inverse = normalize(middle)
    second_normed = (second_unit * second_gain.astype(jnp.float32)).astype(jnp.bfloat16)
    gate_pre = product('bld,df->blf', second_normed, gate_weight)
    up_pre = product('bld,df->blf', second_normed, up_weight)
    sigmoid_gate = jax.nn.sigmoid(gate_pre)
    silu_gate = gate_pre * sigmoid_gate
    hidden = (silu_gate * up_pre).astype(jnp.bfloat16)
    block_out = (middle + product('blf,fd->bld', hidden, down_weight)).astype(jnp.bfloat16)
    down_weight_grad = product('blf,bld->fd', hidden, grad_out)
    hidden_grad = product('bld,fd->blf', grad_out, down_weight)
    gate_pre_grad = (hidden_grad * up_pre * sigmoid_gate * (1.0 + gate_pre * (1.0 - sigmoid_gate))).astype(jnp.bfloat16)
    up_pre_grad = (hidden_grad * silu_gate).astype(jnp.bfloat16)
    gate_weight_grad = product('bld,blf->df', second_normed, gate_pre_grad)
    up_weight_grad = product('bld,blf->df', second_normed, up_pre_grad)
    normed_grad = product('blf,df->bld', gate_pre_grad, gate_weight) + product('blf,df->bld', up_pre_grad, up_weight)
    second_gain_grad = lax.optimization_barrier(jnp.sum(normed_grad * second_unit, axis=(0, 1)))
    middle_grad = grad_out.astype(jnp.float32) + norm_backward(normed_grad, second_unit, second_inverse, second_gain.astype(jnp.float32))
    middle_low = middle_grad.astype(jnp.bfloat16)
    out_weight_grad = product('ble,bld->ed', attended_flat, middle_low)
    attended_grad = product('bld,ed->ble', middle_low, out_weight).astype(jnp.bfloat16)
    grouped_grad = attended_grad.reshape(seq_count, seq_len, kv_heads, group_size, head_dim)
    query_rot_grad, key_rot_grad, value_grad = attend_backward(grouped, key_rot, value_rows, doc_ids, log_totals, grouped_grad)
    query_scaled_grad = rotate(query_rot_grad.reshape(seq_count, seq_len, query_heads, head_dim).astype(jnp.float32), cosine, -sine)
    key_scaled_grad = rotate(key_rot_grad.astype(jnp.float32), cosine, -sine)
    query_gain_grad = lax.optimization_barrier(jnp.sum(query_scaled_grad * query_unit, axis=(0, 1, 2)))
    key_gain_grad = lax.optimization_barrier(jnp.sum(key_scaled_grad * key_unit, axis=(0, 1, 2)))
    query_raw_grad = norm_backward(query_scaled_grad, query_unit, query_inverse, query_gain.astype(jnp.float32)).astype(jnp.bfloat16).reshape(seq_count, seq_len, query_heads * head_dim)
    key_raw_grad = norm_backward(key_scaled_grad, key_unit, key_inverse, key_gain.astype(jnp.float32)).astype(jnp.bfloat16).reshape(seq_count, seq_len, kv_heads * head_dim)
    value_flat = value_grad.reshape(seq_count, seq_len, kv_heads * head_dim)
    query_weight_grad = product('bld,ble->de', first_normed, query_raw_grad)
    key_weight_grad = product('bld,ble->de', first_normed, key_raw_grad)
    value_weight_grad = product('bld,ble->de', first_normed, value_flat)
    first_normed_grad = product('ble,de->bld', query_raw_grad, query_weight) + product('ble,de->bld', key_raw_grad, key_weight) + product('ble,de->bld', value_flat, value_matrix)
    first_gain_grad = lax.optimization_barrier(jnp.sum(first_normed_grad * first_unit, axis=(0, 1)))
    input_grad = middle_grad + norm_backward(first_normed_grad, first_unit, first_inverse, first_gain.astype(jnp.float32))
    grads = (first_gain_grad, query_weight_grad, key_weight_grad, value_weight_grad, query_gain_grad, key_gain_grad, out_weight_grad, second_gain_grad, gate_weight_grad, up_weight_grad, down_weight_grad)
    return (block_out, input_grad, grads)

def reference(block_in, positions, doc_ids, first_gain, query_weight, key_weight, value_matrix, query_gain, key_gain, out_weight, second_gain, gate_weight, up_weight, down_weight, grad_out):
    seq_total = block_in.shape[0]
    seq_len = block_in.shape[1]
    group_count = math.gcd(seq_total, max(1, 4096 // seq_len))
    params = (first_gain, query_weight, key_weight, value_matrix, query_gain, key_gain, out_weight, second_gain, gate_weight, up_weight, down_weight)

    def grouped_rows(array):
        return array.reshape((seq_total // group_count, group_count) + array.shape[1:])
    initial = tuple((jnp.zeros(param.shape, jnp.float32) for param in params))

    def scan_step(carry, items):
        block_part, position_part, doc_part, grad_part = items
        out_part, input_part, grads = layer(block_part, position_part, doc_part, grad_part, params)
        return (tuple((held + added for held, added in zip(carry, grads))), (out_part, input_part))
    totals, (outputs, input_grads) = lax.scan(scan_step, initial, (grouped_rows(block_in), grouped_rows(positions), grouped_rows(doc_ids), grouped_rows(grad_out)))
    return (outputs.reshape(block_in.shape), input_grads.reshape(block_in.shape), totals[0], totals[1], totals[2], totals[3], totals[4], totals[5], totals[6], totals[7], totals[8], totals[9], totals[10])
```

```python
import jax
import jax.numpy as jnp
from jax import lax
from jax.sharding import PartitionSpec as P

EPSILON = 1e-06
THETA = 1000000.0


def product(einsum_form, left_side, right_side):
    return jnp.einsum(einsum_form, left_side, right_side, preferred_element_type=jnp.float32)


def normalize(values):
    inverse = lax.rsqrt(jnp.mean(values * values, axis=-1, keepdims=True) + EPSILON)
    return (values * inverse, inverse)


def norm_backward(upstream, unit_rows, inverse, gain_values):
    scaled = upstream * gain_values
    return inverse * (scaled - unit_rows * jnp.mean(scaled * unit_rows, axis=-1, keepdims=True))


def rope_tables(positions, head_dim):
    half_dim = head_dim // 2
    inverse_freq = 1.0 / THETA ** (jnp.arange(half_dim, dtype=jnp.float32) * 2.0 / head_dim)
    angles = positions.astype(jnp.float32)[..., None] * inverse_freq
    return (jnp.cos(angles)[..., None, :], jnp.sin(angles)[..., None, :])


def rotate(values, cosine, sine):
    half_dim = values.shape[-1] // 2
    first_half = values[..., :half_dim]
    second_half = values[..., half_dim:]
    return jnp.concatenate(
        [first_half * cosine - second_half * sine, second_half * cosine + first_half * sine],
        axis=-1,
    )


def block_mask(doc_ids, first_row, last_row):
    query_index = jnp.arange(first_row, last_row)[:, None]
    key_index = jnp.arange(last_row)[None, :]
    causal = key_index <= query_index
    same_doc = doc_ids[:, first_row:last_row, None] == doc_ids[:, None, :last_row]
    return (causal[None] & same_doc)[:, None, None]


def attend_forward(grouped, key_rows, value_rows, doc_ids):
    full_len = grouped.shape[1]
    block_rows = min(512, full_len)
    scale = grouped.shape[-1] ** (-0.5)
    outputs = []
    logs = []
    for first_row in range(0, full_len, block_rows):
        last_row = first_row + block_rows
        allowed = block_mask(doc_ids, first_row, last_row)
        scores = (
            product("bqkgd,btkd->bkgqt", grouped[:, first_row:last_row], key_rows[:, :last_row])
            * scale
        )
        masked = jnp.where(allowed, scores, -jnp.inf)
        largest = jnp.max(masked, axis=-1, keepdims=True)
        log_block = largest + jnp.log(jnp.sum(jnp.exp(masked - largest), axis=-1, keepdims=True))
        probs = jnp.exp(masked - log_block).astype(jnp.bfloat16)
        outputs.append(
            product("bkgqt,btkd->bqkgd", probs, value_rows[:, :last_row]).astype(jnp.bfloat16)
        )
        logs.append(log_block)
    return (jnp.concatenate(outputs, axis=1), jnp.concatenate(logs, axis=3))


def attend_backward(grouped, key_rows, value_rows, doc_ids, log_totals, grouped_grad):
    full_len = grouped.shape[1]
    block_rows = min(512, full_len)
    scale = grouped.shape[-1] ** (-0.5)
    key_acc = jnp.zeros(key_rows.shape, jnp.float32)
    value_acc = jnp.zeros(value_rows.shape, jnp.float32)
    query_parts = []
    for first_row in range(0, full_len, block_rows):
        last_row = first_row + block_rows
        allowed = block_mask(doc_ids, first_row, last_row)
        scores = (
            product("bqkgd,btkd->bkgqt", grouped[:, first_row:last_row], key_rows[:, :last_row])
            * scale
        )
        weights = jnp.exp(
            jnp.where(allowed, scores, -jnp.inf) - log_totals[:, :, :, first_row:last_row]
        )
        grad_block = grouped_grad[:, first_row:last_row]
        value_acc = value_acc.at[:, :last_row].add(
            product("bkgqt,bqkgd->btkd", weights.astype(jnp.bfloat16), grad_block)
        )
        prob_grad = product("bqkgd,btkd->bkgqt", grad_block, value_rows[:, :last_row])
        row_delta = jnp.sum(weights * prob_grad, axis=-1, keepdims=True)
        score_grad = (weights * (prob_grad - row_delta) * scale).astype(jnp.bfloat16)
        query_parts.append(
            product("bkgqt,btkd->bqkgd", score_grad, key_rows[:, :last_row]).astype(jnp.bfloat16)
        )
        key_acc = key_acc.at[:, :last_row].add(
            product("bkgqt,bqkgd->btkd", score_grad, grouped[:, first_row:last_row])
        )
    return (
        jnp.concatenate(query_parts, axis=1),
        key_acc.astype(jnp.bfloat16),
        value_acc.astype(jnp.bfloat16),
    )


def exchange(pieces):
    return lax.all_to_all(pieces, "seq", split_axis=0, concat_axis=0, tiled=True)


def gather_tokens(rows, seq_size):
    spread = jnp.broadcast_to(rows[None], (seq_size,) + rows.shape)
    received = exchange(spread)
    return received.reshape((seq_size * rows.shape[0],) + rows.shape[1:])


def scatter_tokens(partial, seq_size):
    pieces = partial.astype(jnp.bfloat16).reshape((seq_size, -1) + partial.shape[1:])
    return jnp.sum(exchange(pieces).astype(jnp.float32), axis=0)


def row_routes(dp_size, seq_size):
    routes = []
    for dp_index in range(dp_size):
        for seq_index in range(seq_size):
            holder = dp_size // seq_size * seq_index + dp_index // seq_size
            routes.append(
                (holder * seq_size + dp_index % seq_size, dp_index * seq_size + seq_index)
            )
    return routes


def on_device(
    block_in,
    positions,
    doc_ids,
    first_gain,
    query_weight,
    key_weight,
    value_matrix,
    query_gain,
    key_gain,
    out_weight,
    second_gain,
    gate_weight,
    up_weight,
    down_weight,
    grad_out,
):
    bf16 = jnp.bfloat16
    f32 = jnp.float32
    dp_size = lax.axis_size("dp")
    seq_size = lax.axis_size("seq")
    seq_index = lax.axis_index("seq")
    seq_count, local_len, model_width = block_in.shape
    full_len = local_len * seq_size
    head_dim = query_gain.shape[0] * dp_size
    query_heads = query_weight.shape[1] // head_dim
    kv_heads = key_weight.shape[1] // head_dim
    group_size = query_heads // kv_heads
    local_kv = kv_heads // seq_size
    local_heads = query_heads // seq_size
    query_cols = local_heads * head_dim
    kv_cols = local_kv * head_dim
    ff_cols = gate_weight.shape[1] // seq_size
    routes = row_routes(dp_size, seq_size)
    back_routes = [(target, source) for source, target in routes]

    def own_columns(matrix, width):
        return lax.dynamic_slice_in_dim(matrix, seq_index * width, width, axis=1)

    def own_rows(matrix):
        count = matrix.shape[0] // seq_size
        piece = lax.dynamic_slice_in_dim(matrix, seq_index * count, count, axis=0)
        return lax.ppermute(piece, ("dp", "seq"), routes)

    x_local = block_in[0]
    x_full = gather_tokens(x_local, seq_size)
    attn_piece = jnp.concatenate(
        [
            own_columns(query_weight, query_cols),
            own_columns(key_weight, kv_cols),
            own_columns(value_matrix, kv_cols),
        ],
        axis=1,
    )
    attn_full = lax.all_gather(attn_piece, "dp", axis=0, tiled=True)
    gains = jnp.concatenate([first_gain, second_gain, query_gain, key_gain])[None]
    gains_full = lax.all_gather(gains, "dp", axis=0, tiled=True).astype(f32)
    share = first_gain.shape[0]
    head_share = query_gain.shape[0]
    first_full = gains_full[:, :share].reshape(-1)
    second_full = gains_full[:, share : 2 * share].reshape(-1)
    query_gain_full = gains_full[:, 2 * share : 2 * share + head_share].reshape(-1)
    key_gain_full = gains_full[:, 2 * share + head_share :].reshape(-1)
    positions_full = gather_tokens(positions, seq_size).reshape(1, full_len)
    out_full = lax.all_gather(out_weight, "dp", axis=0, tiled=True)
    grad_full = gather_tokens(grad_out[0], seq_size)
    mlp_piece = jnp.concatenate(
        [own_columns(gate_weight, ff_cols), own_columns(up_weight, ff_cols)], axis=1
    )
    mlp_full = lax.all_gather(mlp_piece, "dp", axis=0, tiled=True)
    down_full = lax.all_gather(own_rows(down_weight), "dp", axis=0, tiled=True)

    residual_full = x_full.astype(f32)
    unit_full, _ = normalize(residual_full)
    normed_full = (unit_full * first_full).astype(bf16)
    raw = product("ld,de->le", normed_full, attn_full)
    query_raw = raw[:, :query_cols].reshape(1, full_len, local_heads, head_dim)
    key_raw = raw[:, query_cols : query_cols + kv_cols].reshape(1, full_len, local_kv, head_dim)
    value_rows = (
        raw[:, query_cols + kv_cols :].astype(bf16).reshape(1, full_len, local_kv, head_dim)
    )
    query_unit, query_inverse = normalize(query_raw)
    key_unit, key_inverse = normalize(key_raw)
    cosine, sine = rope_tables(positions_full, head_dim)
    query_rot = rotate(query_unit * query_gain_full, cosine, sine).astype(bf16)
    key_rot = rotate(key_unit * key_gain_full, cosine, sine).astype(bf16)
    grouped = query_rot.reshape(1, full_len, local_kv, group_size, head_dim)
    attended, log_totals = attend_forward(grouped, key_rot, value_rows, doc_ids)
    attended_heads = attended.reshape(full_len, query_cols)
    attended_tokens = exchange(attended_heads.reshape(seq_size, local_len, query_cols))
    out_parts = out_full.reshape(seq_size, query_cols, model_width)
    residual = x_local.astype(f32)
    middle = residual + product("sle,sed->ld", attended_tokens, out_parts)
    second_unit, second_inverse = normalize(middle)
    second_normed = gather_tokens((second_unit * second_full).astype(bf16), seq_size)
    gate_up = product("ld,df->lf", second_normed, mlp_full)
    gate_pre = gate_up[:, :ff_cols]
    up_pre = gate_up[:, ff_cols:]
    sigmoid_gate = jax.nn.sigmoid(gate_pre)
    silu_gate = gate_pre * sigmoid_gate
    hidden = (silu_gate * up_pre).astype(bf16)
    hidden_grad = product("ld,fd->lf", grad_full, down_full)
    gate_pre_grad = (
        hidden_grad * up_pre * sigmoid_gate * (1.0 + gate_pre * (1.0 - sigmoid_gate))
    ).astype(bf16)
    up_pre_grad = (hidden_grad * silu_gate).astype(bf16)
    gate_up_grad = jnp.concatenate([gate_pre_grad, up_pre_grad], axis=1)
    normed_grad = scatter_tokens(product("lf,df->ld", gate_up_grad, mlp_full), seq_size)
    second_gain_grad = jnp.sum(normed_grad * second_unit, axis=0)
    middle_grad = grad_out[0].astype(f32) + norm_backward(
        normed_grad, second_unit, second_inverse, second_full
    )
    middle_low = middle_grad.astype(bf16)
    attended_grad = product("ld,sed->sle", middle_low, out_parts).astype(bf16)
    head_grad = exchange(attended_grad)
    grouped_grad = head_grad.reshape(1, full_len, local_kv, group_size, head_dim)

    def scatter_grad(partial):
        return lax.psum_scatter(
            partial.astype(bf16), "dp", scatter_dimension=0, tiled=True
        )

    mlp_grad = scatter_grad(product("ld,lf->df", second_normed, gate_up_grad))
    down_grad = scatter_grad(product("lf,ld->fd", hidden, grad_full))
    block_out = (
        middle + scatter_tokens(product("lf,fd->ld", hidden, down_full), seq_size)
    ).astype(bf16)
    middle_low_full = gather_tokens(middle_low, seq_size)
    out_grad = scatter_grad(product("le,ld->ed", attended_heads, middle_low_full))

    query_rot_grad, key_rot_grad, value_grad = attend_backward(
        grouped, key_rot, value_rows, doc_ids, log_totals, grouped_grad
    )
    query_scaled_grad = rotate(
        query_rot_grad.reshape(1, full_len, local_heads, head_dim).astype(f32), cosine, -sine
    )
    key_scaled_grad = rotate(key_rot_grad.astype(f32), cosine, -sine)
    query_gain_grad = jnp.sum(query_scaled_grad * query_unit, axis=(0, 1, 2))
    key_gain_grad = jnp.sum(key_scaled_grad * key_unit, axis=(0, 1, 2))
    query_raw_grad = norm_backward(
        query_scaled_grad, query_unit, query_inverse, query_gain_full
    ).astype(bf16)
    key_raw_grad = norm_backward(key_scaled_grad, key_unit, key_inverse, key_gain_full).astype(
        bf16
    )
    raw_grad = jnp.concatenate(
        [
            query_raw_grad.reshape(full_len, query_cols),
            key_raw_grad.reshape(full_len, kv_cols),
            value_grad.reshape(full_len, kv_cols),
        ],
        axis=1,
    )
    attn_grad = scatter_grad(product("ld,le->de", normed_full, raw_grad))
    first_normed_grad = scatter_tokens(product("le,de->ld", raw_grad, attn_full), seq_size)
    first_unit, first_inverse = normalize(residual)
    first_gain_grad = jnp.sum(first_normed_grad * first_unit, axis=0)
    input_grad = middle_grad + norm_backward(
        first_normed_grad, first_unit, first_inverse, first_full
    )
    gain_sums = lax.psum(
        jnp.concatenate([first_gain_grad, second_gain_grad, query_gain_grad, key_gain_grad]),
        ("dp", "seq"),
    )
    dp_index = lax.axis_index("dp")

    def own_gain(first, width):
        return lax.dynamic_slice_in_dim(gain_sums, first + dp_index * width, width, axis=0)

    def gather_columns(piece):
        spread = jnp.broadcast_to(piece[None], (seq_size,) + piece.shape)
        received = exchange(spread).astype(f32)
        return jnp.swapaxes(received, 0, 1)

    def gather_rows(piece):
        home = lax.ppermute(piece, ("dp", "seq"), back_routes)
        return gather_tokens(home, seq_size).astype(f32)

    mlp_parts = gather_columns(mlp_grad)
    gate_weight_grad = mlp_parts[:, :, :ff_cols].reshape(gate_weight.shape)
    up_weight_grad = mlp_parts[:, :, ff_cols:].reshape(up_weight.shape)
    down_weight_grad = gather_rows(down_grad)
    out_weight_grad = gather_rows(out_grad)
    attn_parts = gather_columns(attn_grad)
    query_weight_grad = attn_parts[:, :, :query_cols].reshape(query_weight.shape)
    key_weight_grad = attn_parts[:, :, query_cols : query_cols + kv_cols].reshape(
        key_weight.shape
    )
    value_weight_grad = attn_parts[:, :, query_cols + kv_cols :].reshape(value_matrix.shape)
    return (
        block_out[None],
        input_grad[None],
        own_gain(0, share),
        query_weight_grad,
        key_weight_grad,
        value_weight_grad,
        own_gain(2 * model_width, head_share),
        own_gain(2 * model_width + head_dim, head_share),
        out_weight_grad,
        own_gain(model_width, share),
        gate_weight_grad,
        up_weight_grad,
        down_weight_grad,
    )


def solution(mesh):
    placed = (
        P("dp", "seq", None),
        P("dp", "seq"),
        P("dp", None),
        P("dp"),
        P("dp", None),
        P("dp", None),
        P("dp", None),
        P("dp"),
        P("dp"),
        P("dp", None),
        P("dp"),
        P("dp", None),
        P("dp", None),
        P("dp", None),
        P("dp", "seq", None),
    )
    return jax.shard_map(
        on_device,
        mesh=mesh,
        in_specs=placed,
        out_specs=(
            P("dp", "seq", None),
            P("dp", "seq", None),
            P("dp"),
            P("dp", None),
            P("dp", None),
            P("dp", None),
            P("dp"),
            P("dp"),
            P("dp", None),
            P("dp"),
            P("dp", None),
            P("dp", None),
            P("dp", None),
        ),
        check_vma=False,
    )
```

```python
import functools

import jax
import jax.numpy as jnp
from jax import lax
from jax.experimental import pallas as pl
from jax.experimental.pallas import tpu as pltpu
from jax.sharding import PartitionSpec as P

EPSILON = 1e-06
THETA = 1000000.0
LOG2E = 1.4426950408889634
GAIN_ROWS = 16
VMEM_LIMIT = 60 * 1024 * 1024


def product(einsum_form, left_side, right_side):
    return jnp.einsum(einsum_form, left_side, right_side, preferred_element_type=jnp.float32)


def dot(left, right, contract):
    return lax.dot_general(
        left, right, (contract, ((), ())), preferred_element_type=jnp.float32
    )


def dot_nn(left, right):
    return dot(left, right, ((1,), (0,)))


def dot_nt(left, right):
    return dot(left, right, ((1,), (1,)))


def normalize(values):
    inverse = lax.rsqrt(jnp.mean(values * values, axis=-1, keepdims=True) + EPSILON)
    return (values * inverse, inverse)


def norm_backward(upstream, unit_rows, inverse, gain_values):
    scaled = upstream * gain_values
    return inverse * (scaled - unit_rows * jnp.mean(scaled * unit_rows, axis=-1, keepdims=True))


def rope_tables(positions, head_dim):
    half_dim = head_dim // 2
    inverse_freq = 1.0 / THETA ** (jnp.arange(half_dim, dtype=jnp.float32) * 2.0 / head_dim)
    angles = positions.astype(jnp.float32)[:, None] * inverse_freq
    cosine = jnp.cos(angles)
    sine = jnp.sin(angles)
    return (
        jnp.concatenate([cosine, cosine], axis=-1),
        jnp.concatenate([-sine, sine], axis=-1),
    )


def turned(values):
    return pltpu.roll(values, values.shape[-1] // 2, axis=1)


def query_blocks(full_len):
    block = min(256, full_len)
    reach = full_len // 2
    for first in range(0, full_len, block):
        yield first, first + block, max(0, first - reach)


def attn_forward_body(
    x_ref, weight_ref, first_gain_ref, head_gain_ref, cos_ref, sin_ref, doc_row_ref, doc_col_ref,
    normed_ref, raw_ref, rot_ref, attended_ref, inverse_ref,
    *, group_size, head_dim,
):
    bf16 = jnp.bfloat16
    full_len = x_ref.shape[0]
    scale = head_dim ** (-0.5)

    @pl.when(pl.program_id(0) == 0)
    def _():
        block = 256
        for first in range(0, full_len, block):
            unit, _ = normalize(x_ref[first : first + block].astype(jnp.float32))
            normed_ref[first : first + block] = (unit * first_gain_ref[...]).astype(bf16)

    share = weight_ref.shape[1] - GAIN_ROWS
    weight = weight_ref[:, :share, :].reshape(-1, weight_ref.shape[2])
    rot_width = (group_size + 1) * head_dim
    for first in range(0, full_len, 256):
        rows = slice(first, first + 256)
        raw = dot_nn(normed_ref[rows], weight)
        raw_ref[rows] = raw[:, :rot_width]
        rot_ref[rows, rot_width:] = raw[:, rot_width:].astype(bf16)
        for head in range(group_size + 1):
            cols = slice(head * head_dim, (head + 1) * head_dim)
            unit, _ = normalize(raw[:, cols])
            gain = head_gain_ref[:1] if head < group_size else head_gain_ref[1:2]
            scaled = unit * gain
            rot_ref[rows, cols] = (
                scaled * cos_ref[rows] + turned(scaled) * sin_ref[rows]
            ).astype(bf16)
    key = slice(group_size * head_dim, rot_width)
    for first, last, start in query_blocks(full_len):
        keys = rot_ref[start:last, key]
        values = rot_ref[start:last, rot_width:]
        widened = jnp.concatenate([values, jnp.ones_like(values)], axis=1)
        count = last - start
        query_index = lax.broadcasted_iota(jnp.int32, (last - first, count), 0) + first
        key_index = lax.broadcasted_iota(jnp.int32, (last - first, count), 1) + start
        allowed = (key_index <= query_index) & (
            doc_col_ref[first:last] == doc_row_ref[:, start:last]
        )
        for head in range(group_size):
            cols = slice(head * head_dim, (head + 1) * head_dim)
            scores = dot_nt(rot_ref[first:last, cols], keys)
            powers = jnp.where(allowed, jnp.exp2(scores * (scale * LOG2E)), 0.0)
            sums = dot_nn(powers.astype(bf16), widened)
            inverse = 1.0 / sums[:, head_dim:]
            attended_ref[first:last, cols] = (sums[:, :head_dim] * inverse).astype(bf16)
            inverse_ref[head * 8 : (head + 1) * 8, first:last] = inverse.T[:8]


def attn_forward(x_full, weight, first_gain, head_gain, cosine, sine, doc_row, doc_col, sizes):
    group_size, head_dim, local_kv = sizes
    full_len, model_width = x_full.shape
    group_cols = (group_size + 2) * head_dim
    whole = lambda shape: pl.BlockSpec(shape, lambda j: (0,) * len(shape))
    columns = lambda rows, width: pl.BlockSpec((rows, width), lambda j: (0, j))
    rot_width = (group_size + 1) * head_dim
    query_width = group_size * head_dim
    return pl.pallas_call(
        functools.partial(attn_forward_body, group_size=group_size, head_dim=head_dim),
        name="attn_forward",
        grid=(local_kv,),
        in_specs=[
            whole(x_full.shape),
            pl.BlockSpec(weight.shape[:2] + (group_cols,), lambda j: (0, 0, j)),
            whole(first_gain.shape),
            whole(head_gain.shape),
            whole(cosine.shape),
            whole(sine.shape),
            whole(doc_row.shape),
            whole(doc_col.shape),
        ],
        out_specs=[
            whole((full_len, model_width)),
            columns(full_len, rot_width),
            columns(full_len, group_cols),
            columns(full_len, query_width),
            pl.BlockSpec((group_size * 8, full_len), lambda j: (j, 0)),
        ],
        out_shape=[
            jax.ShapeDtypeStruct((full_len, model_width), jnp.bfloat16),
            jax.ShapeDtypeStruct((full_len, local_kv * rot_width), jnp.float32),
            jax.ShapeDtypeStruct((full_len, local_kv * group_cols), jnp.bfloat16),
            jax.ShapeDtypeStruct((full_len, local_kv * query_width), jnp.bfloat16),
            jax.ShapeDtypeStruct((local_kv * group_size * 8, full_len), jnp.float32),
        ],
        compiler_params=pltpu.CompilerParams(vmem_limit_bytes=VMEM_LIMIT),
        cost_estimate=pl.CostEstimate(flops=1000, transcendentals=0, bytes_accessed=1000),
    )(x_full, weight, first_gain, head_gain, cosine, sine, doc_row, doc_col)


def attn_backward_body(
    x_ref, weight_ref, head_gain_ref, cos_ref, sin_ref, doc_row_ref, doc_col_ref,
    raw_ref, rot_ref, inverse_ref, grad_ref,
    raw_grad_ref, normed_grad_ref, first_gain_ref, head_gain_grad_ref,
    acc_ref, query_acc_ref, key_acc_ref, value_acc_ref,
    *, group_size, head_dim,
):
    bf16 = jnp.bfloat16
    full_len = x_ref.shape[0]
    scale = head_dim ** (-0.5)
    step = pl.program_id(0)
    rot_width = (group_size + 1) * head_dim
    key = slice(group_size * head_dim, rot_width)
    key_acc_ref[...] = jnp.zeros_like(key_acc_ref)
    value_acc_ref[...] = jnp.zeros_like(value_acc_ref)
    key_turned = rot_ref[:, key].T
    for first, last, start in query_blocks(full_len):
        keys = rot_ref[start:last, key]
        values = rot_ref[start:last, rot_width:]
        count = last - start
        key_index = lax.broadcasted_iota(jnp.int32, (count, last - first), 0) + start
        query_index = lax.broadcasted_iota(jnp.int32, (count, last - first), 1) + first
        allowed = (key_index <= query_index) & (
            doc_col_ref[start:last] == doc_row_ref[:, first:last]
        )
        for head in range(group_size):
            cols = slice(head * head_dim, (head + 1) * head_dim)
            queries = rot_ref[first:last, cols]
            grads = grad_ref[first:last, cols]
            scores = dot_nt(keys, queries)
            powers = jnp.where(allowed, jnp.exp2(scores * (scale * LOG2E)), 0.0)
            weights = powers * inverse_ref[head * 8 : head * 8 + 1, first:last]
            value_acc_ref[start:last] += dot_nn(weights.astype(bf16), grads)
            prob_grad = dot_nt(values, grads)
            delta = jnp.sum(weights * prob_grad, axis=0, keepdims=True)
            score_grad = (weights * (prob_grad - delta)).astype(bf16)
            key_acc_ref[start:last] += dot_nn(score_grad, queries)
            query_acc_ref[first:last, cols] = dot_nn(key_turned[:, start:last], score_grad).T

    @pl.when(step == 0)
    def _():
        head_gain_grad_ref[...] = jnp.zeros_like(head_gain_grad_ref)
        acc_ref[...] = jnp.zeros_like(acc_ref)

    query_sum = jnp.zeros((1, head_dim), jnp.float32)
    key_sum = jnp.zeros((1, head_dim), jnp.float32)
    for first in range(0, full_len, 256):
        rows = slice(first, first + 256)
        for head in range(group_size + 1):
            cols = slice(head * head_dim, (head + 1) * head_dim)
            is_query = head < group_size
            rot_grad = query_acc_ref[rows, cols] if is_query else key_acc_ref[rows]
            rot_grad = (rot_grad * scale).astype(bf16).astype(jnp.float32)
            scaled_grad = rot_grad * cos_ref[rows] - turned(rot_grad) * sin_ref[rows]
            unit, inverse = normalize(raw_ref[rows, cols])
            part = jnp.sum(scaled_grad * unit, axis=0, keepdims=True)
            if is_query:
                query_sum = query_sum + part
            else:
                key_sum = key_sum + part
            gain = head_gain_ref[:1] if is_query else head_gain_ref[1:2]
            raw_grad_ref[rows, cols] = norm_backward(scaled_grad, unit, inverse, gain).astype(bf16)
        raw_grad_ref[rows, rot_width:] = value_acc_ref[rows].astype(bf16)
    head_gain_grad_ref[:1] += query_sum
    head_gain_grad_ref[1:2] += key_sum

    share = weight_ref.shape[1] - GAIN_ROWS
    weight = weight_ref[:, :share, :].reshape(-1, weight_ref.shape[2])
    for first in range(0, full_len, 256):
        rows = slice(first, first + 256)
        acc_ref[rows] += dot_nt(raw_grad_ref[rows], weight)

    @pl.when(step == pl.num_programs(0) - 1)
    def _():
        gain_sum = jnp.zeros((1, x_ref.shape[1]), jnp.float32)
        for first in range(0, full_len, 256):
            rows = slice(first, first + 256)
            unit, _ = normalize(x_ref[rows].astype(jnp.float32))
            total = acc_ref[rows]
            normed_grad_ref[rows] = total.astype(bf16)
            gain_sum = gain_sum + jnp.sum(total * unit, axis=0, keepdims=True)
        first_gain_ref[...] = gain_sum


def attn_backward(
    x_full, weight, head_gain, cosine, sine, doc_row, doc_col, raw, rot, inverse, grads, sizes
):
    group_size, head_dim, local_kv = sizes
    full_len, model_width = x_full.shape
    group_cols = (group_size + 2) * head_dim
    whole = lambda shape: pl.BlockSpec(shape, lambda j: (0,) * len(shape))
    columns = lambda rows, width: pl.BlockSpec((rows, width), lambda j: (0, j))
    rot_width = (group_size + 1) * head_dim
    query_width = group_size * head_dim
    return pl.pallas_call(
        functools.partial(attn_backward_body, group_size=group_size, head_dim=head_dim),
        name="attn_backward",
        grid=(local_kv,),
        in_specs=[
            whole(x_full.shape),
            pl.BlockSpec(weight.shape[:2] + (group_cols,), lambda j: (0, 0, j)),
            whole(head_gain.shape),
            whole(cosine.shape),
            whole(sine.shape),
            whole(doc_row.shape),
            whole(doc_col.shape),
            columns(full_len, rot_width),
            columns(full_len, group_cols),
            pl.BlockSpec((group_size * 8, full_len), lambda j: (j, 0)),
            columns(full_len, query_width),
        ],
        out_specs=[
            columns(full_len, group_cols),
            whole((full_len, model_width)),
            whole((1, model_width)),
            whole((8, head_dim)),
        ],
        out_shape=[
            jax.ShapeDtypeStruct((full_len, local_kv * group_cols), jnp.bfloat16),
            jax.ShapeDtypeStruct((full_len, model_width), jnp.bfloat16),
            jax.ShapeDtypeStruct((1, model_width), jnp.float32),
            jax.ShapeDtypeStruct((8, head_dim), jnp.float32),
        ],
        scratch_shapes=[
            pltpu.VMEM((full_len, model_width), jnp.float32),
            pltpu.VMEM((full_len, query_width), jnp.float32),
            pltpu.VMEM((full_len, head_dim), jnp.float32),
            pltpu.VMEM((full_len, head_dim), jnp.float32),
        ],
        compiler_params=pltpu.CompilerParams(vmem_limit_bytes=VMEM_LIMIT),
        cost_estimate=pl.CostEstimate(flops=1000, transcendentals=0, bytes_accessed=1000),
    )(x_full, weight, head_gain, cosine, sine, doc_row, doc_col, raw, rot, inverse, grads)


def mlp_body(normed_ref, grad_ref, pair_ref, down_ref, hidden_ref, pair_grad_ref, normed_grad_ref):
    bf16 = jnp.bfloat16
    width = hidden_ref.shape[1]
    pair = dot_nn(normed_ref[...], pair_ref[...])
    hidden_grad = dot_nt(grad_ref[...], down_ref[...])
    gate_pre = pair[:, :width]
    up_pre = pair[:, width:]
    sigmoid_gate = jax.nn.sigmoid(gate_pre)
    silu_gate = gate_pre * sigmoid_gate
    hidden_ref[...] = (silu_gate * up_pre).astype(bf16)
    gate_pre_grad = (
        hidden_grad * up_pre * sigmoid_gate * (1.0 + gate_pre * (1.0 - sigmoid_gate))
    )
    pair_grad_ref[:, :width] = gate_pre_grad.astype(bf16)
    pair_grad_ref[:, width:] = (hidden_grad * silu_gate).astype(bf16)
    normed_grad_ref[...] = dot_nt(pair_grad_ref[...], pair_ref[...]).astype(bf16)


def mlp_forward_backward(normed, grads, pair_weight, down_weight):
    full_len, model_width = normed.shape
    width = down_weight.shape[0]
    block = min(256, full_len)
    rows = lambda cols: pl.BlockSpec((block, cols), lambda i: (i, 0))
    whole = lambda shape: pl.BlockSpec(shape, lambda i: (0, 0))
    return pl.pallas_call(
        mlp_body,
        name="mlp_forward_backward",
        grid=(full_len // block,),
        in_specs=[
            rows(model_width), rows(model_width), whole(pair_weight.shape),
            whole(down_weight.shape),
        ],
        out_specs=[rows(width), rows(2 * width), rows(model_width)],
        out_shape=[
            jax.ShapeDtypeStruct((full_len, width), jnp.bfloat16),
            jax.ShapeDtypeStruct((full_len, 2 * width), jnp.bfloat16),
            jax.ShapeDtypeStruct((full_len, model_width), jnp.bfloat16),
        ],
        compiler_params=pltpu.CompilerParams(vmem_limit_bytes=VMEM_LIMIT),
        cost_estimate=pl.CostEstimate(flops=1000, transcendentals=0, bytes_accessed=1000),
    )(normed, grads, pair_weight, down_weight)


def exchange(pieces):
    return lax.all_to_all(pieces, "seq", split_axis=0, concat_axis=0, tiled=True)


def gather_tokens(rows, seq_size):
    spread = jnp.broadcast_to(rows[None], (seq_size,) + rows.shape)
    received = exchange(spread)
    return received.reshape((seq_size * rows.shape[0],) + rows.shape[1:])


def scatter_tokens(partial, seq_size):
    pieces = partial.astype(jnp.bfloat16).reshape((seq_size, -1) + partial.shape[1:])
    return jnp.sum(exchange(pieces).astype(jnp.float32), axis=0)


def row_routes(dp_size, seq_size):
    routes = []
    for dp_index in range(dp_size):
        for seq_index in range(seq_size):
            holder = dp_size // seq_size * seq_index + dp_index // seq_size
            routes.append(
                (holder * seq_size + dp_index % seq_size, dp_index * seq_size + seq_index)
            )
    return routes


def on_device(
    block_in,
    positions,
    doc_ids,
    first_gain,
    query_weight,
    key_weight,
    value_matrix,
    query_gain,
    key_gain,
    out_weight,
    second_gain,
    gate_weight,
    up_weight,
    down_weight,
    grad_out,
):
    bf16 = jnp.bfloat16
    f32 = jnp.float32
    dp_size = lax.axis_size("dp")
    seq_size = lax.axis_size("seq")
    seq_index = lax.axis_index("seq")
    seq_count, local_len, model_width = block_in.shape
    full_len = local_len * seq_size
    head_dim = query_gain.shape[0] * dp_size
    query_heads = query_weight.shape[1] // head_dim
    kv_heads = key_weight.shape[1] // head_dim
    group_size = query_heads // kv_heads
    local_kv = kv_heads // seq_size
    query_cols = local_kv * group_size * head_dim
    group_cols = (group_size + 2) * head_dim
    ff_cols = gate_weight.shape[1] // seq_size
    share = first_gain.shape[0]
    head_share = query_gain.shape[0]
    gain_width = 2 * share + 2 * head_share
    sizes = (group_size, head_dim, local_kv)
    routes = row_routes(dp_size, seq_size)
    back_routes = [(target, source) for source, target in routes]

    def own_columns(matrix, width):
        return lax.dynamic_slice_in_dim(matrix, seq_index * width, width, axis=1)

    def own_rows(matrix):
        count = matrix.shape[0] // seq_size
        piece = lax.dynamic_slice_in_dim(matrix, seq_index * count, count, axis=0)
        return lax.ppermute(piece, ("dp", "seq"), routes)

    x_local = block_in[0]
    query_own = own_columns(query_weight, query_cols).reshape(share, local_kv, -1)
    key_own = own_columns(key_weight, local_kv * head_dim).reshape(share, local_kv, -1)
    value_own = own_columns(value_matrix, local_kv * head_dim).reshape(share, local_kv, -1)
    attn_piece = jnp.concatenate([query_own, key_own, value_own], axis=2).reshape(share, -1)
    gains = jnp.concatenate([first_gain, second_gain, query_gain, key_gain])[None]
    gains = jnp.pad(gains, ((0, GAIN_ROWS - 1), (0, local_kv * group_cols - gain_width)))
    attn_piece = jnp.concatenate([attn_piece, gains], axis=0)
    attn_full = lax.all_gather(attn_piece, "dp", axis=0)
    gains_full = attn_full[:, share, :gain_width].astype(f32)
    first_full = gains_full[:, :share].reshape(1, -1)
    second_full = gains_full[:, share : 2 * share].reshape(1, -1)
    head_gain = jnp.pad(
        gains_full[:, 2 * share :].reshape(dp_size, 2, head_share).swapaxes(0, 1).reshape(2, -1),
        ((0, 6), (0, 0)),
    )
    x_full = gather_tokens(x_local, seq_size)
    positions_full = gather_tokens(positions, seq_size).reshape(full_len)
    cosine, sine = rope_tables(positions_full, head_dim)
    doc_row = doc_ids
    doc_col = doc_ids.reshape(full_len, 1)
    out_full = lax.all_gather(out_weight, "dp", axis=0, tiled=True)
    grad_full = gather_tokens(grad_out[0], seq_size)
    mlp_piece = jnp.concatenate(
        [own_columns(gate_weight, ff_cols), own_columns(up_weight, ff_cols)], axis=1
    )
    mlp_full = lax.all_gather(mlp_piece, "dp", axis=0, tiled=True)
    down_full = lax.all_gather(own_rows(down_weight), "dp", axis=0, tiled=True)

    normed_full, raw, rot, attended_heads, inverse = attn_forward(
        x_full, attn_full, first_full, head_gain, cosine, sine, doc_row, doc_col, sizes
    )
    attended_heads, grad_full = lax.optimization_barrier((attended_heads, grad_full))
    attended_tokens = exchange(attended_heads.reshape(seq_size, local_len, query_cols))
    out_parts = out_full.reshape(seq_size, query_cols, model_width)
    residual = x_local.astype(f32)
    middle = residual + product("sle,sed->ld", attended_tokens, out_parts)
    second_unit, second_inverse = normalize(middle)
    second_normed = gather_tokens((second_unit * second_full).astype(bf16), seq_size)
    hidden, pair_grad, normed_grad_part = mlp_forward_backward(
        second_normed, grad_full, mlp_full, down_full
    )
    normed_grad = scatter_tokens(normed_grad_part, seq_size)
    second_gain_grad = jnp.sum(normed_grad * second_unit, axis=0)
    middle_grad = grad_out[0].astype(f32) + norm_backward(
        normed_grad, second_unit, second_inverse, second_full
    )
    middle_low = middle_grad.astype(bf16)
    attended_grad = product("ld,sed->sle", middle_low, out_parts).astype(bf16)
    head_grad = exchange(attended_grad).reshape(full_len, query_cols)

    def scatter_grad(partial):
        return lax.psum_scatter(
            partial.astype(bf16), "dp", scatter_dimension=0, tiled=True
        )

    mlp_grad = scatter_grad(product("ld,lf->df", second_normed, pair_grad))
    down_grad = scatter_grad(product("lf,ld->fd", hidden, grad_full))
    middle_low, head_grad = lax.optimization_barrier((middle_low, head_grad))
    middle_low_full = gather_tokens(middle_low, seq_size)
    raw_grad, first_normed_part, first_gain_part, head_gain_part = attn_backward(
        x_full, attn_full, head_gain, cosine, sine, doc_row, doc_col, raw, rot, inverse,
        head_grad, sizes,
    )
    raw_grad, first_normed_part, middle_low_full = lax.optimization_barrier(
        (raw_grad, first_normed_part, middle_low_full)
    )
    first_normed_grad = scatter_tokens(first_normed_part, seq_size)
    first_unit, first_inverse = normalize(residual)
    input_grad = middle_grad + norm_backward(
        first_normed_grad, first_unit, first_inverse, first_full
    )
    gain_parts = jnp.concatenate(
        [
            first_gain_part.reshape(dp_size, share),
            second_gain_grad.reshape(dp_size, share),
            head_gain_part[0].reshape(dp_size, head_share),
            head_gain_part[1].reshape(dp_size, head_share),
        ],
        axis=1,
    )
    gain_parts = jnp.pad(
        gain_parts[:, None],
        ((0, 0), (0, GAIN_ROWS - 1), (0, local_kv * group_cols - gain_width)),
    ).astype(bf16)
    attn_part = product("ld,le->de", normed_full, raw_grad).astype(bf16)
    attn_part = jnp.concatenate(
        [attn_part.reshape(dp_size, share, -1), gain_parts], axis=1
    ).reshape(dp_size * (share + GAIN_ROWS), -1)
    attn_grad = scatter_grad(attn_part)
    out_grad = scatter_grad(product("le,ld->ed", attended_heads, middle_low_full))
    block_out = (
        middle + scatter_tokens(product("lf,fd->ld", hidden, down_full), seq_size)
    ).astype(bf16)

    def gather_columns(piece):
        spread = jnp.broadcast_to(piece[None], (seq_size,) + piece.shape)
        return exchange(spread)

    def gather_rows(piece):
        home = lax.ppermute(piece, ("dp", "seq"), back_routes)
        return gather_tokens(home, seq_size).astype(f32)

    def side_by_side(parts, rows):
        return jnp.swapaxes(parts, 0, 1).reshape(rows, -1).astype(f32)

    mlp_parts = gather_columns(mlp_grad)
    gate_weight_grad = side_by_side(mlp_parts[:, :, :ff_cols], share)
    up_weight_grad = side_by_side(mlp_parts[:, :, ff_cols:], share)
    down_weight_grad = gather_rows(down_grad)
    out_weight_grad = gather_rows(out_grad)
    attn_parts = gather_columns(attn_grad)
    gain_sums = jnp.sum(attn_parts[:, share, :gain_width].astype(f32), axis=0)
    attn_parts = attn_parts[:, :share].reshape(seq_size, share, local_kv, group_cols)
    rot_cols = group_size * head_dim
    query_weight_grad = side_by_side(attn_parts[..., :rot_cols], share)
    key_weight_grad = side_by_side(attn_parts[..., rot_cols : rot_cols + head_dim], share)
    value_weight_grad = side_by_side(attn_parts[..., rot_cols + head_dim :], share)
    return (
        block_out[None],
        input_grad[None],
        gain_sums[:share],
        query_weight_grad,
        key_weight_grad,
        value_weight_grad,
        gain_sums[2 * share : 2 * share + head_share],
        gain_sums[2 * share + head_share :],
        out_weight_grad,
        gain_sums[share : 2 * share],
        gate_weight_grad,
        up_weight_grad,
        down_weight_grad,
    )


def solution(mesh):
    placed = (
        P("dp", "seq", None),
        P("dp", "seq"),
        P("dp", None),
        P("dp"),
        P("dp", None),
        P("dp", None),
        P("dp", None),
        P("dp"),
        P("dp"),
        P("dp", None),
        P("dp"),
        P("dp", None),
        P("dp", None),
        P("dp", None),
        P("dp", "seq", None),
    )
    return jax.shard_map(
        on_device,
        mesh=mesh,
        in_specs=placed,
        out_specs=(
            P("dp", "seq", None),
            P("dp", "seq", None),
            P("dp"),
            P("dp", None),
            P("dp", None),
            P("dp", None),
            P("dp"),
            P("dp"),
            P("dp", None),
            P("dp"),
            P("dp", None),
            P("dp", None),
            P("dp", None),
        ),
        check_vma=False,
    )
```

```python
import functools

import jax
import jax.numpy as jnp
from jax import lax
from jax.experimental import pallas as pl
from jax.experimental.pallas import tpu as pltpu
from jax.sharding import PartitionSpec as P

EPSILON = 1e-06
THETA = 1000000.0
LOG2E = 1.4426950408889634
EXTRA_ROWS = 16
GAIN_SLOT = 128
PACK_COLS = 256
VMEM_LIMIT = 60 * 1024 * 1024


def product(einsum_form, left_side, right_side):
    return jnp.einsum(einsum_form, left_side, right_side, preferred_element_type=jnp.float32)


def dot(left, right, contract):
    return lax.dot_general(
        left, right, (contract, ((), ())), preferred_element_type=jnp.float32
    )


def dot_nn(left, right):
    return dot(left, right, ((1,), (0,)))


def dot_nt(left, right):
    return dot(left, right, ((1,), (1,)))


def normalize(values):
    inverse = lax.rsqrt(jnp.mean(values * values, axis=-1, keepdims=True) + EPSILON)
    return (values * inverse, inverse)


def norm_backward(upstream, unit_rows, inverse, gain_values):
    scaled = upstream * gain_values
    return inverse * (scaled - unit_rows * jnp.mean(scaled * unit_rows, axis=-1, keepdims=True))


def rope_tables(positions, head_dim):
    half_dim = head_dim // 2
    inverse_freq = 1.0 / THETA ** (jnp.arange(half_dim, dtype=jnp.float32) * 2.0 / head_dim)
    angles = positions.astype(jnp.float32)[:, None] * inverse_freq
    cosine = jnp.cos(angles)
    sine = jnp.sin(angles)
    return (
        jnp.concatenate([cosine, cosine], axis=-1),
        jnp.concatenate([-sine, sine], axis=-1),
    )


def turned(values):
    return pltpu.roll(values, values.shape[-1] // 2, axis=1)


def query_blocks(full_len):
    block = min(256, full_len)
    reach = full_len // 2
    for first in range(0, full_len, block):
        yield first, first + block, max(0, first - reach)


def attn_forward_body(
    x_ref, weight_ref, first_gain_ref, head_gain_ref, cos_ref, sin_ref, doc_row_ref, doc_col_ref,
    normed_ref, raw_ref, rot_ref, attended_ref, inverse_ref,
    *, group_size, head_dim,
):
    bf16 = jnp.bfloat16
    full_len = normed_ref.shape[0]
    local_len = x_ref.shape[1] - EXTRA_ROWS
    scale = head_dim ** (-0.5)

    @pl.when(pl.program_id(0) == 0)
    def _():
        for index in range(x_ref.shape[0]):
            unit, _ = normalize(x_ref[index, :local_len].astype(jnp.float32))
            normed_ref[index * local_len : (index + 1) * local_len] = (
                unit * first_gain_ref[...]
            ).astype(bf16)

    share = weight_ref.shape[1] - EXTRA_ROWS
    weight = weight_ref[:, :share, :].reshape(-1, weight_ref.shape[2])
    rot_width = (group_size + 1) * head_dim
    for first in range(0, full_len, 256):
        rows = slice(first, first + 256)
        raw = dot_nn(normed_ref[rows], weight)
        raw_ref[rows] = raw[:, :rot_width]
        rot_ref[rows, rot_width:] = raw[:, rot_width:].astype(bf16)
        for head in range(group_size + 1):
            cols = slice(head * head_dim, (head + 1) * head_dim)
            unit, _ = normalize(raw[:, cols])
            gain = head_gain_ref[:1] if head < group_size else head_gain_ref[1:2]
            scaled = unit * gain
            rot_ref[rows, cols] = (
                scaled * cos_ref[rows] + turned(scaled) * sin_ref[rows]
            ).astype(bf16)
    key = slice(group_size * head_dim, rot_width)
    for first, last, start in query_blocks(full_len):
        keys = rot_ref[start:last, key]
        values = rot_ref[start:last, rot_width:]
        widened = jnp.concatenate([values, jnp.ones_like(values)], axis=1)
        count = last - start
        query_index = lax.broadcasted_iota(jnp.int32, (last - first, count), 0) + first
        key_index = lax.broadcasted_iota(jnp.int32, (last - first, count), 1) + start
        allowed = (key_index <= query_index) & (
            doc_col_ref[first:last] == doc_row_ref[:, start:last]
        )
        for head in range(group_size):
            cols = slice(head * head_dim, (head + 1) * head_dim)
            scores = dot_nt(rot_ref[first:last, cols], keys)
            powers = jnp.where(allowed, jnp.exp2(scores * (scale * LOG2E)), 0.0)
            sums = dot_nn(powers.astype(bf16), widened)
            inverse = 1.0 / sums[:, head_dim:]
            attended_ref[first:last, cols] = (sums[:, :head_dim] * inverse).astype(bf16)
            inverse_ref[head * 8 : (head + 1) * 8, first:last] = inverse.T[:8]


def attn_forward(x_parts, weight, first_gain, head_gain, cosine, sine, doc_row, doc_col, sizes):
    group_size, head_dim, local_kv = sizes
    full_len = doc_col.shape[0]
    model_width = x_parts.shape[2]
    group_cols = (group_size + 2) * head_dim
    whole = lambda shape: pl.BlockSpec(shape, lambda j: (0,) * len(shape))
    columns = lambda rows, width: pl.BlockSpec((rows, width), lambda j: (0, j))
    rot_width = (group_size + 1) * head_dim
    query_width = group_size * head_dim
    return pl.pallas_call(
        functools.partial(attn_forward_body, group_size=group_size, head_dim=head_dim),
        name="attn_forward",
        grid=(local_kv,),
        in_specs=[
            whole(x_parts.shape),
            pl.BlockSpec(weight.shape[:2] + (group_cols,), lambda j: (0, 0, j)),
            whole(first_gain.shape),
            whole(head_gain.shape),
            whole(cosine.shape),
            whole(sine.shape),
            whole(doc_row.shape),
            whole(doc_col.shape),
        ],
        out_specs=[
            whole((full_len, model_width)),
            columns(full_len, rot_width),
            columns(full_len, group_cols),
            columns(full_len, query_width),
            pl.BlockSpec((group_size * 8, full_len), lambda j: (j, 0)),
        ],
        out_shape=[
            jax.ShapeDtypeStruct((full_len, model_width), jnp.bfloat16),
            jax.ShapeDtypeStruct((full_len, local_kv * rot_width), jnp.float32),
            jax.ShapeDtypeStruct((full_len, local_kv * group_cols), jnp.bfloat16),
            jax.ShapeDtypeStruct((full_len, local_kv * query_width), jnp.bfloat16),
            jax.ShapeDtypeStruct((local_kv * group_size * 8, full_len), jnp.float32),
        ],
        compiler_params=pltpu.CompilerParams(vmem_limit_bytes=VMEM_LIMIT),
        cost_estimate=pl.CostEstimate(flops=1000, transcendentals=0, bytes_accessed=1000),
    )(x_parts, weight, first_gain, head_gain, cosine, sine, doc_row, doc_col)


def attn_backward_body(
    middle_ref, out_weight_ref, attended_t_ref, normed_t_ref, weight_ref, first_gain_ref,
    second_sum_ref, head_gain_ref, cos_ref, sin_ref, doc_row_ref, doc_col_ref,
    raw_ref, rot_ref, inverse_ref,
    raw_grad_ref, pack_ref,
    gain_acc_ref, head_acc_ref, grad_acc_ref, query_acc_ref, key_acc_ref, value_acc_ref,
    *, group_size, head_dim,
):
    bf16 = jnp.bfloat16
    full_len = middle_ref.shape[0]
    scale = head_dim ** (-0.5)
    step = pl.program_id(0)
    rot_width = (group_size + 1) * head_dim
    key = slice(group_size * head_dim, rot_width)

    @pl.when(step == 0)
    def _():
        gain_acc_ref[...] = jnp.zeros_like(gain_acc_ref)
        head_acc_ref[...] = jnp.zeros_like(head_acc_ref)

    for first in range(0, full_len, 256):
        rows = slice(first, first + 256)
        grad_acc_ref[rows] = dot_nt(middle_ref[rows], out_weight_ref[...]).astype(bf16)
    key_acc_ref[...] = jnp.zeros_like(key_acc_ref)
    value_acc_ref[...] = jnp.zeros_like(value_acc_ref)
    key_turned = rot_ref[:, key].T
    for first, last, start in query_blocks(full_len):
        keys = rot_ref[start:last, key]
        values = rot_ref[start:last, rot_width:]
        count = last - start
        key_index = lax.broadcasted_iota(jnp.int32, (count, last - first), 0) + start
        query_index = lax.broadcasted_iota(jnp.int32, (count, last - first), 1) + first
        allowed = (key_index <= query_index) & (
            doc_col_ref[start:last] == doc_row_ref[:, first:last]
        )
        for head in range(group_size):
            cols = slice(head * head_dim, (head + 1) * head_dim)
            queries = rot_ref[first:last, cols]
            grads = grad_acc_ref[first:last, cols]
            scores = dot_nt(keys, queries)
            powers = jnp.where(allowed, jnp.exp2(scores * (scale * LOG2E)), 0.0)
            weights = powers * inverse_ref[head * 8 : head * 8 + 1, first:last]
            value_acc_ref[start:last] += dot_nn(weights.astype(bf16), grads)
            prob_grad = dot_nt(values, grads)
            delta = jnp.sum(weights * prob_grad, axis=0, keepdims=True)
            score_grad = (weights * (prob_grad - delta)).astype(bf16)
            key_acc_ref[start:last] += dot_nn(score_grad, queries)
            query_acc_ref[first:last, cols] = dot_nn(key_turned[:, start:last], score_grad).T

    query_sum = jnp.zeros((1, head_dim), jnp.float32)
    key_sum = jnp.zeros((1, head_dim), jnp.float32)
    for first in range(0, full_len, 256):
        rows = slice(first, first + 256)
        for head in range(group_size + 1):
            cols = slice(head * head_dim, (head + 1) * head_dim)
            is_query = head < group_size
            rot_grad = query_acc_ref[rows, cols] if is_query else key_acc_ref[rows]
            rot_grad = (rot_grad * scale).astype(bf16).astype(jnp.float32)
            scaled_grad = rot_grad * cos_ref[rows] - turned(rot_grad) * sin_ref[rows]
            unit, inverse = normalize(raw_ref[rows, cols])
            part = jnp.sum(scaled_grad * unit, axis=0, keepdims=True)
            if is_query:
                query_sum = query_sum + part
            else:
                key_sum = key_sum + part
            gain = head_gain_ref[:1] if is_query else head_gain_ref[1:2]
            raw_grad_ref[rows, cols] = norm_backward(scaled_grad, unit, inverse, gain).astype(bf16)
        raw_grad_ref[rows, rot_width:] = value_acc_ref[rows].astype(bf16)
    head_acc_ref[:1] += query_sum
    head_acc_ref[1:2] += key_sum

    dp_size, pack_rows, cols = pack_ref.shape
    share = weight_ref.shape[1] - EXTRA_ROWS
    for index in range(dp_size):
        mine = slice(index * share, (index + 1) * share)
        grad = dot_nn(normed_t_ref[mine], raw_grad_ref[...])
        pack_ref[index, :share] = grad.astype(bf16)
        terms = grad * weight_ref[index, :share].astype(jnp.float32)
        folded = terms[:, :128]
        for chunk in range(128, cols, 128):
            folded = folded + terms[:, chunk : chunk + 128]
        gain_acc_ref[:1, mine] += jnp.sum(folded.T, axis=0, keepdims=True)
        pack_ref[index, share : share + EXTRA_ROWS] = jnp.zeros((EXTRA_ROWS, cols), bf16)

    @pl.when(step == pl.num_programs(0) - 1)
    def _():
        for index in range(dp_size):
            mine = slice(index * share, (index + 1) * share)
            slots = [
                gain_acc_ref[:1, mine] / first_gain_ref[:, mine],
                second_sum_ref[:, mine],
                head_acc_ref[:1],
                head_acc_ref[1:2],
            ]
            slots = [
                slot
                if slot.shape[1] == GAIN_SLOT
                else jnp.concatenate(
                    [slot, jnp.zeros((1, GAIN_SLOT - slot.shape[1]), jnp.float32)], axis=1
                )
                for slot in slots
            ]
            row = jnp.concatenate(slots, axis=1)
            pack_ref[index, share : share + EXTRA_ROWS] = jnp.broadcast_to(
                row, (EXTRA_ROWS, cols)
            ).astype(bf16)

    out_rows = attended_t_ref.shape[0] // dp_size
    blocks = middle_ref.shape[1] // (cols * pl.num_programs(0))
    for block in range(blocks):
        begin = pl.multiple_of((block * pl.num_programs(0) + step) * cols, 128)
        grad = dot_nn(attended_t_ref[...], middle_ref[:, pl.ds(begin, cols)]).astype(bf16)
        base = share + EXTRA_ROWS + block * out_rows
        for index in range(dp_size):
            pack_ref[index, base : base + out_rows] = grad[index * out_rows : (index + 1) * out_rows]


def attn_backward(
    middle, out_weight, attended_t, normed_t, weight, first_gain, second_sum, head_gain, cosine,
    sine, doc_row, doc_col, raw, rot, inverse, sizes,
):
    group_size, head_dim, local_kv = sizes
    full_len, model_width = middle.shape
    dp_size, share = weight.shape[0], weight.shape[1] - EXTRA_ROWS
    group_cols = (group_size + 2) * head_dim
    total_cols = local_kv * group_cols
    rot_width = (group_size + 1) * head_dim
    query_width = group_size * head_dim
    out_rows = out_weight.shape[0] // dp_size * (model_width // total_cols)
    pack_rows = share + EXTRA_ROWS + out_rows
    whole = lambda shape: pl.BlockSpec(shape, lambda j: (0,) * len(shape))
    columns = lambda rows, width: pl.BlockSpec((rows, width), lambda j: (0, j))
    return pl.pallas_call(
        functools.partial(attn_backward_body, group_size=group_size, head_dim=head_dim),
        name="attn_backward",
        grid=(local_kv,),
        in_specs=[
            whole(middle.shape),
            pl.BlockSpec((query_width, model_width), lambda j: (j, 0)),
            whole(attended_t.shape),
            whole(normed_t.shape),
            pl.BlockSpec(weight.shape[:2] + (group_cols,), lambda j: (0, 0, j)),
            whole(first_gain.shape),
            whole(second_sum.shape),
            whole(head_gain.shape),
            whole(cosine.shape),
            whole(sine.shape),
            whole(doc_row.shape),
            whole(doc_col.shape),
            columns(full_len, rot_width),
            columns(full_len, group_cols),
            pl.BlockSpec((group_size * 8, full_len), lambda j: (j, 0)),
        ],
        out_specs=[
            columns(full_len, group_cols),
            pl.BlockSpec((dp_size, pack_rows, group_cols), lambda j: (0, 0, j)),
        ],
        out_shape=[
            jax.ShapeDtypeStruct((full_len, total_cols), jnp.bfloat16),
            jax.ShapeDtypeStruct((dp_size, pack_rows, total_cols), jnp.bfloat16),
        ],
        scratch_shapes=[
            pltpu.VMEM((8, model_width), jnp.float32),
            pltpu.VMEM((8, head_dim), jnp.float32),
            pltpu.VMEM((full_len, query_width), jnp.bfloat16),
            pltpu.VMEM((full_len, query_width), jnp.float32),
            pltpu.VMEM((full_len, head_dim), jnp.float32),
            pltpu.VMEM((full_len, head_dim), jnp.float32),
        ],
        compiler_params=pltpu.CompilerParams(vmem_limit_bytes=VMEM_LIMIT),
        cost_estimate=pl.CostEstimate(flops=1000, transcendentals=0, bytes_accessed=1000),
    )(
        middle, out_weight, attended_t, normed_t, weight, first_gain, second_sum, head_gain, cosine,
        sine, doc_row, doc_col, raw, rot, inverse,
    )


def column_group(down_rows, own_rows, dp_size):
    count = 1
    while own_rows * count % 128 or dp_size % count:
        count += 1
    return count


def column_choice(seq_index, count, down_rows, own_rows):
    own = lax.broadcasted_iota(jnp.int32, (1, own_rows * count), 1)
    target = own + own_rows * seq_index
    for block in range(1, count):
        target = target + jnp.where(own >= block * own_rows, down_rows - own_rows, 0)
    whole = lax.broadcasted_iota(jnp.int32, (down_rows * count, own_rows * count), 0)
    return jnp.where(whole == target, 1.0, 0.0).astype(jnp.bfloat16)


def pack_mlp_body(index_ref, gate_ref, up_ref, down_ref, pack_ref, *, dp_size, seq_size):
    share = gate_ref.shape[0]
    own_rows = down_ref.shape[0]
    down_rows = own_rows * seq_size
    count = column_group(down_rows, own_rows, dp_size)
    choice = column_choice(index_ref[0], count, down_rows, own_rows)
    width = down_rows * count
    column = 0
    for source in (gate_ref, up_ref):
        for first in range(0, source.shape[1], width):
            chosen = dot_nn(source[:, first : first + width], choice).astype(jnp.bfloat16)
            for part in range(0, chosen.shape[1], 128):
                base = column // PACK_COLS * share
                half = column % PACK_COLS
                pack_ref[base : base + share, half : half + 128] = chosen[:, part : part + 128]
                column += 128
    base = column // PACK_COLS * share
    for first in range(0, down_ref.shape[1], PACK_COLS):
        pack_ref[base : base + own_rows] = down_ref[:, first : first + PACK_COLS]
        base += own_rows


def pack_mlp(seq_index, gate_weight, up_weight, down_weight, dp_size, seq_size):
    share, ff_total = gate_weight.shape
    model_width = down_weight.shape[1]
    own_rows = down_weight.shape[0] // seq_size
    rows = share * (2 * ff_total // seq_size // PACK_COLS) + own_rows * (model_width // PACK_COLS)
    whole = pl.BlockSpec((share, ff_total), lambda i, index: (0, 0))
    return pl.pallas_call(
        functools.partial(pack_mlp_body, dp_size=dp_size, seq_size=seq_size),
        name="pack_mlp",
        grid_spec=pltpu.PrefetchScalarGridSpec(
            num_scalar_prefetch=1,
            grid=(1,),
            in_specs=[
                whole, whole, pl.BlockSpec((own_rows, model_width), lambda i, index: (index[0], 0))
            ],
            out_specs=pl.BlockSpec((rows, PACK_COLS), lambda i, index: (0, 0)),
        ),
        out_shape=jax.ShapeDtypeStruct((rows, PACK_COLS), jnp.bfloat16),
        compiler_params=pltpu.CompilerParams(vmem_limit_bytes=VMEM_LIMIT),
        cost_estimate=pl.CostEstimate(flops=1000, transcendentals=0, bytes_accessed=1000),
    )(jnp.reshape(seq_index, (1,)).astype(jnp.int32), gate_weight, up_weight, down_weight)


def mlp_body(
    normed_ref, grad_ref, weight_ref, hidden_ref, pair_grad_ref, normed_grad_ref,
    block_ref, pair_ref, down_ref,
):
    bf16 = jnp.bfloat16
    width = hidden_ref.shape[1]
    dp_size = weight_ref.shape[0]
    share = pair_ref.shape[0] // dp_size
    down_share = width // dp_size

    @pl.when(pl.program_id(0) == 0)
    def _():
        for index in range(dp_size):
            base = 0
            rows = slice(index * share, (index + 1) * share)
            for first in range(0, 2 * width, PACK_COLS):
                pair_ref[rows, first : first + PACK_COLS] = weight_ref[index, base : base + share]
                base += share
            rows = slice(index * down_share, (index + 1) * down_share)
            for first in range(0, down_ref.shape[1], PACK_COLS):
                down_ref[rows, first : first + PACK_COLS] = weight_ref[
                    index, base : base + down_share
                ]
                base += down_share

    pair = dot_nn(normed_ref[...], pair_ref[...])
    hidden_grad = dot_nt(grad_ref[...], down_ref[...])
    gate_pre = pair[:, :width]
    up_pre = pair[:, width:]
    sigmoid_gate = jax.nn.sigmoid(gate_pre)
    silu_gate = gate_pre * sigmoid_gate
    hidden_ref[...] = (silu_gate * up_pre).astype(bf16)
    gate_pre_grad = (
        hidden_grad * up_pre * sigmoid_gate * (1.0 + gate_pre * (1.0 - sigmoid_gate))
    )
    pair_grad_ref[:, :width] = gate_pre_grad.astype(bf16)
    pair_grad_ref[:, width:] = (hidden_grad * silu_gate).astype(bf16)
    normed_grad_ref[...] = dot_nt(pair_grad_ref[...], pair_ref[...]).astype(bf16)
    block_ref[...] = dot_nn(hidden_ref[...], down_ref[...]).astype(bf16)


def mlp_forward_backward(normed, grads, weight, width):
    full_len, model_width = normed.shape
    block = min(256, full_len)
    rows = lambda cols: pl.BlockSpec((block, cols), lambda i: (i, 0))
    whole = lambda shape: pl.BlockSpec(shape, lambda i: (0,) * len(shape))
    return pl.pallas_call(
        mlp_body,
        name="mlp_forward_backward",
        grid=(full_len // block,),
        in_specs=[rows(model_width), rows(model_width), whole(weight.shape)],
        out_specs=[rows(width), rows(2 * width), rows(model_width), rows(model_width)],
        out_shape=[
            jax.ShapeDtypeStruct((full_len, width), jnp.bfloat16),
            jax.ShapeDtypeStruct((full_len, 2 * width), jnp.bfloat16),
            jax.ShapeDtypeStruct((full_len, model_width), jnp.bfloat16),
            jax.ShapeDtypeStruct((full_len, model_width), jnp.bfloat16),
        ],
        scratch_shapes=[
            pltpu.VMEM((model_width, 2 * width), jnp.bfloat16),
            pltpu.VMEM((width, model_width), jnp.bfloat16),
        ],
        compiler_params=pltpu.CompilerParams(vmem_limit_bytes=VMEM_LIMIT),
        cost_estimate=pl.CostEstimate(flops=1000, transcendentals=0, bytes_accessed=1000),
    )(normed, grads, weight)


def mlp_grads_body(normed_ref, pair_grad_ref, hidden_ref, grad_ref, pack_ref):
    bf16 = jnp.bfloat16
    dp_size = pack_ref.shape[0]
    share = normed_ref.shape[1] // dp_size
    down_share = hidden_ref.shape[1] // dp_size
    normed_t = normed_ref[...].T
    for index in range(dp_size):
        grad = dot_nn(normed_t[index * share : (index + 1) * share], pair_grad_ref[...])
        grad = grad.astype(bf16)
        base = 0
        for first in range(0, grad.shape[1], PACK_COLS):
            pack_ref[index, base : base + share] = grad[:, first : first + PACK_COLS]
            base += share
    grad = dot_nn(hidden_ref[...].T, grad_ref[...])
    for index in range(dp_size):
        base = share * (pair_grad_ref.shape[1] // PACK_COLS)
        mine = grad[index * down_share : (index + 1) * down_share].astype(bf16)
        for first in range(0, grad.shape[1], PACK_COLS):
            pack_ref[index, base : base + down_share] = mine[:, first : first + PACK_COLS]
            base += down_share


def mlp_grads(normed, pair_grad, hidden, grads, pack_shape):
    return pl.pallas_call(
        mlp_grads_body,
        name="mlp_grads",
        out_shape=jax.ShapeDtypeStruct(pack_shape, jnp.bfloat16),
        compiler_params=pltpu.CompilerParams(vmem_limit_bytes=VMEM_LIMIT),
        cost_estimate=pl.CostEstimate(flops=1000, transcendentals=0, bytes_accessed=1000),
    )(normed, pair_grad, hidden, grads)


def input_body(raw_grad_ref, weight_ref, out_ref):
    share = weight_ref.shape[1] - EXTRA_ROWS
    weight = weight_ref[:, :share, :].reshape(-1, weight_ref.shape[2])
    out_ref[...] = dot_nt(raw_grad_ref[...], weight).astype(jnp.bfloat16)


def input_partial(raw_grad, weight):
    full_len, cols = raw_grad.shape
    block = min(256, full_len)
    model_width = weight.shape[0] * (weight.shape[1] - EXTRA_ROWS)
    return pl.pallas_call(
        input_body,
        name="input_partial",
        grid=(full_len // block,),
        in_specs=[
            pl.BlockSpec((block, cols), lambda i: (i, 0)),
            pl.BlockSpec(weight.shape, lambda i: (0, 0, 0)),
        ],
        out_specs=pl.BlockSpec((block, model_width), lambda i: (i, 0)),
        out_shape=jax.ShapeDtypeStruct((full_len, model_width), jnp.bfloat16),
        compiler_params=pltpu.CompilerParams(vmem_limit_bytes=VMEM_LIMIT),
        cost_estimate=pl.CostEstimate(flops=1000, transcendentals=0, bytes_accessed=1000),
    )(raw_grad, weight)


def finish_attn_body(parts_ref, query_ref, key_ref, value_ref, gain_ref, *, group_size, head_dim):
    f32 = jnp.float32
    seq_size, rows, cols = parts_ref.shape
    share = rows - EXTRA_ROWS
    group_cols = (group_size + 2) * head_dim
    rot_width = group_size * head_dim
    total = jnp.zeros((EXTRA_ROWS, group_cols), f32)
    head = 0
    for index in range(seq_size):
        for first in range(0, cols, group_cols):
            part = parts_ref[index, :share, first : first + group_cols].astype(f32)
            query_ref[:, head * rot_width : (head + 1) * rot_width] = part[:, :rot_width]
            spot = slice(head * head_dim, (head + 1) * head_dim)
            key_ref[:, spot] = part[:, rot_width : rot_width + head_dim]
            value_ref[:, spot] = part[:, rot_width + head_dim :]
            head += 1
        total = total + parts_ref[index, share:, cols - group_cols :].astype(f32)
    gain_ref[...] = total


def finish_attn(parts, sizes):
    group_size, head_dim, local_kv = sizes
    seq_size, rows, cols = parts.shape
    share = rows - EXTRA_ROWS
    heads = seq_size * local_kv
    return pl.pallas_call(
        functools.partial(finish_attn_body, group_size=group_size, head_dim=head_dim),
        name="finish_attn",
        out_shape=[
            jax.ShapeDtypeStruct((share, heads * group_size * head_dim), jnp.float32),
            jax.ShapeDtypeStruct((share, heads * head_dim), jnp.float32),
            jax.ShapeDtypeStruct((share, heads * head_dim), jnp.float32),
            jax.ShapeDtypeStruct((EXTRA_ROWS, (group_size + 2) * head_dim), jnp.float32),
        ],
        compiler_params=pltpu.CompilerParams(vmem_limit_bytes=VMEM_LIMIT),
        cost_estimate=pl.CostEstimate(flops=1000, transcendentals=0, bytes_accessed=1000),
    )(parts)


def finish_mlp_body(parts_ref, gate_ref, up_ref, down_ref, *, dp_size):
    f32 = jnp.float32
    seq_size = parts_ref.shape[0]
    share, ff_total = gate_ref.shape
    down_rows = down_ref.shape[0]
    own_rows = down_rows // seq_size
    count = column_group(down_rows, own_rows, dp_size)
    choices = [column_choice(index, count, down_rows, own_rows) for index in range(seq_size)]
    width = down_rows * count
    column = 0
    for target_ref in (gate_ref, up_ref):
        for first in range(0, ff_total, width):
            total = jnp.zeros((share, width), f32)
            for index in range(seq_size):
                pieces = []
                for part in range(column, column + own_rows * count, 128):
                    base = part // PACK_COLS * share
                    half = part % PACK_COLS
                    pieces.append(parts_ref[index, base : base + share, half : half + 128])
                total = total + dot_nt(jnp.concatenate(pieces, axis=1), choices[index])
            target_ref[:, first : first + width] = total
            column += own_rows * count
    for index in range(seq_size):
        base = column // PACK_COLS * share
        for first in range(0, down_ref.shape[1], PACK_COLS):
            part = parts_ref[index, base : base + own_rows]
            down_ref[
                index * own_rows : (index + 1) * own_rows, first : first + PACK_COLS
            ] = part.astype(f32)
            base += own_rows


def finish_mlp(parts, share, ff_total, model_width, down_rows, dp_size):
    return pl.pallas_call(
        functools.partial(finish_mlp_body, dp_size=dp_size),
        name="finish_mlp",
        out_shape=[
            jax.ShapeDtypeStruct((share, ff_total), jnp.float32),
            jax.ShapeDtypeStruct((share, ff_total), jnp.float32),
            jax.ShapeDtypeStruct((down_rows, model_width), jnp.float32),
        ],
        compiler_params=pltpu.CompilerParams(vmem_limit_bytes=VMEM_LIMIT),
        cost_estimate=pl.CostEstimate(flops=1000, transcendentals=0, bytes_accessed=1000),
    )(parts)


def exchange(pieces):
    return lax.all_to_all(pieces, "seq", split_axis=0, concat_axis=0, tiled=True)


def gather_parts(rows, seq_size):
    return exchange(jnp.broadcast_to(rows[None], (seq_size,) + rows.shape))


def gather_tokens(rows, seq_size):
    return gather_parts(rows, seq_size).reshape((seq_size * rows.shape[0],) + rows.shape[1:])


def scatter_tokens(partial, seq_size):
    pieces = partial.astype(jnp.bfloat16).reshape((seq_size, -1) + partial.shape[1:])
    return jnp.sum(exchange(pieces).astype(jnp.float32), axis=0)


def row_routes(dp_size, seq_size):
    routes = []
    for dp_index in range(dp_size):
        for seq_index in range(seq_size):
            holder = dp_size // seq_size * seq_index + dp_index // seq_size
            routes.append(
                (holder * seq_size + dp_index % seq_size, dp_index * seq_size + seq_index)
            )
    return routes


def on_device(
    block_in,
    positions,
    doc_ids,
    first_gain,
    query_weight,
    key_weight,
    value_matrix,
    query_gain,
    key_gain,
    out_weight,
    second_gain,
    gate_weight,
    up_weight,
    down_weight,
    grad_out,
):
    bf16 = jnp.bfloat16
    f32 = jnp.float32
    dp_size = lax.axis_size("dp")
    seq_size = lax.axis_size("seq")
    seq_index = lax.axis_index("seq")
    dp_index = lax.axis_index("dp")
    local_len, model_width = block_in.shape[1:]
    full_len = local_len * seq_size
    head_dim = query_gain.shape[0] * dp_size
    query_heads = query_weight.shape[1] // head_dim
    kv_heads = key_weight.shape[1] // head_dim
    group_size = query_heads // kv_heads
    local_kv = kv_heads // seq_size
    query_cols = local_kv * group_size * head_dim
    group_cols = (group_size + 2) * head_dim
    attn_cols = local_kv * group_cols
    ff_cols = gate_weight.shape[1] // seq_size
    share = first_gain.shape[0]
    head_share = query_gain.shape[0]
    gain_width = 2 * share + 2 * head_share
    sizes = (group_size, head_dim, local_kv)
    routes = row_routes(dp_size, seq_size)
    back_routes = [(target, source) for source, target in routes]

    def own_columns(matrix, width):
        return lax.dynamic_slice_in_dim(matrix, seq_index * width, width, axis=1)

    def own_rows(matrix):
        count = matrix.shape[0] // seq_size
        return lax.dynamic_slice_in_dim(matrix, seq_index * count, count, axis=0)

    x_local = block_in[0]
    coarse = jnp.pad(positions // 64, ((0, 0), (0, model_width - local_len)))
    fine = jnp.pad(positions % 64, ((0, 0), (0, model_width - local_len)))
    extra = jnp.pad(jnp.concatenate([coarse, fine]), ((0, EXTRA_ROWS - 2), (0, 0))).astype(bf16)
    x_parts = gather_parts(jnp.concatenate([x_local, extra]), seq_size)

    query_own = own_columns(query_weight, query_cols).reshape(share, local_kv, -1)
    key_own = own_columns(key_weight, local_kv * head_dim).reshape(share, local_kv, -1)
    value_own = own_columns(value_matrix, local_kv * head_dim).reshape(share, local_kv, -1)
    attn_piece = jnp.concatenate([query_own, key_own, value_own], axis=2).reshape(share, -1)
    gains = jnp.concatenate([first_gain, second_gain, query_gain, key_gain])[None]
    gains = jnp.pad(gains, ((0, EXTRA_ROWS - 1), (0, attn_cols - gain_width)))
    attn_full = lax.all_gather(jnp.concatenate([attn_piece, gains], axis=0), "dp", axis=0)
    gains_full = attn_full[:, share, :gain_width].astype(f32)
    first_full = gains_full[:, :share].reshape(1, -1)
    second_full = gains_full[:, share : 2 * share].reshape(1, -1)
    head_gain = jnp.pad(
        gains_full[:, 2 * share :].reshape(dp_size, 2, head_share).swapaxes(0, 1).reshape(2, -1),
        ((0, 6), (0, 0)),
    )

    out_count = out_weight.shape[0] // seq_size
    routed = lax.ppermute(own_rows(out_weight), ("dp", "seq"), routes)
    mlp_piece = pack_mlp(seq_index, gate_weight, up_weight, down_weight, dp_size, seq_size)
    x_parts, routed, mlp_piece = lax.optimization_barrier((x_parts, routed, mlp_piece))
    out_full = lax.all_gather(routed, "dp", axis=0, tiled=True)
    mlp_full = lax.all_gather(mlp_piece, "dp", axis=0)
    grad_full = gather_tokens(grad_out[0], seq_size)

    coarse_full = x_parts[:, local_len, :local_len].astype(f32)
    fine_full = x_parts[:, local_len + 1, :local_len].astype(f32)
    cosine, sine = rope_tables((coarse_full * 64.0 + fine_full).reshape(full_len), head_dim)
    doc_row = doc_ids
    doc_col = doc_ids.reshape(full_len, 1)
    normed_full, raw, rot, attended_heads, inverse = attn_forward(
        x_parts, attn_full, first_full, head_gain, cosine, sine, doc_row, doc_col, sizes
    )
    attended_heads, grad_full = lax.optimization_barrier((attended_heads, grad_full))
    residual = x_local.astype(f32)
    middle = residual + scatter_tokens(
        product("le,ed->ld", attended_heads, out_full), seq_size
    )
    normed_t = normed_full.T
    attended_t = attended_heads.T
    middle, normed_t, attended_t = lax.optimization_barrier((middle, normed_t, attended_t))
    second_unit, second_inverse = normalize(middle)
    second_normed = gather_tokens((second_unit * second_full).astype(bf16), seq_size)
    hidden, pair_grad, normed_grad_part, block_part = mlp_forward_backward(
        second_normed, grad_full, mlp_full, ff_cols
    )
    normed_grad = scatter_tokens(normed_grad_part, seq_size)

    def scatter_grad(pack):
        return lax.psum_scatter(pack, "dp", scatter_dimension=0, tiled=False)

    mlp_pack = mlp_grads(second_normed, pair_grad, hidden, grad_full, mlp_full.shape)
    second_sum = jnp.sum(normed_grad * second_unit, axis=0, keepdims=True)
    middle_grad = grad_out[0].astype(f32) + norm_backward(
        normed_grad, second_unit, second_inverse, second_full
    )
    middle_low, mlp_pack = lax.optimization_barrier((middle_grad.astype(bf16), mlp_pack))
    mlp_grad = scatter_grad(mlp_pack)
    middle_low = gather_tokens(middle_low, seq_size)
    middle_low, block_part = lax.optimization_barrier((middle_low, block_part))
    block_sum = scatter_tokens(block_part, seq_size)
    raw_grad, attn_pack = attn_backward(
        middle_low, out_full, attended_t, normed_t, attn_full, first_full, second_sum, head_gain,
        cosine, sine, doc_row, doc_col, raw, rot, inverse, sizes,
    )
    raw_grad, attn_pack, block_sum = lax.optimization_barrier((raw_grad, attn_pack, block_sum))
    attn_grad = scatter_grad(attn_pack)
    pair_parts = gather_parts(mlp_grad, seq_size)
    first_normed_part, pair_parts = lax.optimization_barrier(
        (input_partial(raw_grad, attn_full), pair_parts)
    )
    first_normed_grad = scatter_tokens(first_normed_part, seq_size)
    first_unit, first_inverse = normalize(residual)
    input_grad = middle_grad + norm_backward(
        first_normed_grad, first_unit, first_inverse, first_full
    )
    block_out = (middle + block_sum).astype(bf16)

    gate_weight_grad, up_weight_grad, down_weight_grad = finish_mlp(
        pair_parts, share, gate_weight.shape[1], model_width, down_weight.shape[0], dp_size
    )
    attn_grad, input_grad, gate_weight_grad = lax.optimization_barrier(
        (attn_grad, input_grad, gate_weight_grad)
    )
    attn_parts = gather_parts(attn_grad[: share + EXTRA_ROWS], seq_size)
    out_home = lax.ppermute(attn_grad[share + EXTRA_ROWS :], ("dp", "seq"), back_routes)
    attn_parts, out_home = lax.optimization_barrier((attn_parts, out_home))
    query_weight_grad, key_weight_grad, value_weight_grad, gain_sums = finish_attn(
        attn_parts, sizes
    )
    out_home = out_home.reshape(-1, out_count, attn_cols).swapaxes(0, 1).reshape(out_count, -1)
    out_weight_grad = gather_tokens(out_home, seq_size).astype(f32)

    def own_gain(slot):
        return lax.dynamic_slice_in_dim(
            gain_sums[0], slot * GAIN_SLOT + dp_index * head_share, head_share, axis=0
        )

    return (
        block_out[None],
        input_grad[None],
        gain_sums[0, :share],
        query_weight_grad,
        key_weight_grad,
        value_weight_grad,
        own_gain(2),
        own_gain(3),
        out_weight_grad,
        gain_sums[0, GAIN_SLOT : GAIN_SLOT + share],
        gate_weight_grad,
        up_weight_grad,
        down_weight_grad,
    )


def solution(mesh):
    placed = (
        P("dp", "seq", None),
        P("dp", "seq"),
        P("dp", None),
        P("dp"),
        P("dp", None),
        P("dp", None),
        P("dp", None),
        P("dp"),
        P("dp"),
        P("dp", None),
        P("dp"),
        P("dp", None),
        P("dp", None),
        P("dp", None),
        P("dp", "seq", None),
    )
    return jax.shard_map(
        on_device,
        mesh=mesh,
        in_specs=placed,
        out_specs=(
            P("dp", "seq", None),
            P("dp", "seq", None),
            P("dp"),
            P("dp", None),
            P("dp", None),
            P("dp", None),
            P("dp"),
            P("dp"),
            P("dp", None),
            P("dp"),
            P("dp", None),
            P("dp", None),
            P("dp", None),
        ),
        check_vma=False,
    )
```

```python
import functools

import jax
import jax.numpy as jnp
from jax import lax
from jax.experimental import pallas as pl
from jax.experimental.pallas import tpu as pltpu
from jax.sharding import PartitionSpec as P

EPSILON = 1e-06
THETA = 1000000.0
LOG2E = 1.4426950408889634
EXTRA_ROWS = 16
GAIN_SLOT = 128
PACK_COLS = 256
VMEM_LIMIT = 60 * 1024 * 1024


def product(einsum_form, left_side, right_side):
    return jnp.einsum(einsum_form, left_side, right_side, preferred_element_type=jnp.float32)


def dot(left, right, contract):
    return lax.dot_general(
        left, right, (contract, ((), ())), preferred_element_type=jnp.float32
    )


def dot_nn(left, right):
    return dot(left, right, ((1,), (0,)))


def dot_nt(left, right):
    return dot(left, right, ((1,), (1,)))


def normalize(values):
    inverse = lax.rsqrt(jnp.mean(values * values, axis=-1, keepdims=True) + EPSILON)
    return (values * inverse, inverse)


def norm_backward(upstream, unit_rows, inverse, gain_values):
    scaled = upstream * gain_values
    return inverse * (scaled - unit_rows * jnp.mean(scaled * unit_rows, axis=-1, keepdims=True))


def rope_tables(positions, head_dim):
    half_dim = head_dim // 2
    inverse_freq = 1.0 / THETA ** (jnp.arange(half_dim, dtype=jnp.float32) * 2.0 / head_dim)
    angles = positions.astype(jnp.float32)[:, None] * inverse_freq
    cosine = jnp.cos(angles)
    sine = jnp.sin(angles)
    return (
        jnp.concatenate([cosine, cosine], axis=-1),
        jnp.concatenate([-sine, sine], axis=-1),
    )


def turned(values):
    return pltpu.roll(values, values.shape[-1] // 2, axis=1)


def query_blocks(full_len):
    block = min(256, full_len)
    reach = full_len // 2
    for first in range(0, full_len, block):
        yield first, first + block, max(0, first - reach)


def block_rows(seq_index, index, count):
    return pl.ds(pl.multiple_of((seq_index ^ index) * count, count), count)


def scalar_index(seq_index):
    return jnp.reshape(seq_index, (1,)).astype(jnp.int32)


def attn_forward_body(
    index_ref, x_ref, weight_ref, first_gain_ref, head_gain_ref, cos_ref, sin_ref, doc_row_ref, doc_col_ref,
    normed_ref, raw_ref, rot_ref, attended_ref, inverse_ref,
    *, group_size, head_dim,
):
    bf16 = jnp.bfloat16
    full_len = normed_ref.shape[0]
    local_len = x_ref.shape[1] - EXTRA_ROWS
    scale = head_dim ** (-0.5)

    @pl.when(pl.program_id(0) == 0)
    def _():
        for index in range(x_ref.shape[0]):
            unit, _ = normalize(x_ref[index, :local_len].astype(jnp.float32))
            normed_ref[block_rows(index_ref[0], index, local_len)] = (
                unit * first_gain_ref[...]
            ).astype(bf16)

    share = weight_ref.shape[1] - EXTRA_ROWS
    weight = weight_ref[:, :share, :].reshape(-1, weight_ref.shape[2])
    rot_width = (group_size + 1) * head_dim
    for first in range(0, full_len, 256):
        rows = slice(first, first + 256)
        raw = dot_nn(normed_ref[rows], weight)
        raw_ref[rows] = raw[:, :rot_width]
        rot_ref[rows, rot_width:] = raw[:, rot_width:].astype(bf16)
        for head in range(group_size + 1):
            cols = slice(head * head_dim, (head + 1) * head_dim)
            unit, _ = normalize(raw[:, cols])
            gain = head_gain_ref[:1] if head < group_size else head_gain_ref[1:2]
            scaled = unit * gain
            rot_ref[rows, cols] = (
                scaled * cos_ref[rows] + turned(scaled) * sin_ref[rows]
            ).astype(bf16)
    key = slice(group_size * head_dim, rot_width)
    for first, last, start in query_blocks(full_len):
        keys = rot_ref[start:last, key]
        values = rot_ref[start:last, rot_width:]
        widened = jnp.concatenate([values, jnp.ones_like(values)], axis=1)
        count = last - start
        query_index = lax.broadcasted_iota(jnp.int32, (last - first, count), 0) + first
        key_index = lax.broadcasted_iota(jnp.int32, (last - first, count), 1) + start
        allowed = (key_index <= query_index) & (
            doc_col_ref[first:last] == doc_row_ref[:, start:last]
        )
        for head in range(group_size):
            cols = slice(head * head_dim, (head + 1) * head_dim)
            scores = dot_nt(rot_ref[first:last, cols], keys)
            powers = jnp.where(allowed, jnp.exp2(scores * (scale * LOG2E)), 0.0)
            sums = dot_nn(powers.astype(bf16), widened)
            inverse = 1.0 / sums[:, head_dim:]
            attended_ref[first:last, cols] = (sums[:, :head_dim] * inverse).astype(bf16)
            inverse_ref[head * 8 : (head + 1) * 8, first:last] = inverse.T[:8]


def attn_forward(seq_index, x_parts, weight, first_gain, head_gain, cosine, sine, doc_row, doc_col, sizes):
    group_size, head_dim, local_kv = sizes
    full_len = doc_col.shape[0]
    model_width = x_parts.shape[2]
    group_cols = (group_size + 2) * head_dim
    whole = lambda shape: pl.BlockSpec(shape, lambda j, index: (0,) * len(shape))
    columns = lambda rows, width: pl.BlockSpec((rows, width), lambda j, index: (0, j))
    rot_width = (group_size + 1) * head_dim
    query_width = group_size * head_dim
    return pl.pallas_call(
        functools.partial(attn_forward_body, group_size=group_size, head_dim=head_dim),
        name="attn_forward",
        grid_spec=pltpu.PrefetchScalarGridSpec(
        num_scalar_prefetch=1,
        grid=(local_kv,),
        in_specs=[
            whole(x_parts.shape),
            pl.BlockSpec(weight.shape[:2] + (group_cols,), lambda j, index: (0, 0, j)),
            whole(first_gain.shape),
            whole(head_gain.shape),
            whole(cosine.shape),
            whole(sine.shape),
            whole(doc_row.shape),
            whole(doc_col.shape),
        ],
        out_specs=[
            whole((full_len, model_width)),
            columns(full_len, rot_width),
            columns(full_len, group_cols),
            columns(full_len, query_width),
            pl.BlockSpec((group_size * 8, full_len), lambda j, index: (j, 0)),
        ],
        ),
        out_shape=[
            jax.ShapeDtypeStruct((full_len, model_width), jnp.bfloat16),
            jax.ShapeDtypeStruct((full_len, local_kv * rot_width), jnp.float32),
            jax.ShapeDtypeStruct((full_len, local_kv * group_cols), jnp.bfloat16),
            jax.ShapeDtypeStruct((full_len, local_kv * query_width), jnp.bfloat16),
            jax.ShapeDtypeStruct((local_kv * group_size * 8, full_len), jnp.float32),
        ],
        compiler_params=pltpu.CompilerParams(vmem_limit_bytes=VMEM_LIMIT),
        cost_estimate=pl.CostEstimate(flops=1000, transcendentals=0, bytes_accessed=1000),
    )(scalar_index(seq_index), x_parts, weight, first_gain, head_gain, cosine, sine, doc_row, doc_col)


def attn_backward_body(
    index_ref, given_ref, out_weight_ref, attended_t_ref, normed_t_ref, weight_ref, first_gain_ref,
    second_sum_ref, head_gain_ref, cos_ref, sin_ref, doc_row_ref, doc_col_ref,
    raw_ref, rot_ref, inverse_ref,
    raw_grad_ref, pack_ref,
    gain_acc_ref, head_acc_ref, grad_acc_ref, query_acc_ref, key_acc_ref, value_acc_ref, middle_ref,
    *, group_size, head_dim, seq_size,
):
    bf16 = jnp.bfloat16
    full_len = middle_ref.shape[0]
    scale = head_dim ** (-0.5)
    step = pl.program_id(0)
    rot_width = (group_size + 1) * head_dim
    key = slice(group_size * head_dim, rot_width)

    @pl.when(step == 0)
    def _():
        gain_acc_ref[...] = jnp.zeros_like(gain_acc_ref)
        head_acc_ref[...] = jnp.zeros_like(head_acc_ref)
        count = full_len // seq_size
        for index in range(seq_size):
            rows = slice(index * count, (index + 1) * count)
            middle_ref[block_rows(index_ref[0], index, count)] = given_ref[rows]

    for first in range(0, full_len, 256):
        rows = slice(first, first + 256)
        grad_acc_ref[rows] = dot_nt(middle_ref[rows], out_weight_ref[...]).astype(bf16)
    key_acc_ref[...] = jnp.zeros_like(key_acc_ref)
    value_acc_ref[...] = jnp.zeros_like(value_acc_ref)
    key_turned = rot_ref[:, key].T
    for first, last, start in query_blocks(full_len):
        keys = rot_ref[start:last, key]
        values = rot_ref[start:last, rot_width:]
        count = last - start
        key_index = lax.broadcasted_iota(jnp.int32, (count, last - first), 0) + start
        query_index = lax.broadcasted_iota(jnp.int32, (count, last - first), 1) + first
        allowed = (key_index <= query_index) & (
            doc_col_ref[start:last] == doc_row_ref[:, first:last]
        )
        for head in range(group_size):
            cols = slice(head * head_dim, (head + 1) * head_dim)
            queries = rot_ref[first:last, cols]
            grads = grad_acc_ref[first:last, cols]
            scores = dot_nt(keys, queries)
            powers = jnp.where(allowed, jnp.exp2(scores * (scale * LOG2E)), 0.0)
            weights = powers * inverse_ref[head * 8 : head * 8 + 1, first:last]
            value_acc_ref[start:last] += dot_nn(weights.astype(bf16), grads)
            prob_grad = dot_nt(values, grads)
            delta = jnp.sum(weights * prob_grad, axis=0, keepdims=True)
            score_grad = (weights * (prob_grad - delta)).astype(bf16)
            key_acc_ref[start:last] += dot_nn(score_grad, queries)
            query_acc_ref[first:last, cols] = dot_nn(key_turned[:, start:last], score_grad).T

    query_sum = jnp.zeros((1, head_dim), jnp.float32)
    key_sum = jnp.zeros((1, head_dim), jnp.float32)
    for first in range(0, full_len, 256):
        rows = slice(first, first + 256)
        for head in range(group_size + 1):
            cols = slice(head * head_dim, (head + 1) * head_dim)
            is_query = head < group_size
            rot_grad = query_acc_ref[rows, cols] if is_query else key_acc_ref[rows]
            rot_grad = (rot_grad * scale).astype(bf16).astype(jnp.float32)
            scaled_grad = rot_grad * cos_ref[rows] - turned(rot_grad) * sin_ref[rows]
            unit, inverse = normalize(raw_ref[rows, cols])
            part = jnp.sum(scaled_grad * unit, axis=0, keepdims=True)
            if is_query:
                query_sum = query_sum + part
            else:
                key_sum = key_sum + part
            gain = head_gain_ref[:1] if is_query else head_gain_ref[1:2]
            raw_grad_ref[rows, cols] = norm_backward(scaled_grad, unit, inverse, gain).astype(bf16)
        raw_grad_ref[rows, rot_width:] = value_acc_ref[rows].astype(bf16)
    head_acc_ref[:1] += query_sum
    head_acc_ref[1:2] += key_sum

    dp_size, pack_rows, cols = pack_ref.shape
    share = weight_ref.shape[1] - EXTRA_ROWS
    for index in range(dp_size):
        mine = slice(index * share, (index + 1) * share)
        grad = dot_nn(normed_t_ref[mine], raw_grad_ref[...])
        pack_ref[index, :share] = grad.astype(bf16)
        terms = grad * weight_ref[index, :share].astype(jnp.float32)
        folded = terms[:, :128]
        for chunk in range(128, cols, 128):
            folded = folded + terms[:, chunk : chunk + 128]
        gain_acc_ref[:1, mine] += jnp.sum(folded.T, axis=0, keepdims=True)
        pack_ref[index, share : share + EXTRA_ROWS] = jnp.zeros((EXTRA_ROWS, cols), bf16)

    @pl.when(step == pl.num_programs(0) - 1)
    def _():
        for index in range(dp_size):
            mine = slice(index * share, (index + 1) * share)
            slots = [
                gain_acc_ref[:1, mine] / first_gain_ref[:, mine],
                second_sum_ref[:, mine],
                head_acc_ref[:1],
                head_acc_ref[1:2],
            ]
            slots = [
                slot
                if slot.shape[1] == GAIN_SLOT
                else jnp.concatenate(
                    [slot, jnp.zeros((1, GAIN_SLOT - slot.shape[1]), jnp.float32)], axis=1
                )
                for slot in slots
            ]
            row = jnp.concatenate(slots, axis=1)
            pack_ref[index, share : share + EXTRA_ROWS] = jnp.broadcast_to(
                row, (EXTRA_ROWS, cols)
            ).astype(bf16)

    out_rows = attended_t_ref.shape[0] // dp_size
    blocks = middle_ref.shape[1] // (cols * pl.num_programs(0))
    for block in range(blocks):
        begin = pl.multiple_of((block * pl.num_programs(0) + step) * cols, 128)
        grad = dot_nn(attended_t_ref[...], middle_ref[:, pl.ds(begin, cols)]).astype(bf16)
        base = share + EXTRA_ROWS + block * out_rows
        for index in range(dp_size):
            pack_ref[index, base : base + out_rows] = grad[index * out_rows : (index + 1) * out_rows]


def attn_backward(
    seq_index, seq_size, middle, out_weight, attended_t, normed_t, weight, first_gain, second_sum, head_gain, cosine,
    sine, doc_row, doc_col, raw, rot, inverse, sizes,
):
    group_size, head_dim, local_kv = sizes
    full_len, model_width = middle.shape
    dp_size, share = weight.shape[0], weight.shape[1] - EXTRA_ROWS
    group_cols = (group_size + 2) * head_dim
    total_cols = local_kv * group_cols
    rot_width = (group_size + 1) * head_dim
    query_width = group_size * head_dim
    out_rows = out_weight.shape[0] // dp_size * (model_width // total_cols)
    pack_rows = share + EXTRA_ROWS + out_rows
    whole = lambda shape: pl.BlockSpec(shape, lambda j, index: (0,) * len(shape))
    columns = lambda rows, width: pl.BlockSpec((rows, width), lambda j, index: (0, j))
    return pl.pallas_call(
        functools.partial(attn_backward_body, group_size=group_size, head_dim=head_dim, seq_size=seq_size),
        name="attn_backward",
        grid_spec=pltpu.PrefetchScalarGridSpec(
        num_scalar_prefetch=1,
        grid=(local_kv,),
        in_specs=[
            whole(middle.shape),
            pl.BlockSpec((query_width, model_width), lambda j, index: (j, 0)),
            whole(attended_t.shape),
            whole(normed_t.shape),
            pl.BlockSpec(weight.shape[:2] + (group_cols,), lambda j, index: (0, 0, j)),
            whole(first_gain.shape),
            whole(second_sum.shape),
            whole(head_gain.shape),
            whole(cosine.shape),
            whole(sine.shape),
            whole(doc_row.shape),
            whole(doc_col.shape),
            columns(full_len, rot_width),
            columns(full_len, group_cols),
            pl.BlockSpec((group_size * 8, full_len), lambda j, index: (j, 0)),
        ],
        out_specs=[
            columns(full_len, group_cols),
            pl.BlockSpec((dp_size, pack_rows, group_cols), lambda j, index: (0, 0, j)),
        ],
        scratch_shapes=[
            pltpu.VMEM((8, model_width), jnp.float32),
            pltpu.VMEM((8, head_dim), jnp.float32),
            pltpu.VMEM((full_len, query_width), jnp.bfloat16),
            pltpu.VMEM((full_len, query_width), jnp.float32),
            pltpu.VMEM((full_len, head_dim), jnp.float32),
            pltpu.VMEM((full_len, head_dim), jnp.float32),
            pltpu.VMEM((full_len, model_width), jnp.bfloat16),
        ],
        ),
        out_shape=[
            jax.ShapeDtypeStruct((full_len, total_cols), jnp.bfloat16),
            jax.ShapeDtypeStruct((dp_size, pack_rows, total_cols), jnp.bfloat16),
        ],
        compiler_params=pltpu.CompilerParams(vmem_limit_bytes=VMEM_LIMIT),
        cost_estimate=pl.CostEstimate(flops=1000, transcendentals=0, bytes_accessed=1000),
    )(
        scalar_index(seq_index), middle, out_weight, attended_t, normed_t, weight, first_gain, second_sum, head_gain, cosine,
        sine, doc_row, doc_col, raw, rot, inverse,
    )


def column_group(down_rows, own_rows, dp_size):
    count = 1
    while own_rows * count % 128 or dp_size % count:
        count += 1
    return count


def column_choice(seq_index, count, down_rows, own_rows):
    own = lax.broadcasted_iota(jnp.int32, (1, own_rows * count), 1)
    target = own + own_rows * seq_index
    for block in range(1, count):
        target = target + jnp.where(own >= block * own_rows, down_rows - own_rows, 0)
    whole = lax.broadcasted_iota(jnp.int32, (down_rows * count, own_rows * count), 0)
    return jnp.where(whole == target, 1.0, 0.0).astype(jnp.bfloat16)


def pack_mlp_body(index_ref, gate_ref, up_ref, down_ref, pack_ref, *, dp_size, seq_size):
    share = gate_ref.shape[0]
    own_rows = down_ref.shape[0]
    down_rows = own_rows * seq_size
    count = column_group(down_rows, own_rows, dp_size)
    choice = column_choice(index_ref[0], count, down_rows, own_rows)
    width = down_rows * count
    column = 0
    for source in (gate_ref, up_ref):
        for first in range(0, source.shape[1], width):
            chosen = dot_nn(source[:, first : first + width], choice).astype(jnp.bfloat16)
            for part in range(0, chosen.shape[1], 128):
                base = column // PACK_COLS * share
                half = column % PACK_COLS
                pack_ref[base : base + share, half : half + 128] = chosen[:, part : part + 128]
                column += 128
    base = column // PACK_COLS * share
    for first in range(0, down_ref.shape[1], PACK_COLS):
        pack_ref[base : base + own_rows] = down_ref[:, first : first + PACK_COLS]
        base += own_rows


def pack_mlp(seq_index, gate_weight, up_weight, down_weight, dp_size, seq_size):
    share, ff_total = gate_weight.shape
    model_width = down_weight.shape[1]
    own_rows = down_weight.shape[0] // seq_size
    rows = share * (2 * ff_total // seq_size // PACK_COLS) + own_rows * (model_width // PACK_COLS)
    whole = pl.BlockSpec((share, ff_total), lambda i, index: (0, 0))
    return pl.pallas_call(
        functools.partial(pack_mlp_body, dp_size=dp_size, seq_size=seq_size),
        name="pack_mlp",
        grid_spec=pltpu.PrefetchScalarGridSpec(
            num_scalar_prefetch=1,
            grid=(1,),
            in_specs=[
                whole, whole, pl.BlockSpec((own_rows, model_width), lambda i, index: (index[0], 0))
            ],
            out_specs=pl.BlockSpec((rows, PACK_COLS), lambda i, index: (0, 0)),
        ),
        out_shape=jax.ShapeDtypeStruct((rows, PACK_COLS), jnp.bfloat16),
        compiler_params=pltpu.CompilerParams(vmem_limit_bytes=VMEM_LIMIT),
        cost_estimate=pl.CostEstimate(flops=1000, transcendentals=0, bytes_accessed=1000),
    )(jnp.reshape(seq_index, (1,)).astype(jnp.int32), gate_weight, up_weight, down_weight)


def mlp_body(
    index_ref, normed_ref, grad_ref, weight_ref, hidden_ref, pair_grad_ref, normed_grad_ref,
    pair_ref, down_ref,
):
    bf16 = jnp.bfloat16
    width = hidden_ref.shape[1]
    dp_size = weight_ref.shape[0]
    share = pair_ref.shape[0] // dp_size
    down_share = width // dp_size

    @pl.when(pl.program_id(0) == 0)
    def _():
        for index in range(dp_size):
            base = 0
            rows = slice(index * share, (index + 1) * share)
            for first in range(0, 2 * width, PACK_COLS):
                pair_ref[rows, first : first + PACK_COLS] = weight_ref[index, base : base + share]
                base += share
            rows = slice(index * down_share, (index + 1) * down_share)
            for first in range(0, down_ref.shape[1], PACK_COLS):
                down_ref[rows, first : first + PACK_COLS] = weight_ref[
                    index, base : base + down_share
                ]
                base += down_share

    pair = dot_nn(normed_ref[...], pair_ref[...])
    hidden_grad = dot_nt(grad_ref[...], down_ref[...])
    gate_pre = pair[:, :width]
    up_pre = pair[:, width:]
    sigmoid_gate = jax.nn.sigmoid(gate_pre)
    silu_gate = gate_pre * sigmoid_gate
    hidden_ref[...] = (silu_gate * up_pre).astype(bf16)
    gate_pre_grad = (
        hidden_grad * up_pre * sigmoid_gate * (1.0 + gate_pre * (1.0 - sigmoid_gate))
    )
    pair_grad_ref[:, :width] = gate_pre_grad.astype(bf16)
    pair_grad_ref[:, width:] = (hidden_grad * silu_gate).astype(bf16)
    normed_grad_ref[...] = dot_nt(pair_grad_ref[...], pair_ref[...]).astype(bf16)


def mlp_forward_backward(seq_index, seq_size, normed, grads, weight, width):
    full_len, model_width = normed.shape
    block = full_len // seq_size
    rows = lambda cols: pl.BlockSpec((block, cols), lambda i, index: (i, 0))
    whole = lambda shape: pl.BlockSpec(shape, lambda i, index: (0,) * len(shape))
    return pl.pallas_call(
        mlp_body,
        name="mlp_forward_backward",
        grid_spec=pltpu.PrefetchScalarGridSpec(
        num_scalar_prefetch=1,
        grid=(full_len // block,),
        in_specs=[rows(model_width), rows(model_width), whole(weight.shape)],
        out_specs=[
            rows(width),
            rows(2 * width),
            pl.BlockSpec((block, model_width), lambda i, index: (i ^ index[0], 0)),
        ],
        scratch_shapes=[
            pltpu.VMEM((model_width, 2 * width), jnp.bfloat16),
            pltpu.VMEM((width, model_width), jnp.bfloat16),
        ],
        ),
        out_shape=[
            jax.ShapeDtypeStruct((full_len, width), jnp.bfloat16),
            jax.ShapeDtypeStruct((full_len, 2 * width), jnp.bfloat16),
            jax.ShapeDtypeStruct((full_len, model_width), jnp.bfloat16),
        ],
        compiler_params=pltpu.CompilerParams(vmem_limit_bytes=VMEM_LIMIT),
        cost_estimate=pl.CostEstimate(flops=1000, transcendentals=0, bytes_accessed=1000),
    )(scalar_index(seq_index), normed, grads, weight)


def mlp_grads_body(
    index_ref, normed_ref, pair_grad_ref, hidden_ref, grad_ref, weight_ref, pack_ref, block_ref,
    down_ref, *, seq_size,
):
    bf16 = jnp.bfloat16
    dp_size = pack_ref.shape[0]
    share = normed_ref.shape[1] // dp_size
    down_share = hidden_ref.shape[1] // dp_size
    normed_t = normed_ref[...].T
    for index in range(dp_size):
        grad = dot_nn(normed_t[index * share : (index + 1) * share], pair_grad_ref[...])
        grad = grad.astype(bf16)
        base = 0
        for first in range(0, grad.shape[1], PACK_COLS):
            pack_ref[index, base : base + share] = grad[:, first : first + PACK_COLS]
            base += share
    grad = dot_nn(hidden_ref[...].T, grad_ref[...])
    for index in range(dp_size):
        base = share * (pair_grad_ref.shape[1] // PACK_COLS)
        rows = slice(index * down_share, (index + 1) * down_share)
        mine = grad[rows].astype(bf16)
        for first in range(0, grad.shape[1], PACK_COLS):
            pack_ref[index, base : base + down_share] = mine[:, first : first + PACK_COLS]
            down_ref[rows, first : first + PACK_COLS] = weight_ref[index, base : base + down_share]
            base += down_share
    count = hidden_ref.shape[0] // seq_size
    for index in range(seq_size):
        rows = slice(index * count, (index + 1) * count)
        block_ref[block_rows(index_ref[0], index, count)] = dot_nn(
            hidden_ref[rows], down_ref[...]
        ).astype(bf16)


def mlp_grads(seq_index, seq_size, normed, pair_grad, hidden, grads, weight):
    whole = lambda shape: pl.BlockSpec(shape, lambda i, index: (0,) * len(shape))
    operands = (normed, pair_grad, hidden, grads, weight)
    return pl.pallas_call(
        functools.partial(mlp_grads_body, seq_size=seq_size),
        name="mlp_grads",
        grid_spec=pltpu.PrefetchScalarGridSpec(
            num_scalar_prefetch=1,
            grid=(1,),
            in_specs=[whole(operand.shape) for operand in operands],
            out_specs=[whole(weight.shape), whole(normed.shape)],
            scratch_shapes=[pltpu.VMEM((hidden.shape[1], normed.shape[1]), jnp.bfloat16)],
        ),
        out_shape=[
            jax.ShapeDtypeStruct(weight.shape, jnp.bfloat16),
            jax.ShapeDtypeStruct(normed.shape, jnp.bfloat16),
        ],
        compiler_params=pltpu.CompilerParams(vmem_limit_bytes=VMEM_LIMIT),
        cost_estimate=pl.CostEstimate(flops=1000, transcendentals=0, bytes_accessed=1000),
    )(scalar_index(seq_index), *operands)


def input_body(raw_grad_ref, weight_ref, out_ref):
    share = weight_ref.shape[1] - EXTRA_ROWS
    weight = weight_ref[:, :share, :].reshape(-1, weight_ref.shape[2])
    out_ref[...] = dot_nt(raw_grad_ref[...], weight).astype(jnp.bfloat16)


def input_partial(raw_grad, weight):
    full_len, cols = raw_grad.shape
    block = min(256, full_len)
    model_width = weight.shape[0] * (weight.shape[1] - EXTRA_ROWS)
    return pl.pallas_call(
        input_body,
        name="input_partial",
        grid=(full_len // block,),
        in_specs=[
            pl.BlockSpec((block, cols), lambda i: (i, 0)),
            pl.BlockSpec(weight.shape, lambda i: (0, 0, 0)),
        ],
        out_specs=pl.BlockSpec((block, model_width), lambda i: (i, 0)),
        out_shape=jax.ShapeDtypeStruct((full_len, model_width), jnp.bfloat16),
        compiler_params=pltpu.CompilerParams(vmem_limit_bytes=VMEM_LIMIT),
        cost_estimate=pl.CostEstimate(flops=1000, transcendentals=0, bytes_accessed=1000),
    )(raw_grad, weight)


def finish_attn_body(parts_ref, query_ref, key_ref, value_ref, gain_ref, *, group_size, head_dim):
    f32 = jnp.float32
    seq_size, rows, cols = parts_ref.shape
    share = rows - EXTRA_ROWS
    group_cols = (group_size + 2) * head_dim
    rot_width = group_size * head_dim
    total = jnp.zeros((EXTRA_ROWS, group_cols), f32)
    head = 0
    for index in range(seq_size):
        for first in range(0, cols, group_cols):
            part = parts_ref[index, :share, first : first + group_cols].astype(f32)
            query_ref[:, head * rot_width : (head + 1) * rot_width] = part[:, :rot_width]
            spot = slice(head * head_dim, (head + 1) * head_dim)
            key_ref[:, spot] = part[:, rot_width : rot_width + head_dim]
            value_ref[:, spot] = part[:, rot_width + head_dim :]
            head += 1
        total = total + parts_ref[index, share:, cols - group_cols :].astype(f32)
    gain_ref[...] = total


def finish_attn(parts, sizes):
    group_size, head_dim, local_kv = sizes
    seq_size, rows, cols = parts.shape
    share = rows - EXTRA_ROWS
    heads = seq_size * local_kv
    return pl.pallas_call(
        functools.partial(finish_attn_body, group_size=group_size, head_dim=head_dim),
        name="finish_attn",
        out_shape=[
            jax.ShapeDtypeStruct((share, heads * group_size * head_dim), jnp.float32),
            jax.ShapeDtypeStruct((share, heads * head_dim), jnp.float32),
            jax.ShapeDtypeStruct((share, heads * head_dim), jnp.float32),
            jax.ShapeDtypeStruct((EXTRA_ROWS, (group_size + 2) * head_dim), jnp.float32),
        ],
        compiler_params=pltpu.CompilerParams(vmem_limit_bytes=VMEM_LIMIT),
        cost_estimate=pl.CostEstimate(flops=1000, transcendentals=0, bytes_accessed=1000),
    )(parts)


def finish_mlp_body(index_ref, parts_ref, gate_ref, up_ref, down_ref, *, dp_size):
    f32 = jnp.float32
    seq_size = parts_ref.shape[0]
    share, ff_total = gate_ref.shape
    down_rows = down_ref.shape[0]
    own_rows = down_rows // seq_size
    count = column_group(down_rows, own_rows, dp_size)
    choices = [
        column_choice(index_ref[0] ^ index, count, down_rows, own_rows)
        for index in range(seq_size)
    ]
    width = down_rows * count
    column = 0
    for target_ref in (gate_ref, up_ref):
        for first in range(0, ff_total, width):
            total = jnp.zeros((share, width), f32)
            for index in range(seq_size):
                pieces = []
                for part in range(column, column + own_rows * count, 128):
                    base = part // PACK_COLS * share
                    half = part % PACK_COLS
                    pieces.append(parts_ref[index, base : base + share, half : half + 128])
                total = total + dot_nt(jnp.concatenate(pieces, axis=1), choices[index])
            target_ref[:, first : first + width] = total
            column += own_rows * count
    for index in range(seq_size):
        base = column // PACK_COLS * share
        for first in range(0, down_ref.shape[1], PACK_COLS):
            part = parts_ref[index, base : base + own_rows]
            down_ref[
                block_rows(index_ref[0], index, own_rows), first : first + PACK_COLS
            ] = part.astype(f32)
            base += own_rows


def finish_mlp(seq_index, parts, share, ff_total, model_width, down_rows, dp_size):
    return pl.pallas_call(
        functools.partial(finish_mlp_body, dp_size=dp_size),
        name="finish_mlp",
        grid_spec=pltpu.PrefetchScalarGridSpec(
            num_scalar_prefetch=1,
            grid=(1,),
            in_specs=[pl.BlockSpec(parts.shape, lambda i, index: (0, 0, 0))],
            out_specs=[
                pl.BlockSpec((share, ff_total), lambda i, index: (0, 0)),
                pl.BlockSpec((share, ff_total), lambda i, index: (0, 0)),
                pl.BlockSpec((down_rows, model_width), lambda i, index: (0, 0)),
            ],
        ),
        out_shape=[
            jax.ShapeDtypeStruct((share, ff_total), jnp.float32),
            jax.ShapeDtypeStruct((share, ff_total), jnp.float32),
            jax.ShapeDtypeStruct((down_rows, model_width), jnp.float32),
        ],
        compiler_params=pltpu.CompilerParams(vmem_limit_bytes=VMEM_LIMIT),
        cost_estimate=pl.CostEstimate(flops=1000, transcendentals=0, bytes_accessed=1000),
    )(scalar_index(seq_index), parts)


def exchange(pieces):
    return lax.all_to_all(pieces, "seq", split_axis=0, concat_axis=0, tiled=True)


def gather_parts(rows, seq_size):
    return exchange(jnp.broadcast_to(rows[None], (seq_size,) + rows.shape))


def gather_tokens(rows, seq_size):
    return gather_parts(rows, seq_size).reshape((seq_size * rows.shape[0],) + rows.shape[1:])


def pass_on(values, seq_size, flip):
    return lax.ppermute(values, "seq", [(index, index ^ flip) for index in range(seq_size)])


def first_hops(rows, seq_size):
    if seq_size != 4:
        return (rows,)
    half = rows.shape[0] // 2
    upper, lower = rows[:half], rows[half:]
    return (
        upper,
        lower,
        pass_on(upper, seq_size, 1),
        pass_on(lower, seq_size, 2),
        pass_on(upper, seq_size, 2),
        pass_on(lower, seq_size, 1),
    )


def second_hops(hops, seq_size, seq_index):
    if seq_size != 4:
        parts = gather_parts(hops[0], seq_size)
        return jnp.stack(
            [
                lax.dynamic_index_in_dim(parts, seq_index ^ index, 0, keepdims=False)
                for index in range(seq_size)
            ]
        )
    upper, lower, upper_one, lower_two, upper_two, lower_one = hops
    upper_three = pass_on(upper_one, seq_size, 2)
    lower_three = pass_on(lower_two, seq_size, 1)
    return jnp.concatenate(
        [upper, lower, upper_one, lower_one, upper_two, lower_two, upper_three, lower_three]
    ).reshape((seq_size, -1) + upper.shape[1:])


def gather_flipped(rows, seq_size, seq_index):
    return second_hops(first_hops(rows, seq_size), seq_size, seq_index)


def scatter_tokens(partial, seq_size):
    pieces = partial.astype(jnp.bfloat16).reshape((seq_size, -1) + partial.shape[1:])
    return jnp.sum(exchange(pieces).astype(jnp.float32), axis=0)


def row_routes(dp_size, seq_size):
    routes = []
    for dp_index in range(dp_size):
        for seq_index in range(seq_size):
            holder = dp_size // seq_size * seq_index + dp_index // seq_size
            routes.append(
                (holder * seq_size + dp_index % seq_size, dp_index * seq_size + seq_index)
            )
    return routes


def on_device(
    block_in,
    positions,
    doc_ids,
    first_gain,
    query_weight,
    key_weight,
    value_matrix,
    query_gain,
    key_gain,
    out_weight,
    second_gain,
    gate_weight,
    up_weight,
    down_weight,
    grad_out,
):
    bf16 = jnp.bfloat16
    f32 = jnp.float32
    dp_size = lax.axis_size("dp")
    seq_size = lax.axis_size("seq")
    seq_index = lax.axis_index("seq")
    dp_index = lax.axis_index("dp")
    local_len, model_width = block_in.shape[1:]
    full_len = local_len * seq_size
    head_dim = query_gain.shape[0] * dp_size
    query_heads = query_weight.shape[1] // head_dim
    kv_heads = key_weight.shape[1] // head_dim
    group_size = query_heads // kv_heads
    local_kv = kv_heads // seq_size
    query_cols = local_kv * group_size * head_dim
    group_cols = (group_size + 2) * head_dim
    attn_cols = local_kv * group_cols
    ff_cols = gate_weight.shape[1] // seq_size
    share = first_gain.shape[0]
    head_share = query_gain.shape[0]
    gain_width = 2 * share + 2 * head_share
    sizes = (group_size, head_dim, local_kv)
    routes = row_routes(dp_size, seq_size)
    back_routes = [(target, source) for source, target in routes]

    def own_columns(matrix, width):
        return lax.dynamic_slice_in_dim(matrix, seq_index * width, width, axis=1)

    def own_rows(matrix):
        count = matrix.shape[0] // seq_size
        return lax.dynamic_slice_in_dim(matrix, seq_index * count, count, axis=0)

    x_local = block_in[0]
    coarse = jnp.pad(positions // 64, ((0, 0), (0, model_width - local_len)))
    fine = jnp.pad(positions % 64, ((0, 0), (0, model_width - local_len)))
    extra = jnp.pad(jnp.concatenate([coarse, fine]), ((0, EXTRA_ROWS - 2), (0, 0))).astype(bf16)
    x_parts = gather_flipped(jnp.concatenate([x_local, extra]), seq_size, seq_index)

    query_own = own_columns(query_weight, query_cols).reshape(share, local_kv, -1)
    key_own = own_columns(key_weight, local_kv * head_dim).reshape(share, local_kv, -1)
    value_own = own_columns(value_matrix, local_kv * head_dim).reshape(share, local_kv, -1)
    attn_piece = jnp.concatenate([query_own, key_own, value_own], axis=2).reshape(share, -1)
    gains = jnp.concatenate([first_gain, second_gain, query_gain, key_gain])[None]
    gains = jnp.pad(gains, ((0, EXTRA_ROWS - 1), (0, attn_cols - gain_width)))
    attn_full = lax.all_gather(jnp.concatenate([attn_piece, gains], axis=0), "dp", axis=0)
    gains_full = attn_full[:, share, :gain_width].astype(f32)
    first_full = gains_full[:, :share].reshape(1, -1)
    second_full = gains_full[:, share : 2 * share].reshape(1, -1)
    head_gain = jnp.pad(
        gains_full[:, 2 * share :].reshape(dp_size, 2, head_share).swapaxes(0, 1).reshape(2, -1),
        ((0, 6), (0, 0)),
    )

    out_count = out_weight.shape[0] // seq_size
    routed = lax.ppermute(own_rows(out_weight), ("dp", "seq"), routes)
    mlp_piece = pack_mlp(seq_index, gate_weight, up_weight, down_weight, dp_size, seq_size)
    x_parts, routed, mlp_piece = lax.optimization_barrier((x_parts, routed, mlp_piece))
    out_full = lax.all_gather(routed, "dp", axis=0, tiled=True)
    mlp_full = lax.all_gather(mlp_piece, "dp", axis=0)

    coarse_full = x_parts[:, local_len, :local_len].astype(f32)
    fine_full = x_parts[:, local_len + 1, :local_len].astype(f32)
    block_ids = jnp.arange(seq_size)
    placed = (block_ids[:, None] ^ seq_index) == block_ids[None]
    positions_full = jnp.sum(
        jnp.where(placed[:, :, None], coarse_full * 64.0 + fine_full, 0.0), axis=1
    )
    cosine, sine = rope_tables(positions_full.reshape(full_len), head_dim)
    doc_row = doc_ids
    doc_col = doc_ids.reshape(full_len, 1)
    cosine, sine, doc_col, grad_local = lax.optimization_barrier(
        (cosine, sine, doc_col, grad_out[0])
    )
    grad_hops = first_hops(grad_local, seq_size)
    normed_full, raw, rot, attended_heads, inverse = attn_forward(
        seq_index, x_parts, attn_full, first_full, head_gain, cosine, sine, doc_row, doc_col, sizes
    )
    attended_heads, grad_hops = lax.optimization_barrier((attended_heads, grad_hops))
    grad_full = second_hops(grad_hops, seq_size, seq_index).reshape(full_len, -1)
    residual = x_local.astype(f32)
    middle = residual + scatter_tokens(
        product("le,ed->ld", attended_heads, out_full), seq_size
    )
    normed_t = normed_full.T
    attended_t = attended_heads.T
    middle, normed_t, attended_t = lax.optimization_barrier((middle, normed_t, attended_t))
    second_unit, second_inverse = normalize(middle)
    second_normed = gather_flipped(
        (second_unit * second_full).astype(bf16), seq_size, seq_index
    ).reshape(full_len, -1)
    hidden, pair_grad, normed_grad_part = mlp_forward_backward(
        seq_index, seq_size, second_normed, grad_full, mlp_full, ff_cols
    )
    normed_grad = scatter_tokens(normed_grad_part, seq_size)

    def scatter_grad(pack):
        return lax.psum_scatter(pack, "dp", scatter_dimension=0, tiled=False)

    mlp_pack, block_part = mlp_grads(
        seq_index, seq_size, second_normed, pair_grad, hidden, grad_full, mlp_full
    )
    second_sum = jnp.sum(normed_grad * second_unit, axis=0, keepdims=True)
    middle_grad = grad_out[0].astype(f32) + norm_backward(
        normed_grad, second_unit, second_inverse, second_full
    )
    middle_low, mlp_pack = lax.optimization_barrier((middle_grad.astype(bf16), mlp_pack))
    mlp_grad = scatter_grad(mlp_pack)
    middle_low = gather_flipped(middle_low, seq_size, seq_index).reshape(full_len, -1)
    middle_low, block_part = lax.optimization_barrier((middle_low, block_part))
    block_parts = exchange(block_part.reshape(seq_size, local_len, model_width))
    raw_grad, attn_pack = attn_backward(
        seq_index, seq_size, middle_low, out_full, attended_t, normed_t, attn_full, first_full, second_sum, head_gain,
        cosine, sine, doc_row, doc_col, raw, rot, inverse, sizes,
    )
    raw_grad, attn_pack, block_parts, mlp_grad = lax.optimization_barrier(
        (raw_grad, attn_pack, block_parts, mlp_grad)
    )
    attn_grad = scatter_grad(attn_pack)
    pair_hops = first_hops(mlp_grad, seq_size)
    raw_grad, pair_hops = lax.optimization_barrier((raw_grad, pair_hops))
    pair_parts = second_hops(pair_hops, seq_size, seq_index)
    first_normed_part, pair_parts = lax.optimization_barrier(
        (input_partial(raw_grad, attn_full), pair_parts)
    )
    first_normed_grad = scatter_tokens(first_normed_part, seq_size)
    first_unit, first_inverse = normalize(residual)
    input_grad = middle_grad + norm_backward(
        first_normed_grad, first_unit, first_inverse, first_full
    )
    block_out = (middle + jnp.sum(block_parts.astype(f32), axis=0)).astype(bf16)

    gate_weight_grad, up_weight_grad, down_weight_grad = finish_mlp(
        seq_index, pair_parts, share, gate_weight.shape[1], model_width, down_weight.shape[0], dp_size
    )
    attn_grad, input_grad, gate_weight_grad = lax.optimization_barrier(
        (attn_grad, input_grad, gate_weight_grad)
    )
    attn_parts = gather_parts(attn_grad[: share + EXTRA_ROWS], seq_size)
    out_home = lax.ppermute(attn_grad[share + EXTRA_ROWS :], ("dp", "seq"), back_routes)
    attn_parts, out_home = lax.optimization_barrier((attn_parts, out_home))
    query_weight_grad, key_weight_grad, value_weight_grad, gain_sums = finish_attn(
        attn_parts, sizes
    )
    out_home = out_home.reshape(-1, out_count, attn_cols).swapaxes(0, 1).reshape(out_count, -1)
    out_weight_grad = gather_tokens(out_home, seq_size).astype(f32)

    def own_gain(slot):
        return lax.dynamic_slice_in_dim(
            gain_sums[0], slot * GAIN_SLOT + dp_index * head_share, head_share, axis=0
        )

    return (
        block_out[None],
        input_grad[None],
        gain_sums[0, :share],
        query_weight_grad,
        key_weight_grad,
        value_weight_grad,
        own_gain(2),
        own_gain(3),
        out_weight_grad,
        gain_sums[0, GAIN_SLOT : GAIN_SLOT + share],
        gate_weight_grad,
        up_weight_grad,
        down_weight_grad,
    )


def solution(mesh):
    placed = (
        P("dp", "seq", None),
        P("dp", "seq"),
        P("dp", None),
        P("dp"),
        P("dp", None),
        P("dp", None),
        P("dp", None),
        P("dp"),
        P("dp"),
        P("dp", None),
        P("dp"),
        P("dp", None),
        P("dp", None),
        P("dp", None),
        P("dp", "seq", None),
    )
    return jax.shard_map(
        on_device,
        mesh=mesh,
        in_specs=placed,
        out_specs=(
            P("dp", "seq", None),
            P("dp", "seq", None),
            P("dp"),
            P("dp", None),
            P("dp", None),
            P("dp", None),
            P("dp"),
            P("dp"),
            P("dp", None),
            P("dp"),
            P("dp", None),
            P("dp", None),
            P("dp", None),
        ),
        check_vma=False,
    )
```

```python
import functools

import jax
import jax.numpy as jnp
from jax import lax
from jax.experimental import pallas as pl
from jax.experimental.pallas import tpu as pltpu
from jax.sharding import PartitionSpec as P

EPSILON = 1e-06
THETA = 1000000.0
LOG2E = 1.4426950408889634
EXTRA_ROWS = 16
GAIN_SLOT = 128
PACK_COLS = 256
VMEM_LIMIT = 60 * 1024 * 1024


def product(einsum_form, left_side, right_side):
    return jnp.einsum(einsum_form, left_side, right_side, preferred_element_type=jnp.float32)


def dot(left, right, contract):
    return lax.dot_general(
        left, right, (contract, ((), ())), preferred_element_type=jnp.float32
    )


def dot_nn(left, right):
    return dot(left, right, ((1,), (0,)))


def dot_nt(left, right):
    return dot(left, right, ((1,), (1,)))


def normalize(values):
    inverse = lax.rsqrt(jnp.mean(values * values, axis=-1, keepdims=True) + EPSILON)
    return (values * inverse, inverse)


def norm_backward(upstream, unit_rows, inverse, gain_values):
    scaled = upstream * gain_values
    return inverse * (scaled - unit_rows * jnp.mean(scaled * unit_rows, axis=-1, keepdims=True))


def rope_tables(positions, head_dim):
    half_dim = head_dim // 2
    inverse_freq = 1.0 / THETA ** (jnp.arange(half_dim, dtype=jnp.float32) * 2.0 / head_dim)
    angles = positions.astype(jnp.float32)[:, None] * inverse_freq
    cosine = jnp.cos(angles)
    sine = jnp.sin(angles)
    return (
        jnp.concatenate([cosine, cosine], axis=-1),
        jnp.concatenate([-sine, sine], axis=-1),
    )


def turned(values):
    return pltpu.roll(values, values.shape[-1] // 2, axis=1)


def query_blocks(full_len):
    block = min(256, full_len)
    reach = full_len // 2
    for first in range(0, full_len, block):
        yield first, first + block, max(0, first - reach)


def block_rows(seq_index, index, count):
    return pl.ds(pl.multiple_of((seq_index ^ index) * count, count), count)


def scalar_index(seq_index):
    return jnp.reshape(seq_index, (1,)).astype(jnp.int32)


def attn_forward_body(
    index_ref, x_ref, weight_ref, first_gain_ref, head_gain_ref, cos_ref, sin_ref, doc_row_ref, doc_col_ref,
    normed_ref, raw_ref, rot_ref, attended_ref, inverse_ref,
    *, group_size, head_dim,
):
    bf16 = jnp.bfloat16
    full_len = normed_ref.shape[0]
    local_len = x_ref.shape[1] - EXTRA_ROWS
    scale = head_dim ** (-0.5)

    @pl.when(pl.program_id(0) == 0)
    def _():
        for index in range(x_ref.shape[0]):
            unit, _ = normalize(x_ref[index, :local_len].astype(jnp.float32))
            normed_ref[block_rows(index_ref[0], index, local_len)] = (
                unit * first_gain_ref[...]
            ).astype(bf16)

    share = weight_ref.shape[1] - EXTRA_ROWS
    weight = weight_ref[:, :share, :].reshape(-1, weight_ref.shape[2])
    rot_width = (group_size + 1) * head_dim
    for first in range(0, full_len, 256):
        rows = slice(first, first + 256)
        raw = dot_nn(normed_ref[rows], weight)
        raw_ref[rows] = raw[:, :rot_width]
        rot_ref[rows, rot_width:] = raw[:, rot_width:].astype(bf16)
        for head in range(group_size + 1):
            cols = slice(head * head_dim, (head + 1) * head_dim)
            unit, _ = normalize(raw[:, cols])
            gain = head_gain_ref[:1] if head < group_size else head_gain_ref[1:2]
            scaled = unit * gain
            rot_ref[rows, cols] = (
                scaled * cos_ref[rows] + turned(scaled) * sin_ref[rows]
            ).astype(bf16)
    key = slice(group_size * head_dim, rot_width)
    for first, last, start in query_blocks(full_len):
        keys = rot_ref[start:last, key]
        values = rot_ref[start:last, rot_width:]
        widened = jnp.concatenate([values, jnp.ones_like(values)], axis=1)
        count = last - start
        query_index = lax.broadcasted_iota(jnp.int32, (last - first, count), 0) + first
        key_index = lax.broadcasted_iota(jnp.int32, (last - first, count), 1) + start
        allowed = (key_index <= query_index) & (
            doc_col_ref[first:last] == doc_row_ref[:, start:last]
        )
        for head in range(group_size):
            cols = slice(head * head_dim, (head + 1) * head_dim)
            scores = dot_nt(rot_ref[first:last, cols], keys)
            powers = jnp.where(allowed, jnp.exp2(scores * (scale * LOG2E)), 0.0)
            sums = dot_nn(powers.astype(bf16), widened)
            inverse = 1.0 / sums[:, head_dim:]
            attended_ref[first:last, cols] = (sums[:, :head_dim] * inverse).astype(bf16)
            inverse_ref[head * 8 : (head + 1) * 8, first:last] = inverse.T[:8]


def attn_forward(seq_index, x_parts, weight, first_gain, head_gain, cosine, sine, doc_row, doc_col, sizes):
    group_size, head_dim, local_kv = sizes
    full_len = doc_col.shape[0]
    model_width = x_parts.shape[2]
    group_cols = (group_size + 2) * head_dim
    whole = lambda shape: pl.BlockSpec(shape, lambda j, index: (0,) * len(shape))
    columns = lambda rows, width: pl.BlockSpec((rows, width), lambda j, index: (0, j))
    rot_width = (group_size + 1) * head_dim
    query_width = group_size * head_dim
    return pl.pallas_call(
        functools.partial(attn_forward_body, group_size=group_size, head_dim=head_dim),
        name="attn_forward",
        grid_spec=pltpu.PrefetchScalarGridSpec(
        num_scalar_prefetch=1,
        grid=(local_kv,),
        in_specs=[
            whole(x_parts.shape),
            pl.BlockSpec(weight.shape[:2] + (group_cols,), lambda j, index: (0, 0, j)),
            whole(first_gain.shape),
            whole(head_gain.shape),
            whole(cosine.shape),
            whole(sine.shape),
            whole(doc_row.shape),
            whole(doc_col.shape),
        ],
        out_specs=[
            whole((full_len, model_width)),
            columns(full_len, rot_width),
            columns(full_len, group_cols),
            columns(full_len, query_width),
            pl.BlockSpec((group_size * 8, full_len), lambda j, index: (j, 0)),
        ],
        ),
        out_shape=[
            jax.ShapeDtypeStruct((full_len, model_width), jnp.bfloat16),
            jax.ShapeDtypeStruct((full_len, local_kv * rot_width), jnp.float32),
            jax.ShapeDtypeStruct((full_len, local_kv * group_cols), jnp.bfloat16),
            jax.ShapeDtypeStruct((full_len, local_kv * query_width), jnp.bfloat16),
            jax.ShapeDtypeStruct((local_kv * group_size * 8, full_len), jnp.float32),
        ],
        compiler_params=pltpu.CompilerParams(vmem_limit_bytes=VMEM_LIMIT),
        cost_estimate=pl.CostEstimate(flops=1000, transcendentals=0, bytes_accessed=1000),
    )(scalar_index(seq_index), x_parts, weight, first_gain, head_gain, cosine, sine, doc_row, doc_col)


def attn_backward_body(
    index_ref, given_ref, out_weight_ref, attended_t_ref, normed_t_ref, weight_ref, first_gain_ref,
    second_sum_ref, head_gain_ref, cos_ref, sin_ref, doc_row_ref, doc_col_ref,
    raw_ref, rot_ref, inverse_ref,
    raw_grad_ref, pack_ref,
    gain_acc_ref, head_acc_ref, grad_acc_ref, query_acc_ref, key_acc_ref, value_acc_ref, middle_ref,
    *, group_size, head_dim, seq_size,
):
    bf16 = jnp.bfloat16
    full_len = middle_ref.shape[0]
    scale = head_dim ** (-0.5)
    step = pl.program_id(0)
    rot_width = (group_size + 1) * head_dim
    key = slice(group_size * head_dim, rot_width)

    @pl.when(step == 0)
    def _():
        gain_acc_ref[...] = jnp.zeros_like(gain_acc_ref)
        head_acc_ref[...] = jnp.zeros_like(head_acc_ref)
        count = full_len // seq_size
        for index in range(seq_size):
            rows = slice(index * count, (index + 1) * count)
            middle_ref[block_rows(index_ref[0], index, count)] = given_ref[rows]

    for first in range(0, full_len, 256):
        rows = slice(first, first + 256)
        grad_acc_ref[rows] = dot_nt(middle_ref[rows], out_weight_ref[...]).astype(bf16)
    key_acc_ref[...] = jnp.zeros_like(key_acc_ref)
    value_acc_ref[...] = jnp.zeros_like(value_acc_ref)
    key_turned = rot_ref[:, key].T
    for first, last, start in query_blocks(full_len):
        keys = rot_ref[start:last, key]
        values = rot_ref[start:last, rot_width:]
        count = last - start
        key_index = lax.broadcasted_iota(jnp.int32, (count, last - first), 0) + start
        query_index = lax.broadcasted_iota(jnp.int32, (count, last - first), 1) + first
        allowed = (key_index <= query_index) & (
            doc_col_ref[start:last] == doc_row_ref[:, first:last]
        )
        for head in range(group_size):
            cols = slice(head * head_dim, (head + 1) * head_dim)
            queries = rot_ref[first:last, cols]
            grads = grad_acc_ref[first:last, cols]
            scores = dot_nt(keys, queries)
            powers = jnp.where(allowed, jnp.exp2(scores * (scale * LOG2E)), 0.0)
            weights = powers * inverse_ref[head * 8 : head * 8 + 1, first:last]
            value_acc_ref[start:last] += dot_nn(weights.astype(bf16), grads)
            prob_grad = dot_nt(values, grads)
            delta = jnp.sum(weights * prob_grad, axis=0, keepdims=True)
            score_grad = (weights * (prob_grad - delta)).astype(bf16)
            key_acc_ref[start:last] += dot_nn(score_grad, queries)
            query_acc_ref[first:last, cols] = dot_nn(key_turned[:, start:last], score_grad).T

    query_sum = jnp.zeros((1, head_dim), jnp.float32)
    key_sum = jnp.zeros((1, head_dim), jnp.float32)
    for first in range(0, full_len, 256):
        rows = slice(first, first + 256)
        for head in range(group_size + 1):
            cols = slice(head * head_dim, (head + 1) * head_dim)
            is_query = head < group_size
            rot_grad = query_acc_ref[rows, cols] if is_query else key_acc_ref[rows]
            rot_grad = (rot_grad * scale).astype(bf16).astype(jnp.float32)
            scaled_grad = rot_grad * cos_ref[rows] - turned(rot_grad) * sin_ref[rows]
            unit, inverse = normalize(raw_ref[rows, cols])
            part = jnp.sum(scaled_grad * unit, axis=0, keepdims=True)
            if is_query:
                query_sum = query_sum + part
            else:
                key_sum = key_sum + part
            gain = head_gain_ref[:1] if is_query else head_gain_ref[1:2]
            raw_grad_ref[rows, cols] = norm_backward(scaled_grad, unit, inverse, gain).astype(bf16)
        raw_grad_ref[rows, rot_width:] = value_acc_ref[rows].astype(bf16)
    head_acc_ref[:1] += query_sum
    head_acc_ref[1:2] += key_sum

    dp_size, pack_rows, cols = pack_ref.shape
    share = weight_ref.shape[1] - EXTRA_ROWS
    for index in range(dp_size):
        mine = slice(index * share, (index + 1) * share)
        grad = dot_nn(normed_t_ref[mine], raw_grad_ref[...])
        pack_ref[index, :share] = grad.astype(bf16)
        terms = grad * weight_ref[index, :share].astype(jnp.float32)
        folded = terms[:, :128]
        for chunk in range(128, cols, 128):
            folded = folded + terms[:, chunk : chunk + 128]
        gain_acc_ref[:1, mine] += jnp.sum(folded.T, axis=0, keepdims=True)
        pack_ref[index, share : share + EXTRA_ROWS] = jnp.zeros((EXTRA_ROWS, cols), bf16)

    @pl.when(step == pl.num_programs(0) - 1)
    def _():
        for index in range(dp_size):
            mine = slice(index * share, (index + 1) * share)
            slots = [
                gain_acc_ref[:1, mine] / first_gain_ref[:, mine],
                second_sum_ref[:, mine],
                head_acc_ref[:1],
                head_acc_ref[1:2],
            ]
            slots = [
                slot
                if slot.shape[1] == GAIN_SLOT
                else jnp.concatenate(
                    [slot, jnp.zeros((1, GAIN_SLOT - slot.shape[1]), jnp.float32)], axis=1
                )
                for slot in slots
            ]
            row = jnp.concatenate(slots, axis=1)
            pack_ref[index, share : share + EXTRA_ROWS] = jnp.broadcast_to(
                row, (EXTRA_ROWS, cols)
            ).astype(bf16)

    out_rows = attended_t_ref.shape[0] // dp_size
    blocks = middle_ref.shape[1] // (cols * pl.num_programs(0))
    for block in range(blocks):
        begin = pl.multiple_of((block * pl.num_programs(0) + step) * cols, 128)
        grad = dot_nn(attended_t_ref[...], middle_ref[:, pl.ds(begin, cols)]).astype(bf16)
        base = share + EXTRA_ROWS + block * out_rows
        for index in range(dp_size):
            pack_ref[index, base : base + out_rows] = grad[index * out_rows : (index + 1) * out_rows]


def attn_backward(
    seq_index, seq_size, middle, out_weight, attended_t, normed_t, weight, first_gain, second_sum, head_gain, cosine,
    sine, doc_row, doc_col, raw, rot, inverse, sizes,
):
    group_size, head_dim, local_kv = sizes
    full_len, model_width = middle.shape
    dp_size, share = weight.shape[0], weight.shape[1] - EXTRA_ROWS
    group_cols = (group_size + 2) * head_dim
    total_cols = local_kv * group_cols
    rot_width = (group_size + 1) * head_dim
    query_width = group_size * head_dim
    out_rows = out_weight.shape[0] // dp_size * (model_width // total_cols)
    pack_rows = share + EXTRA_ROWS + out_rows
    whole = lambda shape: pl.BlockSpec(shape, lambda j, index: (0,) * len(shape))
    columns = lambda rows, width: pl.BlockSpec((rows, width), lambda j, index: (0, j))
    return pl.pallas_call(
        functools.partial(attn_backward_body, group_size=group_size, head_dim=head_dim, seq_size=seq_size),
        name="attn_backward",
        grid_spec=pltpu.PrefetchScalarGridSpec(
        num_scalar_prefetch=1,
        grid=(local_kv,),
        in_specs=[
            whole(middle.shape),
            pl.BlockSpec((query_width, model_width), lambda j, index: (j, 0)),
            whole(attended_t.shape),
            whole(normed_t.shape),
            pl.BlockSpec(weight.shape[:2] + (group_cols,), lambda j, index: (0, 0, j)),
            whole(first_gain.shape),
            whole(second_sum.shape),
            whole(head_gain.shape),
            whole(cosine.shape),
            whole(sine.shape),
            whole(doc_row.shape),
            whole(doc_col.shape),
            columns(full_len, rot_width),
            columns(full_len, group_cols),
            pl.BlockSpec((group_size * 8, full_len), lambda j, index: (j, 0)),
        ],
        out_specs=[
            columns(full_len, group_cols),
            pl.BlockSpec((dp_size, pack_rows, group_cols), lambda j, index: (0, 0, j)),
        ],
        scratch_shapes=[
            pltpu.VMEM((8, model_width), jnp.float32),
            pltpu.VMEM((8, head_dim), jnp.float32),
            pltpu.VMEM((full_len, query_width), jnp.bfloat16),
            pltpu.VMEM((full_len, query_width), jnp.float32),
            pltpu.VMEM((full_len, head_dim), jnp.float32),
            pltpu.VMEM((full_len, head_dim), jnp.float32),
            pltpu.VMEM((full_len, model_width), jnp.bfloat16),
        ],
        ),
        out_shape=[
            jax.ShapeDtypeStruct((full_len, total_cols), jnp.bfloat16),
            jax.ShapeDtypeStruct((dp_size, pack_rows, total_cols), jnp.bfloat16),
        ],
        compiler_params=pltpu.CompilerParams(vmem_limit_bytes=VMEM_LIMIT),
        cost_estimate=pl.CostEstimate(flops=1000, transcendentals=0, bytes_accessed=1000),
    )(
        scalar_index(seq_index), middle, out_weight, attended_t, normed_t, weight, first_gain, second_sum, head_gain, cosine,
        sine, doc_row, doc_col, raw, rot, inverse,
    )


def column_group(down_rows, own_rows, dp_size):
    count = 1
    while own_rows * count % 128 or dp_size % count:
        count += 1
    return count


def column_choice(seq_index, count, down_rows, own_rows):
    own = lax.broadcasted_iota(jnp.int32, (1, own_rows * count), 1)
    target = own + own_rows * seq_index
    for block in range(1, count):
        target = target + jnp.where(own >= block * own_rows, down_rows - own_rows, 0)
    whole = lax.broadcasted_iota(jnp.int32, (down_rows * count, own_rows * count), 0)
    return jnp.where(whole == target, 1.0, 0.0).astype(jnp.bfloat16)


def pack_mlp_body(index_ref, gate_ref, up_ref, down_ref, pack_ref, *, dp_size, seq_size):
    share = gate_ref.shape[0]
    own_rows = down_ref.shape[0]
    down_rows = own_rows * seq_size
    count = column_group(down_rows, own_rows, dp_size)
    choice = column_choice(index_ref[0], count, down_rows, own_rows)
    width = down_rows * count
    column = 0
    for source in (gate_ref, up_ref):
        for first in range(0, source.shape[1], width):
            chosen = dot_nn(source[:, first : first + width], choice).astype(jnp.bfloat16)
            for part in range(0, chosen.shape[1], 128):
                base = column // PACK_COLS * share
                half = column % PACK_COLS
                pack_ref[base : base + share, half : half + 128] = chosen[:, part : part + 128]
                column += 128
    base = column // PACK_COLS * share
    for first in range(0, down_ref.shape[1], PACK_COLS):
        pack_ref[base : base + own_rows] = down_ref[:, first : first + PACK_COLS]
        base += own_rows


def pack_mlp(seq_index, gate_weight, up_weight, down_weight, dp_size, seq_size):
    share, ff_total = gate_weight.shape
    model_width = down_weight.shape[1]
    own_rows = down_weight.shape[0] // seq_size
    rows = share * (2 * ff_total // seq_size // PACK_COLS) + own_rows * (model_width // PACK_COLS)
    whole = pl.BlockSpec((share, ff_total), lambda i, index: (0, 0))
    return pl.pallas_call(
        functools.partial(pack_mlp_body, dp_size=dp_size, seq_size=seq_size),
        name="pack_mlp",
        grid_spec=pltpu.PrefetchScalarGridSpec(
            num_scalar_prefetch=1,
            grid=(1,),
            in_specs=[
                whole, whole, pl.BlockSpec((own_rows, model_width), lambda i, index: (index[0], 0))
            ],
            out_specs=pl.BlockSpec((rows, PACK_COLS), lambda i, index: (0, 0)),
        ),
        out_shape=jax.ShapeDtypeStruct((rows, PACK_COLS), jnp.bfloat16),
        compiler_params=pltpu.CompilerParams(vmem_limit_bytes=VMEM_LIMIT),
        cost_estimate=pl.CostEstimate(flops=1000, transcendentals=0, bytes_accessed=1000),
    )(jnp.reshape(seq_index, (1,)).astype(jnp.int32), gate_weight, up_weight, down_weight)


def mlp_body(
    index_ref, normed_ref, grad_ref, weight_ref, hidden_ref, pair_grad_ref, normed_grad_ref,
    pair_ref, down_ref,
):
    bf16 = jnp.bfloat16
    width = hidden_ref.shape[1]
    dp_size = weight_ref.shape[0]
    share = pair_ref.shape[0] // dp_size
    down_share = width // dp_size

    @pl.when(pl.program_id(0) == 0)
    def _():
        for index in range(dp_size):
            base = 0
            rows = slice(index * share, (index + 1) * share)
            for first in range(0, 2 * width, PACK_COLS):
                pair_ref[rows, first : first + PACK_COLS] = weight_ref[index, base : base + share]
                base += share
            rows = slice(index * down_share, (index + 1) * down_share)
            for first in range(0, down_ref.shape[1], PACK_COLS):
                down_ref[rows, first : first + PACK_COLS] = weight_ref[
                    index, base : base + down_share
                ]
                base += down_share

    pair = dot_nn(normed_ref[...], pair_ref[...])
    hidden_grad = dot_nt(grad_ref[...], down_ref[...])
    gate_pre = pair[:, :width]
    up_pre = pair[:, width:]
    sigmoid_gate = jax.nn.sigmoid(gate_pre)
    silu_gate = gate_pre * sigmoid_gate
    hidden_ref[...] = (silu_gate * up_pre).astype(bf16)
    gate_pre_grad = (
        hidden_grad * up_pre * sigmoid_gate * (1.0 + gate_pre * (1.0 - sigmoid_gate))
    )
    pair_grad_ref[:, :width] = gate_pre_grad.astype(bf16)
    pair_grad_ref[:, width:] = (hidden_grad * silu_gate).astype(bf16)
    normed_grad_ref[...] = dot_nt(pair_grad_ref[...], pair_ref[...]).astype(bf16)


def mlp_forward_backward(seq_index, seq_size, normed, grads, weight, width):
    full_len, model_width = normed.shape
    block = full_len // seq_size
    rows = lambda cols: pl.BlockSpec((block, cols), lambda i, index: (i, 0))
    whole = lambda shape: pl.BlockSpec(shape, lambda i, index: (0,) * len(shape))
    return pl.pallas_call(
        mlp_body,
        name="mlp_forward_backward",
        grid_spec=pltpu.PrefetchScalarGridSpec(
        num_scalar_prefetch=1,
        grid=(full_len // block,),
        in_specs=[rows(model_width), rows(model_width), whole(weight.shape)],
        out_specs=[
            rows(width),
            rows(2 * width),
            pl.BlockSpec((block, model_width), lambda i, index: (i ^ index[0], 0)),
        ],
        scratch_shapes=[
            pltpu.VMEM((model_width, 2 * width), jnp.bfloat16),
            pltpu.VMEM((width, model_width), jnp.bfloat16),
        ],
        ),
        out_shape=[
            jax.ShapeDtypeStruct((full_len, width), jnp.bfloat16),
            jax.ShapeDtypeStruct((full_len, 2 * width), jnp.bfloat16),
            jax.ShapeDtypeStruct((full_len, model_width), jnp.bfloat16),
        ],
        compiler_params=pltpu.CompilerParams(vmem_limit_bytes=VMEM_LIMIT),
        cost_estimate=pl.CostEstimate(flops=1000, transcendentals=0, bytes_accessed=1000),
    )(scalar_index(seq_index), normed, grads, weight)


def mlp_grads_body(
    index_ref, normed_ref, pair_grad_ref, hidden_ref, grad_ref, weight_ref, pack_ref, block_ref,
    down_ref, *, seq_size,
):
    bf16 = jnp.bfloat16
    dp_size = pack_ref.shape[0]
    share = normed_ref.shape[1] // dp_size
    down_share = hidden_ref.shape[1] // dp_size
    normed_t = normed_ref[...].T
    for index in range(dp_size):
        grad = dot_nn(normed_t[index * share : (index + 1) * share], pair_grad_ref[...])
        grad = grad.astype(bf16)
        base = 0
        for first in range(0, grad.shape[1], PACK_COLS):
            pack_ref[index, base : base + share] = grad[:, first : first + PACK_COLS]
            base += share
    grad = dot_nn(hidden_ref[...].T, grad_ref[...])
    for index in range(dp_size):
        base = share * (pair_grad_ref.shape[1] // PACK_COLS)
        rows = slice(index * down_share, (index + 1) * down_share)
        mine = grad[rows].astype(bf16)
        for first in range(0, grad.shape[1], PACK_COLS):
            pack_ref[index, base : base + down_share] = mine[:, first : first + PACK_COLS]
            down_ref[rows, first : first + PACK_COLS] = weight_ref[index, base : base + down_share]
            base += down_share
    count = hidden_ref.shape[0] // seq_size
    for index in range(seq_size):
        rows = slice(index * count, (index + 1) * count)
        block_ref[block_rows(index_ref[0], index, count)] = dot_nn(
            hidden_ref[rows], down_ref[...]
        ).astype(bf16)


def mlp_grads(seq_index, seq_size, normed, pair_grad, hidden, grads, weight):
    whole = lambda shape: pl.BlockSpec(shape, lambda i, index: (0,) * len(shape))
    operands = (normed, pair_grad, hidden, grads, weight)
    return pl.pallas_call(
        functools.partial(mlp_grads_body, seq_size=seq_size),
        name="mlp_grads",
        grid_spec=pltpu.PrefetchScalarGridSpec(
            num_scalar_prefetch=1,
            grid=(1,),
            in_specs=[whole(operand.shape) for operand in operands],
            out_specs=[whole(weight.shape), whole(normed.shape)],
            scratch_shapes=[pltpu.VMEM((hidden.shape[1], normed.shape[1]), jnp.bfloat16)],
        ),
        out_shape=[
            jax.ShapeDtypeStruct(weight.shape, jnp.bfloat16),
            jax.ShapeDtypeStruct(normed.shape, jnp.bfloat16),
        ],
        compiler_params=pltpu.CompilerParams(vmem_limit_bytes=VMEM_LIMIT),
        cost_estimate=pl.CostEstimate(flops=1000, transcendentals=0, bytes_accessed=1000),
    )(scalar_index(seq_index), *operands)


def input_body(raw_grad_ref, weight_ref, out_ref):
    share = weight_ref.shape[1] - EXTRA_ROWS
    weight = weight_ref[:, :share, :].reshape(-1, weight_ref.shape[2])
    out_ref[...] = dot_nt(raw_grad_ref[...], weight).astype(jnp.bfloat16)


def input_partial(raw_grad, weight):
    full_len, cols = raw_grad.shape
    block = min(256, full_len)
    model_width = weight.shape[0] * (weight.shape[1] - EXTRA_ROWS)
    return pl.pallas_call(
        input_body,
        name="input_partial",
        grid=(full_len // block,),
        in_specs=[
            pl.BlockSpec((block, cols), lambda i: (i, 0)),
            pl.BlockSpec(weight.shape, lambda i: (0, 0, 0)),
        ],
        out_specs=pl.BlockSpec((block, model_width), lambda i: (i, 0)),
        out_shape=jax.ShapeDtypeStruct((full_len, model_width), jnp.bfloat16),
        compiler_params=pltpu.CompilerParams(vmem_limit_bytes=VMEM_LIMIT),
        cost_estimate=pl.CostEstimate(flops=1000, transcendentals=0, bytes_accessed=1000),
    )(raw_grad, weight)


def finish_attn_body(parts_ref, query_ref, key_ref, value_ref, gain_ref, *, group_size, head_dim):
    f32 = jnp.float32
    seq_size, rows, cols = parts_ref.shape
    share = rows - EXTRA_ROWS
    group_cols = (group_size + 2) * head_dim
    rot_width = group_size * head_dim
    total = jnp.zeros((EXTRA_ROWS, group_cols), f32)
    head = 0
    for index in range(seq_size):
        for first in range(0, cols, group_cols):
            part = parts_ref[index, :share, first : first + group_cols].astype(f32)
            query_ref[:, head * rot_width : (head + 1) * rot_width] = part[:, :rot_width]
            spot = slice(head * head_dim, (head + 1) * head_dim)
            key_ref[:, spot] = part[:, rot_width : rot_width + head_dim]
            value_ref[:, spot] = part[:, rot_width + head_dim :]
            head += 1
        total = total + parts_ref[index, share:, cols - group_cols :].astype(f32)
    gain_ref[...] = total


def finish_attn(parts, sizes):
    group_size, head_dim, local_kv = sizes
    seq_size, rows, cols = parts.shape
    share = rows - EXTRA_ROWS
    heads = seq_size * local_kv
    return pl.pallas_call(
        functools.partial(finish_attn_body, group_size=group_size, head_dim=head_dim),
        name="finish_attn",
        out_shape=[
            jax.ShapeDtypeStruct((share, heads * group_size * head_dim), jnp.float32),
            jax.ShapeDtypeStruct((share, heads * head_dim), jnp.float32),
            jax.ShapeDtypeStruct((share, heads * head_dim), jnp.float32),
            jax.ShapeDtypeStruct((EXTRA_ROWS, (group_size + 2) * head_dim), jnp.float32),
        ],
        compiler_params=pltpu.CompilerParams(vmem_limit_bytes=VMEM_LIMIT),
        cost_estimate=pl.CostEstimate(flops=1000, transcendentals=0, bytes_accessed=1000),
    )(parts)


def finish_mlp_body(index_ref, parts_ref, gate_ref, up_ref, down_ref, *, dp_size):
    f32 = jnp.float32
    seq_size = parts_ref.shape[0]
    share, ff_total = gate_ref.shape
    down_rows = down_ref.shape[0]
    own_rows = down_rows // seq_size
    count = column_group(down_rows, own_rows, dp_size)
    choices = [
        column_choice(index_ref[0] ^ index, count, down_rows, own_rows)
        for index in range(seq_size)
    ]
    width = down_rows * count
    column = 0
    for target_ref in (gate_ref, up_ref):
        for first in range(0, ff_total, width):
            total = jnp.zeros((share, width), f32)
            for index in range(seq_size):
                pieces = []
                for part in range(column, column + own_rows * count, 128):
                    base = part // PACK_COLS * share
                    half = part % PACK_COLS
                    pieces.append(parts_ref[index, base : base + share, half : half + 128])
                total = total + dot_nt(jnp.concatenate(pieces, axis=1), choices[index])
            target_ref[:, first : first + width] = total
            column += own_rows * count
    for index in range(seq_size):
        base = column // PACK_COLS * share
        for first in range(0, down_ref.shape[1], PACK_COLS):
            part = parts_ref[index, base : base + own_rows]
            down_ref[
                block_rows(index_ref[0], index, own_rows), first : first + PACK_COLS
            ] = part.astype(f32)
            base += own_rows


def finish_mlp(seq_index, parts, share, ff_total, model_width, down_rows, dp_size):
    return pl.pallas_call(
        functools.partial(finish_mlp_body, dp_size=dp_size),
        name="finish_mlp",
        grid_spec=pltpu.PrefetchScalarGridSpec(
            num_scalar_prefetch=1,
            grid=(1,),
            in_specs=[pl.BlockSpec(parts.shape, lambda i, index: (0, 0, 0))],
            out_specs=[
                pl.BlockSpec((share, ff_total), lambda i, index: (0, 0)),
                pl.BlockSpec((share, ff_total), lambda i, index: (0, 0)),
                pl.BlockSpec((down_rows, model_width), lambda i, index: (0, 0)),
            ],
        ),
        out_shape=[
            jax.ShapeDtypeStruct((share, ff_total), jnp.float32),
            jax.ShapeDtypeStruct((share, ff_total), jnp.float32),
            jax.ShapeDtypeStruct((down_rows, model_width), jnp.float32),
        ],
        compiler_params=pltpu.CompilerParams(vmem_limit_bytes=VMEM_LIMIT),
        cost_estimate=pl.CostEstimate(flops=1000, transcendentals=0, bytes_accessed=1000),
    )(scalar_index(seq_index), parts)


def exchange(pieces):
    return lax.all_to_all(pieces, "seq", split_axis=0, concat_axis=0, tiled=True)


def gather_parts(rows, seq_size):
    return exchange(jnp.broadcast_to(rows[None], (seq_size,) + rows.shape))


def gather_tokens(rows, seq_size):
    return gather_parts(rows, seq_size).reshape((seq_size * rows.shape[0],) + rows.shape[1:])


def pass_on(values, seq_size, flip):
    return lax.ppermute(values, "seq", [(index, index ^ flip) for index in range(seq_size)])


def first_hops(rows, seq_size):
    if seq_size != 4:
        return (rows,)
    half = rows.shape[0] // 2
    upper, lower = rows[:half], rows[half:]
    return (
        upper,
        lower,
        pass_on(upper, seq_size, 1),
        pass_on(lower, seq_size, 2),
        pass_on(upper, seq_size, 2),
        pass_on(lower, seq_size, 1),
    )


def second_hops(hops, seq_size, seq_index):
    if seq_size != 4:
        parts = gather_parts(hops[0], seq_size)
        return jnp.stack(
            [
                lax.dynamic_index_in_dim(parts, seq_index ^ index, 0, keepdims=False)
                for index in range(seq_size)
            ]
        )
    upper, lower, upper_one, lower_two, upper_two, lower_one = hops
    upper_three = pass_on(upper_one, seq_size, 2)
    lower_three = pass_on(lower_two, seq_size, 1)
    return jnp.concatenate(
        [upper, lower, upper_one, lower_one, upper_two, lower_two, upper_three, lower_three]
    ).reshape((seq_size, -1) + upper.shape[1:])


def gather_flipped(rows, seq_size, seq_index):
    return second_hops(first_hops(rows, seq_size), seq_size, seq_index)


def scatter_tokens(partial, seq_size):
    pieces = partial.astype(jnp.bfloat16).reshape((seq_size, -1) + partial.shape[1:])
    return jnp.sum(exchange(pieces).astype(jnp.float32), axis=0)


def row_routes(dp_size, seq_size):
    routes = []
    for dp_index in range(dp_size):
        for seq_index in range(seq_size):
            holder = dp_size // seq_size * seq_index + dp_index // seq_size
            routes.append(
                (holder * seq_size + dp_index % seq_size, dp_index * seq_size + seq_index)
            )
    return routes


def on_device(
    block_in,
    positions,
    doc_ids,
    first_gain,
    query_weight,
    key_weight,
    value_matrix,
    query_gain,
    key_gain,
    out_weight,
    second_gain,
    gate_weight,
    up_weight,
    down_weight,
    grad_out,
):
    bf16 = jnp.bfloat16
    f32 = jnp.float32
    dp_size = lax.axis_size("dp")
    seq_size = lax.axis_size("seq")
    seq_index = lax.axis_index("seq")
    dp_index = lax.axis_index("dp")
    local_len, model_width = block_in.shape[1:]
    full_len = local_len * seq_size
    head_dim = query_gain.shape[0] * dp_size
    query_heads = query_weight.shape[1] // head_dim
    kv_heads = key_weight.shape[1] // head_dim
    group_size = query_heads // kv_heads
    local_kv = kv_heads // seq_size
    query_cols = local_kv * group_size * head_dim
    group_cols = (group_size + 2) * head_dim
    attn_cols = local_kv * group_cols
    ff_cols = gate_weight.shape[1] // seq_size
    share = first_gain.shape[0]
    head_share = query_gain.shape[0]
    gain_width = 2 * share + 2 * head_share
    sizes = (group_size, head_dim, local_kv)
    routes = row_routes(dp_size, seq_size)
    back_routes = [(target, source) for source, target in routes]

    def own_columns(matrix, width):
        return lax.dynamic_slice_in_dim(matrix, seq_index * width, width, axis=1)

    def own_rows(matrix):
        count = matrix.shape[0] // seq_size
        return lax.dynamic_slice_in_dim(matrix, seq_index * count, count, axis=0)

    x_local = block_in[0]
    coarse = jnp.pad(positions // 64, ((0, 0), (0, model_width - local_len)))
    fine = jnp.pad(positions % 64, ((0, 0), (0, model_width - local_len)))
    extra = jnp.pad(jnp.concatenate([coarse, fine]), ((0, EXTRA_ROWS - 2), (0, 0))).astype(bf16)
    x_parts = gather_flipped(jnp.concatenate([x_local, extra]), seq_size, seq_index)

    query_own = own_columns(query_weight, query_cols).reshape(share, local_kv, -1)
    key_own = own_columns(key_weight, local_kv * head_dim).reshape(share, local_kv, -1)
    value_own = own_columns(value_matrix, local_kv * head_dim).reshape(share, local_kv, -1)
    attn_piece = jnp.concatenate([query_own, key_own, value_own], axis=2).reshape(share, -1)
    gains = jnp.concatenate([first_gain, second_gain, query_gain, key_gain])[None]
    gains = jnp.pad(gains, ((0, EXTRA_ROWS - 1), (0, attn_cols - gain_width)))
    attn_full = lax.all_gather(jnp.concatenate([attn_piece, gains], axis=0), "dp", axis=0)
    gains_full = attn_full[:, share, :gain_width].astype(f32)
    first_full = gains_full[:, :share].reshape(1, -1)
    second_full = gains_full[:, share : 2 * share].reshape(1, -1)
    head_gain = jnp.pad(
        gains_full[:, 2 * share :].reshape(dp_size, 2, head_share).swapaxes(0, 1).reshape(2, -1),
        ((0, 6), (0, 0)),
    )

    out_count = out_weight.shape[0] // seq_size
    routed = lax.ppermute(own_rows(out_weight), ("dp", "seq"), routes)
    mlp_piece = pack_mlp(seq_index, gate_weight, up_weight, down_weight, dp_size, seq_size)
    x_parts, routed, mlp_piece = lax.optimization_barrier((x_parts, routed, mlp_piece))
    out_full = lax.all_gather(routed, "dp", axis=0, tiled=True)
    mlp_full = lax.all_gather(mlp_piece, "dp", axis=0)

    coarse_full = x_parts[:, local_len, :local_len].astype(f32)
    fine_full = x_parts[:, local_len + 1, :local_len].astype(f32)
    block_ids = jnp.arange(seq_size)
    placed = (block_ids[:, None] ^ seq_index) == block_ids[None]
    positions_full = jnp.sum(
        jnp.where(placed[:, :, None], coarse_full * 64.0 + fine_full, 0.0), axis=1
    )
    cosine, sine = rope_tables(positions_full.reshape(full_len), head_dim)
    doc_row = doc_ids
    doc_col = doc_ids.reshape(full_len, 1)
    cosine, sine, doc_col, grad_local = lax.optimization_barrier(
        (cosine, sine, doc_col, grad_out[0])
    )
    grad_hops = first_hops(grad_local, seq_size)
    normed_full, raw, rot, attended_heads, inverse = attn_forward(
        seq_index, x_parts, attn_full, first_full, head_gain, cosine, sine, doc_row, doc_col, sizes
    )
    attended_heads, grad_hops = lax.optimization_barrier((attended_heads, grad_hops))
    grad_full = second_hops(grad_hops, seq_size, seq_index).reshape(full_len, -1)
    residual = x_local.astype(f32)
    middle = residual + scatter_tokens(
        product("le,ed->ld", attended_heads, out_full), seq_size
    )
    normed_t = normed_full.T
    attended_t = attended_heads.T
    middle, normed_t, attended_t = lax.optimization_barrier((middle, normed_t, attended_t))
    second_unit, second_inverse = normalize(middle)
    second_normed = gather_flipped(
        (second_unit * second_full).astype(bf16), seq_size, seq_index
    ).reshape(full_len, -1)
    hidden, pair_grad, normed_grad_part = mlp_forward_backward(
        seq_index, seq_size, second_normed, grad_full, mlp_full, ff_cols
    )
    normed_grad = scatter_tokens(normed_grad_part, seq_size)

    def scatter_grad(pack):
        return lax.psum_scatter(pack, "dp", scatter_dimension=0, tiled=False)

    mlp_pack, block_part = mlp_grads(
        seq_index, seq_size, second_normed, pair_grad, hidden, grad_full, mlp_full
    )
    second_sum = jnp.sum(normed_grad * second_unit, axis=0, keepdims=True)
    middle_grad = grad_out[0].astype(f32) + norm_backward(
        normed_grad, second_unit, second_inverse, second_full
    )
    middle_low, mlp_pack = lax.optimization_barrier((middle_grad.astype(bf16), mlp_pack))
    mlp_grad = scatter_grad(mlp_pack)
    middle_low = gather_flipped(middle_low, seq_size, seq_index).reshape(full_len, -1)
    middle_low, block_part = lax.optimization_barrier((middle_low, block_part))
    block_parts = exchange(block_part.reshape(seq_size, local_len, model_width))
    raw_grad, attn_pack = attn_backward(
        seq_index, seq_size, middle_low, out_full, attended_t, normed_t, attn_full, first_full, second_sum, head_gain,
        cosine, sine, doc_row, doc_col, raw, rot, inverse, sizes,
    )
    first_normed_part = input_partial(raw_grad, attn_full)
    first_normed_part, attn_pack, block_parts, mlp_grad = lax.optimization_barrier(
        (first_normed_part, attn_pack, block_parts, mlp_grad)
    )
    attn_grad = scatter_grad(attn_pack)
    pair_hops = first_hops(mlp_grad, seq_size)
    pair_parts = second_hops(pair_hops, seq_size, seq_index)
    first_normed_part, pair_parts = lax.optimization_barrier(
        (first_normed_part, pair_parts)
    )
    first_normed_grad = scatter_tokens(first_normed_part, seq_size)
    first_unit, first_inverse = normalize(residual)
    input_grad = middle_grad + norm_backward(
        first_normed_grad, first_unit, first_inverse, first_full
    )
    block_out = (middle + jnp.sum(block_parts.astype(f32), axis=0)).astype(bf16)

    gate_weight_grad, up_weight_grad, down_weight_grad = finish_mlp(
        seq_index, pair_parts, share, gate_weight.shape[1], model_width, down_weight.shape[0], dp_size
    )
    attn_grad, input_grad, gate_weight_grad = lax.optimization_barrier(
        (attn_grad, input_grad, gate_weight_grad)
    )
    attn_parts = gather_parts(attn_grad[: share + EXTRA_ROWS], seq_size)
    out_home = lax.ppermute(attn_grad[share + EXTRA_ROWS :], ("dp", "seq"), back_routes)
    attn_parts, out_home = lax.optimization_barrier((attn_parts, out_home))
    query_weight_grad, key_weight_grad, value_weight_grad, gain_sums = finish_attn(
        attn_parts, sizes
    )
    out_home = out_home.reshape(-1, out_count, attn_cols).swapaxes(0, 1).reshape(out_count, -1)
    out_weight_grad = gather_tokens(out_home, seq_size).astype(f32)

    def own_gain(slot):
        return lax.dynamic_slice_in_dim(
            gain_sums[0], slot * GAIN_SLOT + dp_index * head_share, head_share, axis=0
        )

    return (
        block_out[None],
        input_grad[None],
        gain_sums[0, :share],
        query_weight_grad,
        key_weight_grad,
        value_weight_grad,
        own_gain(2),
        own_gain(3),
        out_weight_grad,
        gain_sums[0, GAIN_SLOT : GAIN_SLOT + share],
        gate_weight_grad,
        up_weight_grad,
        down_weight_grad,
    )


def solution(mesh):
    placed = (
        P("dp", "seq", None),
        P("dp", "seq"),
        P("dp", None),
        P("dp"),
        P("dp", None),
        P("dp", None),
        P("dp", None),
        P("dp"),
        P("dp"),
        P("dp", None),
        P("dp"),
        P("dp", None),
        P("dp", None),
        P("dp", None),
        P("dp", "seq", None),
    )
    return jax.shard_map(
        on_device,
        mesh=mesh,
        in_specs=placed,
        out_specs=(
            P("dp", "seq", None),
            P("dp", "seq", None),
            P("dp"),
            P("dp", None),
            P("dp", None),
            P("dp", None),
            P("dp"),
            P("dp"),
            P("dp", None),
            P("dp"),
            P("dp", None),
            P("dp", None),
            P("dp", None),
        ),
        check_vma=False,
    )
```

```python
import functools

import jax
import jax.numpy as jnp
from jax import lax
from jax.experimental import pallas as pl
from jax.experimental.pallas import tpu as pltpu
from jax.sharding import PartitionSpec as P

EPSILON = 1e-06
THETA = 1000000.0
LOG2E = 1.4426950408889634
EXTRA_ROWS = 16
GAIN_SLOT = 128
PACK_COLS = 256
VMEM_LIMIT = 60 * 1024 * 1024


def product(einsum_form, left_side, right_side):
    return jnp.einsum(einsum_form, left_side, right_side, preferred_element_type=jnp.float32)


def dot(left, right, contract):
    return lax.dot_general(
        left, right, (contract, ((), ())), preferred_element_type=jnp.float32
    )


def dot_nn(left, right):
    return dot(left, right, ((1,), (0,)))


def dot_nt(left, right):
    return dot(left, right, ((1,), (1,)))


def normalize(values):
    inverse = lax.rsqrt(jnp.mean(values * values, axis=-1, keepdims=True) + EPSILON)
    return (values * inverse, inverse)


def norm_backward(upstream, unit_rows, inverse, gain_values):
    scaled = upstream * gain_values
    return inverse * (scaled - unit_rows * jnp.mean(scaled * unit_rows, axis=-1, keepdims=True))


def rope_tables(positions, head_dim):
    half_dim = head_dim // 2
    inverse_freq = 1.0 / THETA ** (jnp.arange(half_dim, dtype=jnp.float32) * 2.0 / head_dim)
    angles = positions.astype(jnp.float32)[:, None] * inverse_freq
    cosine = jnp.cos(angles)
    sine = jnp.sin(angles)
    return (
        jnp.concatenate([cosine, cosine], axis=-1),
        jnp.concatenate([-sine, sine], axis=-1),
    )


def turned(values):
    return pltpu.roll(values, values.shape[-1] // 2, axis=1)


def query_blocks(full_len):
    block = min(256, full_len)
    reach = full_len // 2
    for first in range(0, full_len, block):
        yield first, first + block, max(0, first - reach)


def block_rows(seq_index, index, count):
    return pl.ds(pl.multiple_of((seq_index ^ index) * count, count), count)


def scalar_index(seq_index):
    return jnp.reshape(seq_index, (1,)).astype(jnp.int32)


def attn_forward_body(
    index_ref, x_ref, weight_ref, first_gain_ref, head_gain_ref, cos_ref, sin_ref, doc_row_ref, doc_col_ref,
    normed_ref, raw_ref, rot_ref, attended_ref, inverse_ref,
    *, group_size, head_dim,
):
    bf16 = jnp.bfloat16
    full_len = normed_ref.shape[0]
    local_len = x_ref.shape[1] - EXTRA_ROWS
    scale = head_dim ** (-0.5)

    @pl.when(pl.program_id(0) == 0)
    def _():
        for index in range(x_ref.shape[0]):
            unit, _ = normalize(x_ref[index, :local_len].astype(jnp.float32))
            normed_ref[block_rows(index_ref[0], index, local_len)] = (
                unit * first_gain_ref[...]
            ).astype(bf16)

    share = weight_ref.shape[1] - EXTRA_ROWS
    weight = weight_ref[:, :share, :].reshape(-1, weight_ref.shape[2])
    rot_width = (group_size + 1) * head_dim
    for first in range(0, full_len, 256):
        rows = slice(first, first + 256)
        raw = dot_nn(normed_ref[rows], weight)
        raw_ref[rows] = raw[:, :rot_width]
        rot_ref[rows, rot_width:] = raw[:, rot_width:].astype(bf16)
        for head in range(group_size + 1):
            cols = slice(head * head_dim, (head + 1) * head_dim)
            unit, _ = normalize(raw[:, cols])
            gain = head_gain_ref[:1] if head < group_size else head_gain_ref[1:2]
            scaled = unit * gain
            rot_ref[rows, cols] = (
                scaled * cos_ref[rows] + turned(scaled) * sin_ref[rows]
            ).astype(bf16)
    key = slice(group_size * head_dim, rot_width)
    for first, last, start in query_blocks(full_len):
        keys = rot_ref[start:last, key]
        values = rot_ref[start:last, rot_width:]
        widened = jnp.concatenate([values, jnp.ones_like(values)], axis=1)
        count = last - start
        query_index = lax.broadcasted_iota(jnp.int32, (last - first, count), 0) + first
        key_index = lax.broadcasted_iota(jnp.int32, (last - first, count), 1) + start
        allowed = (key_index <= query_index) & (
            doc_col_ref[first:last] == doc_row_ref[:, start:last]
        )
        for head in range(group_size):
            cols = slice(head * head_dim, (head + 1) * head_dim)
            scores = dot_nt(rot_ref[first:last, cols], keys)
            powers = jnp.where(allowed, jnp.exp2(scores * (scale * LOG2E)), 0.0)
            sums = dot_nn(powers.astype(bf16), widened)
            inverse = 1.0 / sums[:, head_dim:]
            attended_ref[first:last, cols] = (sums[:, :head_dim] * inverse).astype(bf16)
            inverse_ref[head * 8 : (head + 1) * 8, first:last] = inverse.T[:8]


def attn_forward(seq_index, x_parts, weight, first_gain, head_gain, cosine, sine, doc_row, doc_col, sizes):
    group_size, head_dim, local_kv = sizes
    full_len = doc_col.shape[0]
    model_width = x_parts.shape[2]
    group_cols = (group_size + 2) * head_dim
    whole = lambda shape: pl.BlockSpec(shape, lambda j, index: (0,) * len(shape))
    columns = lambda rows, width: pl.BlockSpec((rows, width), lambda j, index: (0, j))
    rot_width = (group_size + 1) * head_dim
    query_width = group_size * head_dim
    return pl.pallas_call(
        functools.partial(attn_forward_body, group_size=group_size, head_dim=head_dim),
        name="attn_forward",
        grid_spec=pltpu.PrefetchScalarGridSpec(
        num_scalar_prefetch=1,
        grid=(local_kv,),
        in_specs=[
            whole(x_parts.shape),
            pl.BlockSpec(weight.shape[:2] + (group_cols,), lambda j, index: (0, 0, j)),
            whole(first_gain.shape),
            whole(head_gain.shape),
            whole(cosine.shape),
            whole(sine.shape),
            whole(doc_row.shape),
            whole(doc_col.shape),
        ],
        out_specs=[
            whole((full_len, model_width)),
            columns(full_len, rot_width),
            columns(full_len, group_cols),
            columns(full_len, query_width),
            pl.BlockSpec((group_size * 8, full_len), lambda j, index: (j, 0)),
        ],
        ),
        out_shape=[
            jax.ShapeDtypeStruct((full_len, model_width), jnp.bfloat16),
            jax.ShapeDtypeStruct((full_len, local_kv * rot_width), jnp.float32),
            jax.ShapeDtypeStruct((full_len, local_kv * group_cols), jnp.bfloat16),
            jax.ShapeDtypeStruct((full_len, local_kv * query_width), jnp.bfloat16),
            jax.ShapeDtypeStruct((local_kv * group_size * 8, full_len), jnp.float32),
        ],
        compiler_params=pltpu.CompilerParams(vmem_limit_bytes=VMEM_LIMIT),
        cost_estimate=pl.CostEstimate(flops=1000, transcendentals=0, bytes_accessed=1000),
    )(scalar_index(seq_index), x_parts, weight, first_gain, head_gain, cosine, sine, doc_row, doc_col)


def attn_backward_body(
    index_ref, given_ref, out_weight_ref, attended_t_ref, normed_t_ref, weight_ref, first_gain_ref,
    second_sum_ref, head_gain_ref, cos_ref, sin_ref, doc_row_ref, doc_col_ref,
    raw_ref, rot_ref, inverse_ref,
    raw_grad_ref, pack_ref,
    gain_acc_ref, head_acc_ref, grad_acc_ref, query_acc_ref, key_acc_ref, value_acc_ref, middle_ref,
    *, group_size, head_dim, seq_size,
):
    bf16 = jnp.bfloat16
    full_len = middle_ref.shape[0]
    scale = head_dim ** (-0.5)
    step = pl.program_id(0)
    rot_width = (group_size + 1) * head_dim
    key = slice(group_size * head_dim, rot_width)

    @pl.when(step == 0)
    def _():
        gain_acc_ref[...] = jnp.zeros_like(gain_acc_ref)
        head_acc_ref[...] = jnp.zeros_like(head_acc_ref)
        count = full_len // seq_size
        for index in range(seq_size):
            rows = slice(index * count, (index + 1) * count)
            middle_ref[block_rows(index_ref[0], index, count)] = given_ref[rows]

    for first in range(0, full_len, 256):
        rows = slice(first, first + 256)
        grad_acc_ref[rows] = dot_nt(middle_ref[rows], out_weight_ref[...]).astype(bf16)
    key_acc_ref[...] = jnp.zeros_like(key_acc_ref)
    value_acc_ref[...] = jnp.zeros_like(value_acc_ref)
    key_turned = rot_ref[:, key].T
    for first, last, start in query_blocks(full_len):
        keys = rot_ref[start:last, key]
        values = rot_ref[start:last, rot_width:]
        count = last - start
        key_index = lax.broadcasted_iota(jnp.int32, (count, last - first), 0) + start
        query_index = lax.broadcasted_iota(jnp.int32, (count, last - first), 1) + first
        allowed = (key_index <= query_index) & (
            doc_col_ref[start:last] == doc_row_ref[:, first:last]
        )
        for head in range(group_size):
            cols = slice(head * head_dim, (head + 1) * head_dim)
            queries = rot_ref[first:last, cols]
            grads = grad_acc_ref[first:last, cols]
            scores = dot_nt(keys, queries)
            powers = jnp.where(allowed, jnp.exp2(scores * (scale * LOG2E)), 0.0)
            weights = powers * inverse_ref[head * 8 : head * 8 + 1, first:last]
            value_acc_ref[start:last] += dot_nn(weights.astype(bf16), grads)
            prob_grad = dot_nt(values, grads)
            delta = jnp.sum(weights * prob_grad, axis=0, keepdims=True)
            score_grad = (weights * (prob_grad - delta)).astype(bf16)
            key_acc_ref[start:last] += dot_nn(score_grad, queries)
            query_acc_ref[first:last, cols] = dot_nn(key_turned[:, start:last], score_grad).T

    query_sum = jnp.zeros((1, head_dim), jnp.float32)
    key_sum = jnp.zeros((1, head_dim), jnp.float32)
    for first in range(0, full_len, 256):
        rows = slice(first, first + 256)
        for head in range(group_size + 1):
            cols = slice(head * head_dim, (head + 1) * head_dim)
            is_query = head < group_size
            rot_grad = query_acc_ref[rows, cols] if is_query else key_acc_ref[rows]
            rot_grad = (rot_grad * scale).astype(bf16).astype(jnp.float32)
            scaled_grad = rot_grad * cos_ref[rows] - turned(rot_grad) * sin_ref[rows]
            unit, inverse = normalize(raw_ref[rows, cols])
            part = jnp.sum(scaled_grad * unit, axis=0, keepdims=True)
            if is_query:
                query_sum = query_sum + part
            else:
                key_sum = key_sum + part
            gain = head_gain_ref[:1] if is_query else head_gain_ref[1:2]
            raw_grad_ref[rows, cols] = norm_backward(scaled_grad, unit, inverse, gain).astype(bf16)
        raw_grad_ref[rows, rot_width:] = value_acc_ref[rows].astype(bf16)
    head_acc_ref[:1] += query_sum
    head_acc_ref[1:2] += key_sum

    dp_size, pack_rows, cols = pack_ref.shape
    share = weight_ref.shape[1] - EXTRA_ROWS
    for index in range(dp_size):
        mine = slice(index * share, (index + 1) * share)
        grad = dot_nn(normed_t_ref[mine], raw_grad_ref[...])
        pack_ref[index, :share] = grad.astype(bf16)
        terms = grad * weight_ref[index, :share].astype(jnp.float32)
        folded = terms[:, :128]
        for chunk in range(128, cols, 128):
            folded = folded + terms[:, chunk : chunk + 128]
        gain_acc_ref[:1, mine] += jnp.sum(folded.T, axis=0, keepdims=True)
        pack_ref[index, share : share + EXTRA_ROWS] = jnp.zeros((EXTRA_ROWS, cols), bf16)

    @pl.when(step == pl.num_programs(0) - 1)
    def _():
        for index in range(dp_size):
            mine = slice(index * share, (index + 1) * share)
            slots = [
                gain_acc_ref[:1, mine] / first_gain_ref[:, mine],
                second_sum_ref[:, mine],
                head_acc_ref[:1],
                head_acc_ref[1:2],
            ]
            slots = [
                slot
                if slot.shape[1] == GAIN_SLOT
                else jnp.concatenate(
                    [slot, jnp.zeros((1, GAIN_SLOT - slot.shape[1]), jnp.float32)], axis=1
                )
                for slot in slots
            ]
            row = jnp.concatenate(slots, axis=1)
            pack_ref[index, share : share + EXTRA_ROWS] = jnp.broadcast_to(
                row, (EXTRA_ROWS, cols)
            ).astype(bf16)

    out_rows = attended_t_ref.shape[0] // dp_size
    blocks = middle_ref.shape[1] // (cols * pl.num_programs(0))
    for block in range(blocks):
        begin = pl.multiple_of((block * pl.num_programs(0) + step) * cols, 128)
        grad = dot_nn(attended_t_ref[...], middle_ref[:, pl.ds(begin, cols)]).astype(bf16)
        base = share + EXTRA_ROWS + block * out_rows
        for index in range(dp_size):
            pack_ref[index, base : base + out_rows] = grad[index * out_rows : (index + 1) * out_rows]


def attn_backward(
    seq_index, seq_size, middle, out_weight, attended_t, normed_t, weight, first_gain, second_sum, head_gain, cosine,
    sine, doc_row, doc_col, raw, rot, inverse, sizes,
):
    group_size, head_dim, local_kv = sizes
    full_len, model_width = middle.shape
    dp_size, share = weight.shape[0], weight.shape[1] - EXTRA_ROWS
    group_cols = (group_size + 2) * head_dim
    total_cols = local_kv * group_cols
    rot_width = (group_size + 1) * head_dim
    query_width = group_size * head_dim
    out_rows = out_weight.shape[0] // dp_size * (model_width // total_cols)
    pack_rows = share + EXTRA_ROWS + out_rows
    whole = lambda shape: pl.BlockSpec(shape, lambda j, index: (0,) * len(shape))
    columns = lambda rows, width: pl.BlockSpec((rows, width), lambda j, index: (0, j))
    return pl.pallas_call(
        functools.partial(attn_backward_body, group_size=group_size, head_dim=head_dim, seq_size=seq_size),
        name="attn_backward",
        grid_spec=pltpu.PrefetchScalarGridSpec(
        num_scalar_prefetch=1,
        grid=(local_kv,),
        in_specs=[
            whole(middle.shape),
            pl.BlockSpec((query_width, model_width), lambda j, index: (j, 0)),
            whole(attended_t.shape),
            whole(normed_t.shape),
            pl.BlockSpec(weight.shape[:2] + (group_cols,), lambda j, index: (0, 0, j)),
            whole(first_gain.shape),
            whole(second_sum.shape),
            whole(head_gain.shape),
            whole(cosine.shape),
            whole(sine.shape),
            whole(doc_row.shape),
            whole(doc_col.shape),
            columns(full_len, rot_width),
            columns(full_len, group_cols),
            pl.BlockSpec((group_size * 8, full_len), lambda j, index: (j, 0)),
        ],
        out_specs=[
            columns(full_len, group_cols),
            pl.BlockSpec((dp_size, pack_rows, group_cols), lambda j, index: (0, 0, j)),
        ],
        scratch_shapes=[
            pltpu.VMEM((8, model_width), jnp.float32),
            pltpu.VMEM((8, head_dim), jnp.float32),
            pltpu.VMEM((full_len, query_width), jnp.bfloat16),
            pltpu.VMEM((full_len, query_width), jnp.float32),
            pltpu.VMEM((full_len, head_dim), jnp.float32),
            pltpu.VMEM((full_len, head_dim), jnp.float32),
            pltpu.VMEM((full_len, model_width), jnp.bfloat16),
        ],
        ),
        out_shape=[
            jax.ShapeDtypeStruct((full_len, total_cols), jnp.bfloat16),
            jax.ShapeDtypeStruct((dp_size, pack_rows, total_cols), jnp.bfloat16),
        ],
        compiler_params=pltpu.CompilerParams(vmem_limit_bytes=VMEM_LIMIT),
        cost_estimate=pl.CostEstimate(flops=1000, transcendentals=0, bytes_accessed=1000),
    )(
        scalar_index(seq_index), middle, out_weight, attended_t, normed_t, weight, first_gain, second_sum, head_gain, cosine,
        sine, doc_row, doc_col, raw, rot, inverse,
    )


def column_group(down_rows, own_rows, dp_size):
    count = 1
    while own_rows * count % 128 or dp_size % count:
        count += 1
    return count


def column_choice(seq_index, count, down_rows, own_rows):
    own = lax.broadcasted_iota(jnp.int32, (1, own_rows * count), 1)
    target = own + own_rows * seq_index
    for block in range(1, count):
        target = target + jnp.where(own >= block * own_rows, down_rows - own_rows, 0)
    whole = lax.broadcasted_iota(jnp.int32, (down_rows * count, own_rows * count), 0)
    return jnp.where(whole == target, 1.0, 0.0).astype(jnp.bfloat16)


def pack_mlp_body(index_ref, gate_ref, up_ref, down_ref, pack_ref, *, dp_size, seq_size):
    share = gate_ref.shape[0]
    own_rows = down_ref.shape[0]
    down_rows = own_rows * seq_size
    count = column_group(down_rows, own_rows, dp_size)
    choice = column_choice(index_ref[0], count, down_rows, own_rows)
    width = down_rows * count
    column = 0
    for source in (gate_ref, up_ref):
        for first in range(0, source.shape[1], width):
            chosen = dot_nn(source[:, first : first + width], choice).astype(jnp.bfloat16)
            for part in range(0, chosen.shape[1], 128):
                base = column // PACK_COLS * share
                half = column % PACK_COLS
                pack_ref[base : base + share, half : half + 128] = chosen[:, part : part + 128]
                column += 128
    base = column // PACK_COLS * share
    for first in range(0, down_ref.shape[1], PACK_COLS):
        pack_ref[base : base + own_rows] = down_ref[:, first : first + PACK_COLS]
        base += own_rows


def pack_mlp(seq_index, gate_weight, up_weight, down_weight, dp_size, seq_size):
    share, ff_total = gate_weight.shape
    model_width = down_weight.shape[1]
    own_rows = down_weight.shape[0] // seq_size
    rows = share * (2 * ff_total // seq_size // PACK_COLS) + own_rows * (model_width // PACK_COLS)
    whole = pl.BlockSpec((share, ff_total), lambda i, index: (0, 0))
    return pl.pallas_call(
        functools.partial(pack_mlp_body, dp_size=dp_size, seq_size=seq_size),
        name="pack_mlp",
        grid_spec=pltpu.PrefetchScalarGridSpec(
            num_scalar_prefetch=1,
            grid=(1,),
            in_specs=[
                whole, whole, pl.BlockSpec((own_rows, model_width), lambda i, index: (index[0], 0))
            ],
            out_specs=pl.BlockSpec((rows, PACK_COLS), lambda i, index: (0, 0)),
        ),
        out_shape=jax.ShapeDtypeStruct((rows, PACK_COLS), jnp.bfloat16),
        compiler_params=pltpu.CompilerParams(vmem_limit_bytes=VMEM_LIMIT),
        cost_estimate=pl.CostEstimate(flops=1000, transcendentals=0, bytes_accessed=1000),
    )(jnp.reshape(seq_index, (1,)).astype(jnp.int32), gate_weight, up_weight, down_weight)


def mlp_body(
    index_ref, normed_ref, grad_ref, weight_ref, hidden_ref, pair_grad_ref, normed_grad_ref,
    pair_ref, down_ref,
):
    bf16 = jnp.bfloat16
    width = hidden_ref.shape[1]
    dp_size = weight_ref.shape[0]
    share = pair_ref.shape[0] // dp_size
    down_share = width // dp_size

    @pl.when(pl.program_id(0) == 0)
    def _():
        for index in range(dp_size):
            base = 0
            rows = slice(index * share, (index + 1) * share)
            for first in range(0, 2 * width, PACK_COLS):
                pair_ref[rows, first : first + PACK_COLS] = weight_ref[index, base : base + share]
                base += share
            rows = slice(index * down_share, (index + 1) * down_share)
            for first in range(0, down_ref.shape[1], PACK_COLS):
                down_ref[rows, first : first + PACK_COLS] = weight_ref[
                    index, base : base + down_share
                ]
                base += down_share

    pair = dot_nn(normed_ref[...], pair_ref[...])
    hidden_grad = dot_nt(grad_ref[...], down_ref[...])
    gate_pre = pair[:, :width]
    up_pre = pair[:, width:]
    sigmoid_gate = jax.nn.sigmoid(gate_pre)
    silu_gate = gate_pre * sigmoid_gate
    hidden_ref[...] = (silu_gate * up_pre).astype(bf16)
    gate_pre_grad = (
        hidden_grad * up_pre * sigmoid_gate * (1.0 + gate_pre * (1.0 - sigmoid_gate))
    )
    pair_grad_ref[:, :width] = gate_pre_grad.astype(bf16)
    pair_grad_ref[:, width:] = (hidden_grad * silu_gate).astype(bf16)
    normed_grad_ref[...] = dot_nt(pair_grad_ref[...], pair_ref[...]).astype(bf16)


def mlp_forward_backward(seq_index, seq_size, normed, grads, weight, width):
    full_len, model_width = normed.shape
    block = full_len // seq_size
    rows = lambda cols: pl.BlockSpec((block, cols), lambda i, index: (i, 0))
    whole = lambda shape: pl.BlockSpec(shape, lambda i, index: (0,) * len(shape))
    return pl.pallas_call(
        mlp_body,
        name="mlp_forward_backward",
        grid_spec=pltpu.PrefetchScalarGridSpec(
        num_scalar_prefetch=1,
        grid=(full_len // block,),
        in_specs=[rows(model_width), rows(model_width), whole(weight.shape)],
        out_specs=[
            rows(width),
            rows(2 * width),
            pl.BlockSpec((block, model_width), lambda i, index: (i ^ index[0], 0)),
        ],
        scratch_shapes=[
            pltpu.VMEM((model_width, 2 * width), jnp.bfloat16),
            pltpu.VMEM((width, model_width), jnp.bfloat16),
        ],
        ),
        out_shape=[
            jax.ShapeDtypeStruct((full_len, width), jnp.bfloat16),
            jax.ShapeDtypeStruct((full_len, 2 * width), jnp.bfloat16),
            jax.ShapeDtypeStruct((full_len, model_width), jnp.bfloat16),
        ],
        compiler_params=pltpu.CompilerParams(vmem_limit_bytes=VMEM_LIMIT),
        cost_estimate=pl.CostEstimate(flops=1000, transcendentals=0, bytes_accessed=1000),
    )(scalar_index(seq_index), normed, grads, weight)


def mlp_grads_body(
    index_ref, normed_ref, pair_grad_ref, hidden_ref, grad_ref, weight_ref, pack_ref, block_ref,
    down_ref, *, seq_size,
):
    bf16 = jnp.bfloat16
    dp_size = pack_ref.shape[0]
    share = normed_ref.shape[1] // dp_size
    down_share = hidden_ref.shape[1] // dp_size
    normed_t = normed_ref[...].T
    for index in range(dp_size):
        grad = dot_nn(normed_t[index * share : (index + 1) * share], pair_grad_ref[...])
        grad = grad.astype(bf16)
        base = 0
        for first in range(0, grad.shape[1], PACK_COLS):
            pack_ref[index, base : base + share] = grad[:, first : first + PACK_COLS]
            base += share
    grad = dot_nn(hidden_ref[...].T, grad_ref[...])
    for index in range(dp_size):
        base = share * (pair_grad_ref.shape[1] // PACK_COLS)
        rows = slice(index * down_share, (index + 1) * down_share)
        mine = grad[rows].astype(bf16)
        for first in range(0, grad.shape[1], PACK_COLS):
            pack_ref[index, base : base + down_share] = mine[:, first : first + PACK_COLS]
            down_ref[rows, first : first + PACK_COLS] = weight_ref[index, base : base + down_share]
            base += down_share
    count = hidden_ref.shape[0] // seq_size
    for index in range(seq_size):
        rows = slice(index * count, (index + 1) * count)
        block_ref[block_rows(index_ref[0], index, count)] = dot_nn(
            hidden_ref[rows], down_ref[...]
        ).astype(bf16)


def mlp_grads(seq_index, seq_size, normed, pair_grad, hidden, grads, weight):
    whole = lambda shape: pl.BlockSpec(shape, lambda i, index: (0,) * len(shape))
    operands = (normed, pair_grad, hidden, grads, weight)
    return pl.pallas_call(
        functools.partial(mlp_grads_body, seq_size=seq_size),
        name="mlp_grads",
        grid_spec=pltpu.PrefetchScalarGridSpec(
            num_scalar_prefetch=1,
            grid=(1,),
            in_specs=[whole(operand.shape) for operand in operands],
            out_specs=[whole(weight.shape), whole(normed.shape)],
            scratch_shapes=[pltpu.VMEM((hidden.shape[1], normed.shape[1]), jnp.bfloat16)],
        ),
        out_shape=[
            jax.ShapeDtypeStruct(weight.shape, jnp.bfloat16),
            jax.ShapeDtypeStruct(normed.shape, jnp.bfloat16),
        ],
        compiler_params=pltpu.CompilerParams(vmem_limit_bytes=VMEM_LIMIT),
        cost_estimate=pl.CostEstimate(flops=1000, transcendentals=0, bytes_accessed=1000),
    )(scalar_index(seq_index), *operands)


def input_body(raw_grad_ref, weight_ref, out_ref):
    share = weight_ref.shape[1] - EXTRA_ROWS
    weight = weight_ref[:, :share, :].reshape(-1, weight_ref.shape[2])
    out_ref[...] = dot_nt(raw_grad_ref[...], weight).astype(jnp.bfloat16)


def input_partial(raw_grad, weight):
    full_len, cols = raw_grad.shape
    block = min(256, full_len)
    model_width = weight.shape[0] * (weight.shape[1] - EXTRA_ROWS)
    return pl.pallas_call(
        input_body,
        name="input_partial",
        grid=(full_len // block,),
        in_specs=[
            pl.BlockSpec((block, cols), lambda i: (i, 0)),
            pl.BlockSpec(weight.shape, lambda i: (0, 0, 0)),
        ],
        out_specs=pl.BlockSpec((block, model_width), lambda i: (i, 0)),
        out_shape=jax.ShapeDtypeStruct((full_len, model_width), jnp.bfloat16),
        compiler_params=pltpu.CompilerParams(vmem_limit_bytes=VMEM_LIMIT),
        cost_estimate=pl.CostEstimate(flops=1000, transcendentals=0, bytes_accessed=1000),
    )(raw_grad, weight)


def finish_attn_body(
    index_ref, parts_ref, query_ref, key_ref, value_ref, gain_ref, *, group_size, head_dim
):
    f32 = jnp.float32
    seq_size, rows, cols = parts_ref.shape
    share = rows - EXTRA_ROWS
    group_cols = (group_size + 2) * head_dim
    local_kv = cols // group_cols
    rot_width = group_size * head_dim
    total = jnp.zeros((EXTRA_ROWS, group_cols), f32)
    for index in range(seq_size):
        for local in range(local_kv):
            first = local * group_cols
            head = (index_ref[0] ^ index) * local_kv + local
            part = parts_ref[index, :share, first : first + group_cols].astype(f32)
            wide = pl.ds(pl.multiple_of(head * rot_width, 128), rot_width)
            spot = pl.ds(pl.multiple_of(head * head_dim, 128), head_dim)
            query_ref[:, wide] = part[:, :rot_width]
            key_ref[:, spot] = part[:, rot_width : rot_width + head_dim]
            value_ref[:, spot] = part[:, rot_width + head_dim :]
        total = total + parts_ref[index, share:, cols - group_cols :].astype(f32)
    gain_ref[...] = total


def finish_attn(seq_index, parts, sizes):
    group_size, head_dim, local_kv = sizes
    seq_size, rows, cols = parts.shape
    share = rows - EXTRA_ROWS
    heads = seq_size * local_kv
    whole = lambda shape: pl.BlockSpec(shape, lambda i, index: (0,) * len(shape))
    shapes = [
        (share, heads * group_size * head_dim),
        (share, heads * head_dim),
        (share, heads * head_dim),
        (EXTRA_ROWS, (group_size + 2) * head_dim),
    ]
    return pl.pallas_call(
        functools.partial(finish_attn_body, group_size=group_size, head_dim=head_dim),
        name="finish_attn",
        grid_spec=pltpu.PrefetchScalarGridSpec(
            num_scalar_prefetch=1,
            grid=(1,),
            in_specs=[whole(parts.shape)],
            out_specs=[whole(shape) for shape in shapes],
        ),
        out_shape=[jax.ShapeDtypeStruct(shape, jnp.float32) for shape in shapes],
        compiler_params=pltpu.CompilerParams(vmem_limit_bytes=VMEM_LIMIT),
        cost_estimate=pl.CostEstimate(flops=1000, transcendentals=0, bytes_accessed=1000),
    )(scalar_index(seq_index), parts)


def finish_mlp_body(index_ref, parts_ref, gate_ref, up_ref, down_ref, *, dp_size):
    f32 = jnp.float32
    seq_size = parts_ref.shape[0]
    share, ff_total = gate_ref.shape
    down_rows = down_ref.shape[0]
    own_rows = down_rows // seq_size
    count = column_group(down_rows, own_rows, dp_size)
    choices = [
        column_choice(index_ref[0] ^ index, count, down_rows, own_rows)
        for index in range(seq_size)
    ]
    width = down_rows * count
    column = 0
    for target_ref in (gate_ref, up_ref):
        for first in range(0, ff_total, width):
            total = jnp.zeros((share, width), f32)
            for index in range(seq_size):
                pieces = []
                for part in range(column, column + own_rows * count, 128):
                    base = part // PACK_COLS * share
                    half = part % PACK_COLS
                    pieces.append(parts_ref[index, base : base + share, half : half + 128])
                total = total + dot_nt(jnp.concatenate(pieces, axis=1), choices[index])
            target_ref[:, first : first + width] = total
            column += own_rows * count
    for index in range(seq_size):
        base = column // PACK_COLS * share
        for first in range(0, down_ref.shape[1], PACK_COLS):
            part = parts_ref[index, base : base + own_rows]
            down_ref[
                block_rows(index_ref[0], index, own_rows), first : first + PACK_COLS
            ] = part.astype(f32)
            base += own_rows


def finish_mlp(seq_index, parts, share, ff_total, model_width, down_rows, dp_size):
    return pl.pallas_call(
        functools.partial(finish_mlp_body, dp_size=dp_size),
        name="finish_mlp",
        grid_spec=pltpu.PrefetchScalarGridSpec(
            num_scalar_prefetch=1,
            grid=(1,),
            in_specs=[pl.BlockSpec(parts.shape, lambda i, index: (0, 0, 0))],
            out_specs=[
                pl.BlockSpec((share, ff_total), lambda i, index: (0, 0)),
                pl.BlockSpec((share, ff_total), lambda i, index: (0, 0)),
                pl.BlockSpec((down_rows, model_width), lambda i, index: (0, 0)),
            ],
        ),
        out_shape=[
            jax.ShapeDtypeStruct((share, ff_total), jnp.float32),
            jax.ShapeDtypeStruct((share, ff_total), jnp.float32),
            jax.ShapeDtypeStruct((down_rows, model_width), jnp.float32),
        ],
        compiler_params=pltpu.CompilerParams(vmem_limit_bytes=VMEM_LIMIT),
        cost_estimate=pl.CostEstimate(flops=1000, transcendentals=0, bytes_accessed=1000),
    )(scalar_index(seq_index), parts)


def exchange(pieces):
    return lax.all_to_all(pieces, "seq", split_axis=0, concat_axis=0, tiled=True)


def gather_parts(rows, seq_size):
    return exchange(jnp.broadcast_to(rows[None], (seq_size,) + rows.shape))


def gather_tokens(rows, seq_size):
    return gather_parts(rows, seq_size).reshape((seq_size * rows.shape[0],) + rows.shape[1:])


def pass_on(values, seq_size, flip):
    return lax.ppermute(values, "seq", [(index, index ^ flip) for index in range(seq_size)])


def first_hops(rows, seq_size):
    if seq_size != 4:
        return (rows,)
    half = rows.shape[0] // 2
    upper, lower = rows[:half], rows[half:]
    return (
        upper,
        lower,
        pass_on(upper, seq_size, 1),
        pass_on(lower, seq_size, 2),
        pass_on(upper, seq_size, 2),
        pass_on(lower, seq_size, 1),
    )


def second_hops(hops, seq_size, seq_index):
    if seq_size != 4:
        parts = gather_parts(hops[0], seq_size)
        return jnp.stack(
            [
                lax.dynamic_index_in_dim(parts, seq_index ^ index, 0, keepdims=False)
                for index in range(seq_size)
            ]
        )
    upper, lower, upper_one, lower_two, upper_two, lower_one = hops
    upper_three = pass_on(upper_one, seq_size, 2)
    lower_three = pass_on(lower_two, seq_size, 1)
    return jnp.concatenate(
        [upper, lower, upper_one, lower_one, upper_two, lower_two, upper_three, lower_three]
    ).reshape((seq_size, -1) + upper.shape[1:])


def gather_flipped(rows, seq_size, seq_index):
    return second_hops(first_hops(rows, seq_size), seq_size, seq_index)


def scatter_tokens(partial, seq_size):
    pieces = partial.astype(jnp.bfloat16).reshape((seq_size, -1) + partial.shape[1:])
    return jnp.sum(exchange(pieces).astype(jnp.float32), axis=0)


def row_routes(dp_size, seq_size):
    routes = []
    for dp_index in range(dp_size):
        for seq_index in range(seq_size):
            holder = dp_size // seq_size * seq_index + dp_index // seq_size
            routes.append(
                (holder * seq_size + dp_index % seq_size, dp_index * seq_size + seq_index)
            )
    return routes


def on_device(
    block_in,
    positions,
    doc_ids,
    first_gain,
    query_weight,
    key_weight,
    value_matrix,
    query_gain,
    key_gain,
    out_weight,
    second_gain,
    gate_weight,
    up_weight,
    down_weight,
    grad_out,
):
    bf16 = jnp.bfloat16
    f32 = jnp.float32
    dp_size = lax.axis_size("dp")
    seq_size = lax.axis_size("seq")
    seq_index = lax.axis_index("seq")
    dp_index = lax.axis_index("dp")
    local_len, model_width = block_in.shape[1:]
    full_len = local_len * seq_size
    head_dim = query_gain.shape[0] * dp_size
    query_heads = query_weight.shape[1] // head_dim
    kv_heads = key_weight.shape[1] // head_dim
    group_size = query_heads // kv_heads
    local_kv = kv_heads // seq_size
    query_cols = local_kv * group_size * head_dim
    group_cols = (group_size + 2) * head_dim
    attn_cols = local_kv * group_cols
    ff_cols = gate_weight.shape[1] // seq_size
    share = first_gain.shape[0]
    head_share = query_gain.shape[0]
    gain_width = 2 * share + 2 * head_share
    sizes = (group_size, head_dim, local_kv)
    routes = row_routes(dp_size, seq_size)
    back_routes = [(target, source) for source, target in routes]

    def own_columns(matrix, width):
        return lax.dynamic_slice_in_dim(matrix, seq_index * width, width, axis=1)

    def own_rows(matrix):
        count = matrix.shape[0] // seq_size
        return lax.dynamic_slice_in_dim(matrix, seq_index * count, count, axis=0)

    x_local = block_in[0]
    coarse = jnp.pad(positions // 64, ((0, 0), (0, model_width - local_len)))
    fine = jnp.pad(positions % 64, ((0, 0), (0, model_width - local_len)))
    extra = jnp.pad(jnp.concatenate([coarse, fine]), ((0, EXTRA_ROWS - 2), (0, 0))).astype(bf16)
    x_parts = gather_flipped(jnp.concatenate([x_local, extra]), seq_size, seq_index)

    query_own = own_columns(query_weight, query_cols).reshape(share, local_kv, -1)
    key_own = own_columns(key_weight, local_kv * head_dim).reshape(share, local_kv, -1)
    value_own = own_columns(value_matrix, local_kv * head_dim).reshape(share, local_kv, -1)
    attn_piece = jnp.concatenate([query_own, key_own, value_own], axis=2).reshape(share, -1)
    gains = jnp.concatenate([first_gain, second_gain, query_gain, key_gain])[None]
    gains = jnp.pad(gains, ((0, EXTRA_ROWS - 1), (0, attn_cols - gain_width)))
    attn_full = lax.all_gather(jnp.concatenate([attn_piece, gains], axis=0), "dp", axis=0)
    gains_full = attn_full[:, share, :gain_width].astype(f32)
    first_full = gains_full[:, :share].reshape(1, -1)
    second_full = gains_full[:, share : 2 * share].reshape(1, -1)
    head_gain = jnp.pad(
        gains_full[:, 2 * share :].reshape(dp_size, 2, head_share).swapaxes(0, 1).reshape(2, -1),
        ((0, 6), (0, 0)),
    )

    out_count = out_weight.shape[0] // seq_size
    routed = lax.ppermute(own_rows(out_weight), ("dp", "seq"), routes)
    mlp_piece = pack_mlp(seq_index, gate_weight, up_weight, down_weight, dp_size, seq_size)
    x_parts, routed, mlp_piece = lax.optimization_barrier((x_parts, routed, mlp_piece))
    out_full = lax.all_gather(routed, "dp", axis=0, tiled=True)
    mlp_full = lax.all_gather(mlp_piece, "dp", axis=0)

    coarse_full = x_parts[:, local_len, :local_len].astype(f32)
    fine_full = x_parts[:, local_len + 1, :local_len].astype(f32)
    block_ids = jnp.arange(seq_size)
    placed = (block_ids[:, None] ^ seq_index) == block_ids[None]
    positions_full = jnp.sum(
        jnp.where(placed[:, :, None], coarse_full * 64.0 + fine_full, 0.0), axis=1
    )
    cosine, sine = rope_tables(positions_full.reshape(full_len), head_dim)
    doc_row = doc_ids
    doc_col = doc_ids.reshape(full_len, 1)
    cosine, sine, doc_col, grad_local = lax.optimization_barrier(
        (cosine, sine, doc_col, grad_out[0])
    )
    grad_hops = first_hops(grad_local, seq_size)
    normed_full, raw, rot, attended_heads, inverse = attn_forward(
        seq_index, x_parts, attn_full, first_full, head_gain, cosine, sine, doc_row, doc_col, sizes
    )
    attended_heads, grad_hops = lax.optimization_barrier((attended_heads, grad_hops))
    grad_full = second_hops(grad_hops, seq_size, seq_index).reshape(full_len, -1)
    residual = x_local.astype(f32)
    middle = residual + scatter_tokens(
        product("le,ed->ld", attended_heads, out_full), seq_size
    )
    normed_t = normed_full.T
    attended_t = attended_heads.T
    middle, normed_t, attended_t = lax.optimization_barrier((middle, normed_t, attended_t))
    second_unit, second_inverse = normalize(middle)
    second_normed = gather_flipped(
        (second_unit * second_full).astype(bf16), seq_size, seq_index
    ).reshape(full_len, -1)
    hidden, pair_grad, normed_grad_part = mlp_forward_backward(
        seq_index, seq_size, second_normed, grad_full, mlp_full, ff_cols
    )
    normed_grad = scatter_tokens(normed_grad_part, seq_size)

    def scatter_grad(pack):
        return lax.psum_scatter(pack, "dp", scatter_dimension=0, tiled=False)

    mlp_pack, block_part = mlp_grads(
        seq_index, seq_size, second_normed, pair_grad, hidden, grad_full, mlp_full
    )
    second_sum = jnp.sum(normed_grad * second_unit, axis=0, keepdims=True)
    middle_grad = grad_out[0].astype(f32) + norm_backward(
        normed_grad, second_unit, second_inverse, second_full
    )
    middle_low, mlp_pack = lax.optimization_barrier((middle_grad.astype(bf16), mlp_pack))
    mlp_grad = scatter_grad(mlp_pack)
    middle_low = gather_flipped(middle_low, seq_size, seq_index).reshape(full_len, -1)
    middle_low, block_part = lax.optimization_barrier((middle_low, block_part))
    block_parts = exchange(block_part.reshape(seq_size, local_len, model_width))
    raw_grad, attn_pack = attn_backward(
        seq_index, seq_size, middle_low, out_full, attended_t, normed_t, attn_full, first_full, second_sum, head_gain,
        cosine, sine, doc_row, doc_col, raw, rot, inverse, sizes,
    )
    first_normed_part = input_partial(raw_grad, attn_full)
    first_normed_part, attn_pack, block_parts, mlp_grad = lax.optimization_barrier(
        (first_normed_part, attn_pack, block_parts, mlp_grad)
    )
    attn_grad = scatter_grad(attn_pack)
    pair_hops = first_hops(mlp_grad, seq_size)
    pair_parts = second_hops(pair_hops, seq_size, seq_index)
    first_normed_part, pair_parts = lax.optimization_barrier(
        (first_normed_part, pair_parts)
    )
    first_normed_grad = scatter_tokens(first_normed_part, seq_size)
    first_unit, first_inverse = normalize(residual)
    input_grad = middle_grad + norm_backward(
        first_normed_grad, first_unit, first_inverse, first_full
    )
    block_out = (middle + jnp.sum(block_parts.astype(f32), axis=0)).astype(bf16)

    gate_weight_grad, up_weight_grad, down_weight_grad = finish_mlp(
        seq_index, pair_parts, share, gate_weight.shape[1], model_width, down_weight.shape[0], dp_size
    )
    attn_grad, input_grad, gate_weight_grad = lax.optimization_barrier(
        (attn_grad, input_grad, gate_weight_grad)
    )
    attn_hops = first_hops(attn_grad[: share + EXTRA_ROWS], seq_size)
    out_home = lax.ppermute(attn_grad[share + EXTRA_ROWS :], ("dp", "seq"), back_routes)
    attn_hops, out_home = lax.optimization_barrier((attn_hops, out_home))
    attn_parts = second_hops(attn_hops, seq_size, seq_index)
    out_home = out_home.reshape(-1, out_count, attn_cols).swapaxes(0, 1).reshape(out_count, -1)
    out_weight_grad = gather_tokens(out_home, seq_size).astype(f32)
    query_weight_grad, key_weight_grad, value_weight_grad, gain_sums = finish_attn(
        seq_index, attn_parts, sizes
    )

    def own_gain(slot):
        return lax.dynamic_slice_in_dim(
            gain_sums[0], slot * GAIN_SLOT + dp_index * head_share, head_share, axis=0
        )

    return (
        block_out[None],
        input_grad[None],
        gain_sums[0, :share],
        query_weight_grad,
        key_weight_grad,
        value_weight_grad,
        own_gain(2),
        own_gain(3),
        out_weight_grad,
        gain_sums[0, GAIN_SLOT : GAIN_SLOT + share],
        gate_weight_grad,
        up_weight_grad,
        down_weight_grad,
    )


def solution(mesh):
    placed = (
        P("dp", "seq", None),
        P("dp", "seq"),
        P("dp", None),
        P("dp"),
        P("dp", None),
        P("dp", None),
        P("dp", None),
        P("dp"),
        P("dp"),
        P("dp", None),
        P("dp"),
        P("dp", None),
        P("dp", None),
        P("dp", None),
        P("dp", "seq", None),
    )
    return jax.shard_map(
        on_device,
        mesh=mesh,
        in_specs=placed,
        out_specs=(
            P("dp", "seq", None),
            P("dp", "seq", None),
            P("dp"),
            P("dp", None),
            P("dp", None),
            P("dp", None),
            P("dp"),
            P("dp"),
            P("dp", None),
            P("dp"),
            P("dp", None),
            P("dp", None),
            P("dp", None),
        ),
        check_vma=False,
    )
```
